256 devices in a mesh: group: 8 (over x, core), batch: 32 (over z, y).
Axes of the slice: x: 4, y: 4, z: 8, core: 2. Of those that a mesh axis runs over, the one named last changes fastest.
Arguments:
- panel_alleles: int32 [64, 131072], P('group', 'batch'), may hold values 0 or 1
- recomb_rates: float32 [64], P('group'), may hold values from 0.001 to 0.3
- genotypes: int32 [2, 64], P(None, 'group'), may hold values from 0 to 2, as said below
Outputs:
- dosage: float32 [2, 64], P(None, 'group')
- log_likelihood: float32 [2], replicated
The draws below stay inside these ranges and needn't reach their ends.
Inputs may be any that keep to these rules, and one draw needn't show every extreme that they name: `genotypes`: 2 marks a marker at which the target's allele is missing; 0 and 1 are observed alleles.
All inputs are finite; a program needn't handle non-finite values. No bound on the sum of `panel_alleles` on one device may be relied on, other than what follows from the above.
Results may differ from the reference program's by a relative error of at most 0.0003.
Values sent between devices are 32-bit elements; how exact they have to be, the bound alone decides.
A program may use at most 64 MiB of HBM per device.

```python
import math
import jax
import jax.numpy as jnp
from jax import lax

K = 131072
MD = 8
H = 2
M = 64
N_GROUP = 8


def draw_genotypes(key, part):
    key_allele = jax.random.fold_in(key, 11)
    key_missing = jax.random.fold_in(key, 23)
    allele = jax.random.randint(key_allele, (H, M), 0, 2, dtype=jnp.int32)
    roll = jax.random.randint(key_missing, (H, M), 0, 4 * M, dtype=jnp.int32)
    position = jnp.arange(M, dtype=jnp.int32)[None, :]
    return jnp.where(roll < M + 2 * position, allele, 2).astype(jnp.int32)


def plant(array, own_key, least, top_value):
    place = [jax.random.randint(jax.random.fold_in(own_key, axis), (), 0, length) for axis, length in enumerate(array.shape)]
    widest = array.shape.index(max(array.shape))
    beside = place[:widest] + [(place[widest] + 1) % array.shape[widest]] + place[widest + 1:]
    return array.at[tuple(place)].set(least).at[tuple(beside)].set(top_value)


def block_scale(own_key, shape, shards, low, top_value):
    level = 1.0
    for axis_at, blocks in shards:
        steps = jax.random.uniform(jax.random.fold_in(jax.random.fold_in(own_key, 6), axis_at), (blocks,), jnp.float32, low / len(shards), top_value / len(shards))
        level = level * jnp.repeat(jnp.exp(steps), shape[axis_at] // blocks).reshape((-1,) + (1,) * (len(shape) - 1 - axis_at))
    return level


def setup_inputs(seed: int = 0) -> dict:
    arg_keys = jax.random.split(jax.random.key(seed), 4)
    return {
        "panel_alleles": plant((jax.random.randint(arg_keys[0], (M, K), 0, 2) < 1).astype(jnp.int32), jax.random.fold_in(arg_keys[0], 1), 0, 1),
        "recomb_rates": jnp.clip(jnp.exp(math.log(0.3) - 5.7037825 * jax.random.uniform(arg_keys[1], (M,), jnp.float32) ** block_scale(arg_keys[1], (M,), ((0, 8),), -0.2, 0.2)), 0.001, 0.3),
        "genotypes": draw_genotypes(jax.random.fold_in(arg_keys[3], 71), 0),
    }


MISMATCH = 0.05


def emission(panel_rows, geno_cols):
    observed = geno_cols.T[:, :, None]
    agrees = jnp.where(panel_rows[:, None, :] == observed, 1.0 - MISMATCH, MISMATCH)
    return jnp.where(observed == 2, 1.0, agrees).astype(jnp.float32)


def forward_marker(scaled, emitted, switch):
    unscaled = emitted * ((1.0 - switch) * scaled + switch / K)
    totals = jnp.sum(unscaled, axis=1, keepdims=True)
    return unscaled / totals, totals[:, 0]


def backward_marker(scaled, emitted, switch):
    weighted = emitted * scaled
    spread = (1.0 - switch) * weighted + switch / K * jnp.sum(weighted, axis=1, keepdims=True)
    return spread / jnp.sum(spread, axis=1, keepdims=True)


def reference(panel_alleles, recomb_rates, genotypes):
    panel_blocks = panel_alleles.reshape(N_GROUP, MD, K)
    geno_blocks = genotypes.reshape(H, N_GROUP, MD).transpose(1, 0, 2)
    rate_blocks = recomb_rates.reshape(N_GROUP, MD)
    uniform = jnp.full((H, K), 1.0 / K, jnp.float32)

    def forward_stretch(carried, inputs):
        alphas, log_total = carried
        emitted = emission(inputs[0], inputs[1])

        def marker_step(status, pieces):
            scaled, totals = forward_marker(status[0], pieces[0], pieces[1])
            return (scaled, status[1] + jnp.log(totals)), None

        (alpha_out, log_total), unused = lax.scan(marker_step, (alphas, log_total), (emitted, inputs[2]))
        return (alpha_out, log_total), alphas

    (alpha_last, log_total), alpha_starts = lax.scan(
        forward_stretch, (uniform, jnp.zeros((H,), jnp.float32)), (panel_blocks, geno_blocks, rate_blocks))

    def backward_stretch(betas, inputs):
        emitted = emission(inputs[0], inputs[1])

        def marker_step(scaled, pieces):
            return backward_marker(scaled, pieces[0], pieces[1]), None

        beta_out, unused = lax.scan(marker_step, betas, (emitted, inputs[2]), reverse=True)
        return beta_out, betas

    beta_first, beta_ends = lax.scan(backward_stretch, uniform, (panel_blocks, geno_blocks, rate_blocks), reverse=True)

    def stretch_dosage(inputs):
        alphas, betas, panel_rows, geno_cols, switches = inputs
        emitted = emission(panel_rows, geno_cols)

        def forward_step(scaled, pieces):
            nextrow, totals = forward_marker(scaled, pieces[0], pieces[1])
            return nextrow, nextrow

        def backward_step(scaled, pieces):
            return backward_marker(scaled, pieces[0], pieces[1]), scaled

        unused_f, forward_rows = lax.scan(forward_step, alphas, (emitted, switches))
        unused_b, backward_rows = lax.scan(backward_step, betas, (emitted, switches), reverse=True)
        product = forward_rows * backward_rows
        numerator = jnp.sum(jnp.where(panel_rows[:, None, :] == 1, product, 0.0), axis=2)
        return numerator / jnp.sum(product, axis=2)

    dosage = lax.map(stretch_dosage, (alpha_starts, beta_ends, panel_blocks, geno_blocks, rate_blocks))
    dosage = dosage.transpose(2, 0, 1).reshape(H, N_GROUP * MD)
    return dosage, log_total / (N_GROUP * MD)
```

```python
import functools
import math

import jax
import jax.numpy as jnp
from jax import lax
from jax.experimental import pallas as pl
from jax.experimental.pallas import tpu as pltpu
from jax.sharding import PartitionSpec as P

HIGHEST = lax.Precision.HIGHEST
MESH = pl.DeviceIdType.MESH

MISMATCH = 0.05
STEP = 0.5 * math.log((1.0 - MISMATCH) / MISMATCH)
LOG_CENTRE = 0.5 * math.log((1.0 - MISMATCH) * MISMATCH)
UP = math.exp(STEP)
DOWN = math.exp(-STEP)
NEG = -1e30
F32 = jnp.float32
BF16 = jnp.bfloat16

MARKERS = 64
BLOCK = 8
BLOCKS = 8


def iota(shape, axis):
    return lax.broadcasted_iota(jnp.int32, shape, axis)


def dot_nt(a, b, precision=None):
    return lax.dot_general(
        a, b, (((1,), (1,)), ((), ())), precision=precision, preferred_element_type=F32
    )


def low_half(x):
    return jnp.where(iota(x.shape, 1) < 64, x, pltpu.roll(x, 64, 1))


def high_half(x):
    return jnp.where(iota(x.shape, 1) < 64, pltpu.roll(x, 64, 1), x)


def meta_tile(rate_row, geno_rows):
    eye = iota((8, 8), 0) == iota((8, 8), 1)
    lane = iota((8, 128), 1)

    def column(row):
        return jnp.sum(jnp.where(eye, jnp.broadcast_to(row, (8, 8)), 0.0), axis=1, keepdims=True)

    rate = column(rate_row)
    first = column(geno_rows[0:1].astype(F32))
    second = column(geno_rows[1:2].astype(F32))
    return jnp.where(lane == 0, rate, jnp.where(lane == 1, first, second))


def anchor_matrix():
    row = iota((128, 64), 0)
    col = iota((128, 64), 1)
    s = row
    t = row - 64
    upper = jnp.where((col >= s) & (col <= 31), 1.0, jnp.where((col >= 32) & (col < s), -1.0, 0.0))
    lower = jnp.where((col >= 32) & (col <= t), 1.0, jnp.where((col > t) & (col <= 31), -1.0, 0.0))
    return jnp.where(row < 64, upper, lower).astype(BF16)


def couplings(signs, genotype):
    width = signs.shape[1]
    sign = jnp.where(genotype == 2.0, 0.0, 2.0 * genotype - 1.0)
    steps = jnp.dot(anchor_matrix(), (signs * sign).astype(BF16), preferred_element_type=F32)
    from_s, to_t = steps[:64], steps[64:]
    u = jnp.exp(STEP * from_s)
    v = jnp.exp(STEP * to_t)
    full = jnp.log(dot_nt(u, jnp.concatenate([v, v], axis=0), HIGHEST))
    left, right = from_s[16:17], to_t[47:48]
    middle = left + right
    top = jnp.max(middle, axis=1, keepdims=True)
    begin = jnp.exp(STEP * (from_s[:16] - left + (middle - top)))
    end = jnp.exp(STEP * (to_t[48:] - right))
    blank = jnp.zeros((48, width), F32)
    corner = jnp.log(dot_nt(begin, jnp.concatenate([blank, end, blank, end], axis=0), HIGHEST))
    corner = corner + STEP * top
    return pack(full, corner)


def pack(full, corner):
    lane = iota((8, 128), 1)
    sub = iota((8, 128), 0)
    col = lane % 64
    rows = [full[8 * a : 8 * a + 8] for a in range(BLOCKS)]
    for a in range(2):
        rows[a] = jnp.where(col >= 48, corner[8 * a : 8 * a + 8], rows[a])
    diagonal = rows[0]
    for a in range(1, BLOCKS):
        diagonal = jnp.where(col // 8 == a, rows[a], diagonal)
    diagonal = jnp.where(col % 8 >= sub, diagonal, 0.0)
    pairs = []
    for a in range(4):
        other = rows[7 - a] if a == 0 else pltpu.roll(rows[7 - a], 8 * a, 1)
        pairs.append(
            jnp.where(col >= 8 * (a + 1), rows[a], jnp.where(col < 8 * a, other, 0.0))
        )
    first = jnp.where(lane < 64, pairs[0], pairs[1])
    second = jnp.where(lane < 64, pairs[2], pairs[3])
    return jnp.concatenate([first, second, diagonal], axis=0)


def unpack(packed):
    first, second, diagonal = packed[0:8], packed[8:16], packed[16:24]
    pairs = [low_half(first), high_half(first), low_half(second), high_half(second)]
    rows = [None] * BLOCKS
    for a in range(4):
        rows[a] = pairs[a]
        rows[7 - a] = pairs[a] if a == 0 else pltpu.roll(pairs[a], 128 - 8 * a, 1)
    col = iota((8, 128), 1) % 64
    return [jnp.where(col // 8 == a, diagonal, rows[a]) for a in range(BLOCKS)], diagonal


def log_total(items):
    top = functools.reduce(jnp.maximum, items)
    return top + jnp.log(functools.reduce(jnp.add, [jnp.exp(x - top) for x in items]))


def row_of(columns):
    col = iota((8, 128), 1) % 64
    sub = iota((8, 128), 0)
    total = None
    for a, column in enumerate(columns):
        part = jnp.where(col == 8 * a + sub, column, 0.0)
        total = part if total is None else total + part
    return jnp.sum(total, axis=0, keepdims=True)


def rate_terms(rates, log_k):
    lane = iota((8, 128), 1)
    col = lane % 64
    sub = iota((8, 128), 0)
    stay = [jnp.log(1.0 - r) for r in rates]
    stay_row = row_of(stay)
    sums = None
    for a in range(BLOCKS):
        part = jnp.where(8 * a + sub <= col, stay[a], 0.0)
        sums = part if sums is None else sums + part
    reach_row = jnp.sum(sums, axis=0, keepdims=True)
    reach_col = [
        jnp.sum(jnp.where((lane < 64) & (col <= 8 * a + sub), stay_row, 0.0), axis=1, keepdims=True)
        for a in range(BLOCKS)
    ]
    jump_col = [jnp.log(r) - log_k for r in rates]
    jump_row = row_of(jump_col)
    start = jnp.full((8, 1), -log_k, F32)
    jump_col[0] = jnp.where(iota((8, 1), 0) == 0, start, jump_col[0])
    return reach_row, reach_col, jump_row, jump_col


def solve(packed, terms, log_k):
    reach_row, reach_col, jump_row, jump_col = terms
    lane = iota((8, 128), 1)
    sub = iota((8, 128), 0)
    col = lane % 64
    block = col // 8
    within = col % 8
    rows, diagonal = unpack(packed)
    paths = [
        jnp.where(col >= 8 * a + sub, rows[a] + (reach_row - reach_col[a]), NEG)
        for a in range(BLOCKS)
    ]
    reach_diag = jnp.broadcast_to(reach_col[0], (8, 128))
    jump_diag = jnp.broadcast_to(jump_col[0], (8, 128))
    for a in range(1, BLOCKS):
        reach_diag = jnp.where(block == a, reach_col[a], reach_diag)
        jump_diag = jnp.where(block == a, jump_col[a], jump_diag)
    path_diag = diagonal + (reach_row - reach_diag)
    ahead = pltpu.roll(path_diag + jump_diag, 7, 0)
    behind = pltpu.roll(path_diag, 1, 1) + jump_row
    inner = jnp.exp(jnp.where(within > sub, jnp.where(lane < 64, ahead, behind), NEG))
    spread = jnp.concatenate(
        [jnp.where(lane % 8 == sub, inner[m : m + 1], 0.0) for m in range(8)], axis=0
    )
    same = (iota((128, 128), 0) // 8 == iota((128, 128), 1) // 8).astype(F32)
    columns = jnp.dot(spread, same, precision=HIGHEST, preferred_element_type=F32)
    inverse = jnp.where(within == sub, 1.0, 0.0)
    for m in range(7):
        inverse = inverse + columns[8 * m : 8 * m + 8] * inverse[m : m + 1]
    forward_inverse = low_half(inverse)
    backward_inverse = high_half(inverse)

    log_sums = []
    injected = []
    reached = jnp.zeros((1, 1), F32)
    for b in range(BLOCKS):
        lead = jnp.exp(paths[b][0:1] + jump_col[b][0:1])
        if b:
            parts = [jnp.exp((injected[a] - reached) + paths[a]) for a in range(b)]
            lead = lead + jnp.sum(functools.reduce(jnp.add, parts), axis=0, keepdims=True)
        sums = jnp.sum(
            jnp.where((block == b) & (lane < 64), lead * forward_inverse, 0.0),
            axis=1,
            keepdims=True,
        )
        here = jnp.broadcast_to(jnp.log(sums) + reached, (8, 128))
        log_sums.append(here)
        injected.append(jump_col[b] + jnp.where(sub == 0, reached, pltpu.roll(here, 1, 0)))
        reached = here[7:8, 0:1]

    row_lane = iota((1, 128), 1)
    row_col = row_lane % 64
    behind_row = jnp.where(row_col == 63, -log_k, NEG)
    back_sums = jnp.zeros((1, 128), F32)
    reached = jnp.zeros((1, 1), F32)
    for b in reversed(range(BLOCKS)):
        lead = jnp.sum(
            jnp.where(lane < 64, jnp.exp(paths[b] + (behind_row - reached)), 0.0),
            axis=1,
            keepdims=True,
        )
        sums = jnp.sum(lead * backward_inverse, axis=0, keepdims=True)
        here = jnp.log(sums) + reached
        back_sums = jnp.where(row_col // 8 == b, here, back_sums)
        if b:
            fresh = pltpu.roll(here + jump_row, 127, 1)
            inside = (row_col >= 8 * b - 1) & (row_col <= 8 * b + 6)
            behind_row = jnp.where(inside, fresh, behind_row)
            reached = here[0:1, 8 * b : 8 * b + 1]
    forward_row = row_of(log_sums)
    return jnp.where(row_lane < 64, forward_row, back_sums)


def by_target(first, second):
    return jnp.where(iota((8, 128), 0) < 4, first, second)


def emission_terms(geno_rows):
    g = by_target(geno_rows[0], geno_rows[1])
    base = jnp.where(g == 2.0, 1.0, jnp.where(g == 1.0, DOWN, UP))
    slope = jnp.where(g == 2.0, 0.0, jnp.where(g == 1.0, UP - DOWN, DOWN - UP))
    return base, slope


def state_terms(solved, rate_row, k):
    lane = iota((8, 128), 1)
    logs = by_target(solved[0], solved[1])
    before = jnp.where(lane == 0, 0.0, pltpu.roll(logs, 1, 1))
    after = jnp.where(lane == 127, 0.0, pltpu.roll(logs, 127, 1))
    over_forward = jnp.exp(before - logs)
    over_backward = pltpu.roll(jnp.exp(after - logs), 64, 1)
    keep = 1.0 - rate_row
    jump = rate_row * (1.0 / k)
    return (
        keep * over_forward,
        jump * over_forward,
        keep * over_backward,
        jnp.broadcast_to(jump, (8, 128)),
    )


def dosage_of(total):
    lane = iota((8, 128), 1)
    sub = iota((8, 128), 0)
    picked = jnp.where((lane // 4) % 2 == sub, total, 0.0)
    src = iota((128, 128), 0)
    dst = iota((128, 128), 1)
    upper = ((src // 8 == dst) & (src < 64)).astype(F32)
    lower = (src // 8 == dst + 8).astype(F32)
    numerator = jnp.dot(picked, upper, precision=HIGHEST, preferred_element_type=F32)
    denominator = jnp.dot(picked, lower, precision=HIGHEST, preferred_element_type=F32)
    return numerator[0:2, 0:8] / denominator[0:2, 0:8]


def kernel(
    n_y, n_z, k,
    panel_ref, rate_ref, geno_ref,
    dosage_ref, like_ref,
    panel_all, meta_all, tiles, emis, fwd, bwd,
    log_send, log_group, log_mid, log_y, log_last, log_z,
    solve_send, solve_recv, sum_send, sum_group, sum_mid, sum_y, sum_last, sum_z,
    own_sem, tile_sem,
    panel_s, panel_r, meta_s, meta_r, group_s, group_r, y_s, y_r, z_s, z_r,
    core_s, core_r, group2_s, group2_r, y2_s, y2_r, z2_s, z2_r,
):
    n_group = BLOCKS
    group = lax.axis_index("group")
    batch = lax.axis_index("batch")
    core = group % 2
    y = batch % n_y
    z = batch // n_y
    width = panel_all.shape[2]
    log_k = math.log(k)

    def in_group(d):
        return (group + d) % n_group

    def group_peer(d):
        return (in_group(d), batch)

    def y_peer(d):
        return (group, z * n_y + (y + d) % n_y)

    def z_peer(d):
        return (group, ((z + d) % n_z) * n_y + y)

    def far_first(n):
        return sorted(range(1, n), key=lambda d: -min(d, n - d))

    barrier = pltpu.get_barrier_semaphore()
    peers = [z_peer(d) for d in far_first(n_z)]
    peers += [group_peer(d) for d in far_first(n_group)]
    peers += [y_peer(d) for d in far_first(n_y)]
    for peer in peers:
        pl.semaphore_signal(barrier, inc=1, device_id=peer, device_id_type=MESH)
    own_panel = pltpu.make_async_copy(
        panel_ref.at[:, pl.ds(pl.multiple_of(group * width, width), width)],
        panel_all.at[group],
        own_sem,
    )
    own_panel.start()
    meta_all[group] = meta_tile(rate_ref[...], geno_ref[...])
    pl.semaphore_wait(barrier, len(peers))

    def remote(src, dst, send, recv, peer):
        return pltpu.make_async_remote_copy(
            src_ref=src, dst_ref=dst, send_sem=send, recv_sem=recv,
            device_id=peer, device_id_type=MESH,
        )

    copies = []
    for d in far_first(n_group):
        start = pl.multiple_of(in_group(d) * width, width)
        copies.append(
            remote(
                panel_ref.at[:, pl.ds(start, width)], panel_all.at[group],
                panel_s.at[d - 1], panel_r.at[d - 1], group_peer(d),
            )
        )
        copies.append(
            remote(
                meta_all.at[group], meta_all.at[group],
                meta_s.at[d - 1], meta_r.at[d - 1], group_peer(d),
            )
        )
    for copy in copies:
        copy.start()
    own_panel.wait()
    for copy in copies:
        copy.wait()

    relayout = []
    for c in range(4):
        for h in range(2):
            copy = pltpu.make_async_copy(
                panel_all.at[:, :, pl.ds(128 * c, 128)],
                tiles.at[:, :, 4 * h + c],
                tile_sem.at[4 * h + c],
            )
            copy.start()
            relayout.append(copy)

    meta = meta_all[...].reshape(MARKERS, 128)
    signs = 2.0 * panel_all[...].reshape(MARKERS, width).astype(F32) - 1.0
    for h in range(2):
        log_send[h] = couplings(signs, meta[:, 1 + h : 2 + h])

    def start_all(n, order, src, slots, send, recv, peer):
        out = [
            remote(src(d), slots.at[d - 1], send.at[d - 1], recv.at[d - 1], peer(d)) for d in order
        ]
        for copy in out:
            copy.start()
        return out

    def finish(copies):
        for copy in copies:
            copy.wait()

    flying = start_all(
        n_group, far_first(n_group), lambda d: log_send.at[in_group(d) % 2],
        log_group, group_s, group_r, group_peer,
    )
    rates = [meta[8 * a : 8 * a + 8, 0:1] for a in range(BLOCKS)]
    terms = rate_terms(rates, log_k)
    rate_row = row_of(rates)
    geno_rows = [
        row_of([meta[8 * a : 8 * a + 8, 1 + h : 2 + h] for a in range(BLOCKS)]) for h in range(2)
    ]
    finish(flying)
    total = log_total([log_send[core]] + [log_group[d] for d in range(n_group - 1)])
    if n_y > 1:
        log_mid[...] = total
        flying = start_all(
            n_y, far_first(n_y), lambda d: log_mid, log_y, y_s, y_r, y_peer
        )
        finish(relayout)
        finish(flying)
        total = log_total([total] + [log_y[d] for d in range(n_y - 1)])
    else:
        finish(relayout)
    base, slope = emission_terms(geno_rows)

    def emissions():
        for t in range(MARKERS):
            allele = tiles[t // 8, t % 8].astype(F32)
            emis[t] = base[:, t : t + 1] + slope[:, t : t + 1] * allele

    if n_z > 1:
        log_last[...] = total
        flying = start_all(
            n_z, far_first(n_z), lambda d: log_last, log_z, z_s, z_r, z_peer
        )
        emissions()
        finish(flying)
        total = log_total([total] + [log_z[d] for d in range(n_z - 1)])
    else:
        emissions()

    mine = solve(total, terms, log_k)
    solve_send[...] = mine
    partner = (group + 1 - 2 * core, batch)
    swap = remote(solve_send, solve_recv, core_s, core_r, partner)
    swap.start()
    swap.wait()
    theirs = solve_recv[...]
    solved = [jnp.where(core == 0, mine, theirs), jnp.where(core == 0, theirs, mine)]

    lane_row = iota((1, 128), 1)
    likes = []
    for h in range(2):
        seen = jnp.sum(
            jnp.where((lane_row < 64) & (geno_rows[h] != 2.0), LOG_CENTRE, 0.0),
            axis=1, keepdims=True,
        )
        likes.append((solved[h][:, 63:64] + seen) * (1.0 / MARKERS))
    like_ref[...] = jnp.where(lane_row == 0, likes[0], likes[1])[:, 0:2]

    keep_f, jump_f, keep_b, jump_b = state_terms(solved, rate_row, float(k))
    ahead = jnp.full((8, 128), 1.0 / k, F32)
    behind = jnp.full((8, 128), 1.0 / k, F32)
    for i in range(MARKERS):
        ahead = emis[i] * (keep_f[:, i : i + 1] * ahead + jump_f[:, i : i + 1])
        fwd[i] = ahead
        t = MARKERS - 1 - i
        bwd[t] = behind
        behind = keep_b[:, t : t + 1] * (emis[t] * behind) + jump_b[:, t : t + 1]

    ones = jnp.ones((8, 128), BF16)
    for a in range(BLOCKS):
        both = fwd[8 * a : 8 * a + 8] * bwd[8 * a : 8 * a + 8]
        carrying = both * tiles[a].astype(F32)
        stacked = jnp.concatenate([carrying.reshape(64, 128), both.reshape(64, 128)], axis=0)
        coarse = stacked.astype(BF16)
        fine = (stacked - coarse.astype(F32)).astype(BF16)
        sums = dot_nt(ones, coarse) + dot_nt(ones, fine)
        sum_send[a] = sums[0:1]

    flying = start_all(
        n_group, far_first(n_group), lambda d: sum_send.at[in_group(d)],
        sum_group, group2_s, group2_r, group_peer,
    )
    finish(flying)
    total = functools.reduce(
        jnp.add, [sum_send[group]] + [sum_group[d] for d in range(n_group - 1)]
    )
    if n_y > 1:
        sum_mid[...] = total
        flying = start_all(
            n_y, far_first(n_y), lambda d: sum_mid, sum_y, y2_s, y2_r, y_peer
        )
        finish(flying)
        total = functools.reduce(jnp.add, [total] + [sum_y[d] for d in range(n_y - 1)])
    if n_z > 1:
        sum_last[...] = total
        flying = start_all(
            n_z, far_first(n_z), lambda d: sum_last, sum_z, z2_s, z2_r, z_peer
        )
        finish(flying)
        total = functools.reduce(jnp.add, [total] + [sum_z[d] for d in range(n_z - 1)])
    dosage_ref[...] = dosage_of(total)


def on_device(n_y, panel, rates, genotypes):
    n_batch = lax.axis_size("batch")
    n_group = lax.axis_size("group")
    n_z = n_batch // n_y
    width = panel.shape[1] // n_group
    k = panel.shape[1] * n_batch
    dma = pltpu.SemaphoreType.DMA
    vmem = pltpu.VMEM
    g1, y1, z1 = n_group - 1, max(n_y - 1, 1), max(n_z - 1, 1)
    scratch = [
        vmem((BLOCKS, BLOCK, width), jnp.int32),
        vmem((BLOCKS, BLOCK, 128), F32),
        vmem((BLOCKS, BLOCK, 8, 128), jnp.int32),
        vmem((MARKERS, 8, 128), F32),
        vmem((MARKERS, 8, 128), F32),
        vmem((MARKERS, 8, 128), F32),
        vmem((2, 24, 128), F32),
        vmem((g1, 24, 128), F32),
        vmem((24, 128), F32),
        vmem((y1, 24, 128), F32),
        vmem((24, 128), F32),
        vmem((z1, 24, 128), F32),
        vmem((1, 128), F32),
        vmem((1, 128), F32),
        vmem((BLOCKS, 1, 128), F32),
        vmem((g1, 1, 128), F32),
        vmem((1, 128), F32),
        vmem((y1, 1, 128), F32),
        vmem((1, 128), F32),
        vmem((z1, 1, 128), F32),
        dma,
        dma((8,)),
        dma((g1,)), dma((g1,)), dma((g1,)), dma((g1,)), dma((g1,)), dma((g1,)),
        dma((y1,)), dma((y1,)), dma((z1,)), dma((z1,)),
        dma, dma,
        dma((g1,)), dma((g1,)), dma((y1,)), dma((y1,)), dma((z1,)), dma((z1,)),
    ]
    dosage, like = pl.pallas_call(
        functools.partial(kernel, n_y, n_z, k),
        out_shape=(
            jax.ShapeDtypeStruct((2, BLOCK), F32),
            jax.ShapeDtypeStruct((1, 2), F32),
        ),
        in_specs=[
            pl.BlockSpec(memory_space=pl.ANY),
            pl.BlockSpec(memory_space=pltpu.VMEM),
            pl.BlockSpec(memory_space=pltpu.VMEM),
        ],
        out_specs=(
            pl.BlockSpec(memory_space=pltpu.VMEM),
            pl.BlockSpec(memory_space=pltpu.VMEM),
        ),
        scratch_shapes=scratch,
        compiler_params=pltpu.CompilerParams(collective_id=0, has_side_effects=True),
    )(panel, rates.reshape(1, BLOCK), genotypes)
    return dosage, like.reshape(2)


def solution(mesh, n_y=4):
    placed = (P("group", "batch"), P("group"), P(None, "group"))
    return jax.shard_map(
        functools.partial(on_device, n_y),
        mesh=mesh,
        in_specs=placed,
        out_specs=(P(None, "group"), P()),
        check_vma=False,
    )
```

```python
import functools
import math

import jax
import jax.numpy as jnp
from jax import lax
from jax.experimental import pallas as pl
from jax.experimental.pallas import tpu as pltpu
from jax.sharding import PartitionSpec as P

HIGHEST = lax.Precision.HIGHEST
MESH = pl.DeviceIdType.MESH

MISMATCH = 0.05
STEP = 0.5 * math.log((1.0 - MISMATCH) / MISMATCH)
LOG_CENTRE = 0.5 * math.log((1.0 - MISMATCH) * MISMATCH)
UP = math.exp(STEP)
DOWN = math.exp(-STEP)
NEG = -1e30
F32 = jnp.float32
BF16 = jnp.bfloat16

MARKERS = 64
BLOCK = 8
BLOCKS = 8


def iota(shape, axis):
    return lax.broadcasted_iota(jnp.int32, shape, axis)


def dot_nt(a, b, precision=None):
    return lax.dot_general(
        a, b, (((1,), (1,)), ((), ())), precision=precision, preferred_element_type=F32
    )


def low_half(x):
    return jnp.where(iota(x.shape, 1) < 64, x, pltpu.roll(x, 64, 1))


def high_half(x):
    return jnp.where(iota(x.shape, 1) < 64, pltpu.roll(x, 64, 1), x)


def meta_tile(rate_row, geno_rows):
    eye = iota((8, 8), 0) == iota((8, 8), 1)
    lane = iota((8, 128), 1)

    def column(row):
        return jnp.sum(jnp.where(eye, jnp.broadcast_to(row, (8, 8)), 0.0), axis=1, keepdims=True)

    rate = column(rate_row)
    first = column(geno_rows[0:1].astype(F32))
    second = column(geno_rows[1:2].astype(F32))
    return jnp.where(lane == 0, rate, jnp.where(lane == 1, first, second))


def anchor_matrix():
    row = iota((128, 64), 0)
    col = iota((128, 64), 1)
    s = row
    t = row - 64
    upper = jnp.where((col >= s) & (col <= 31), 1.0, jnp.where((col >= 32) & (col < s), -1.0, 0.0))
    lower = jnp.where((col >= 32) & (col <= t), 1.0, jnp.where((col > t) & (col <= 31), -1.0, 0.0))
    return jnp.where(row < 64, upper, lower).astype(BF16)


def couplings(signs, genotype):
    width = signs.shape[1]
    sign = jnp.where(genotype == 2.0, 0.0, 2.0 * genotype - 1.0)
    steps = jnp.dot(anchor_matrix(), (signs * sign).astype(BF16), preferred_element_type=F32)
    from_s, to_t = steps[:64], steps[64:]
    u = jnp.exp(STEP * from_s)
    v = jnp.exp(STEP * to_t)
    full = jnp.log(dot_nt(u, jnp.concatenate([v, v], axis=0), HIGHEST))
    left, right = from_s[16:17], to_t[47:48]
    middle = left + right
    top = jnp.max(middle, axis=1, keepdims=True)
    begin = jnp.exp(STEP * (from_s[:16] - left + (middle - top)))
    end = jnp.exp(STEP * (to_t[48:] - right))
    blank = jnp.zeros((48, width), F32)
    corner = jnp.log(dot_nt(begin, jnp.concatenate([blank, end, blank, end], axis=0), HIGHEST))
    corner = corner + STEP * top
    return pack(full, corner)


def pack(full, corner):
    lane = iota((8, 128), 1)
    sub = iota((8, 128), 0)
    col = lane % 64
    rows = [full[8 * a : 8 * a + 8] for a in range(BLOCKS)]
    for a in range(2):
        rows[a] = jnp.where(col >= 48, corner[8 * a : 8 * a + 8], rows[a])
    diagonal = rows[0]
    for a in range(1, BLOCKS):
        diagonal = jnp.where(col // 8 == a, rows[a], diagonal)
    diagonal = jnp.where(col % 8 >= sub, diagonal, 0.0)
    pairs = []
    for a in range(4):
        other = rows[7 - a] if a == 0 else pltpu.roll(rows[7 - a], 8 * a, 1)
        pairs.append(
            jnp.where(col >= 8 * (a + 1), rows[a], jnp.where(col < 8 * a, other, 0.0))
        )
    first = jnp.where(lane < 64, pairs[0], pairs[1])
    second = jnp.where(lane < 64, pairs[2], pairs[3])
    return jnp.concatenate([first, second, diagonal], axis=0)


def unpack(packed):
    first, second, diagonal = packed[0:8], packed[8:16], packed[16:24]
    pairs = [low_half(first), high_half(first), low_half(second), high_half(second)]
    rows = [None] * BLOCKS
    for a in range(4):
        rows[a] = pairs[a]
        rows[7 - a] = pairs[a] if a == 0 else pltpu.roll(pairs[a], 128 - 8 * a, 1)
    col = iota((8, 128), 1) % 64
    return [jnp.where(col // 8 == a, diagonal, rows[a]) for a in range(BLOCKS)], diagonal


def log_total(items):
    top = functools.reduce(jnp.maximum, items)
    return top + jnp.log(functools.reduce(jnp.add, [jnp.exp(x - top) for x in items]))


def row_of(columns):
    col = iota((8, 128), 1) % 64
    sub = iota((8, 128), 0)
    total = None
    for a, column in enumerate(columns):
        part = jnp.where(col == 8 * a + sub, column, 0.0)
        total = part if total is None else total + part
    return jnp.sum(total, axis=0, keepdims=True)


def rate_terms(rates, log_k):
    lane = iota((8, 128), 1)
    col = lane % 64
    sub = iota((8, 128), 0)
    stay = [jnp.log(1.0 - r) for r in rates]
    stay_row = row_of(stay)
    sums = None
    for a in range(BLOCKS):
        part = jnp.where(8 * a + sub <= col, stay[a], 0.0)
        sums = part if sums is None else sums + part
    reach_row = jnp.sum(sums, axis=0, keepdims=True)
    reach_col = [
        jnp.sum(jnp.where((lane < 64) & (col <= 8 * a + sub), stay_row, 0.0), axis=1, keepdims=True)
        for a in range(BLOCKS)
    ]
    jump_col = [jnp.log(r) - log_k for r in rates]
    jump_row = row_of(jump_col)
    start = jnp.full((8, 1), -log_k, F32)
    jump_col[0] = jnp.where(iota((8, 1), 0) == 0, start, jump_col[0])
    return reach_row, reach_col, jump_row, jump_col


def solve(packed, terms, log_k):
    reach_row, reach_col, jump_row, jump_col = terms
    lane = iota((8, 128), 1)
    sub = iota((8, 128), 0)
    col = lane % 64
    block = col // 8
    within = col % 8
    rows, diagonal = unpack(packed)
    paths = [
        jnp.where(col >= 8 * a + sub, rows[a] + (reach_row - reach_col[a]), NEG)
        for a in range(BLOCKS)
    ]
    reach_diag = jnp.broadcast_to(reach_col[0], (8, 128))
    jump_diag = jnp.broadcast_to(jump_col[0], (8, 128))
    for a in range(1, BLOCKS):
        reach_diag = jnp.where(block == a, reach_col[a], reach_diag)
        jump_diag = jnp.where(block == a, jump_col[a], jump_diag)
    path_diag = diagonal + (reach_row - reach_diag)
    ahead = pltpu.roll(path_diag + jump_diag, 7, 0)
    behind = pltpu.roll(path_diag, 1, 1) + jump_row
    inner = jnp.exp(jnp.where(within > sub, jnp.where(lane < 64, ahead, behind), NEG))
    spread = jnp.concatenate(
        [jnp.where(lane % 8 == sub, inner[m : m + 1], 0.0) for m in range(8)], axis=0
    )
    same = (iota((128, 128), 0) // 8 == iota((128, 128), 1) // 8).astype(F32)
    columns = jnp.dot(spread, same, precision=HIGHEST, preferred_element_type=F32)
    inverse = jnp.where(within == sub, 1.0, 0.0)
    for m in range(7):
        inverse = inverse + columns[8 * m : 8 * m + 8] * inverse[m : m + 1]
    forward_inverse = low_half(inverse)
    backward_inverse = high_half(inverse)

    log_sums = []
    injected = []
    reached = jnp.zeros((1, 1), F32)
    for b in range(BLOCKS):
        lead = jnp.exp(paths[b][0:1] + jump_col[b][0:1])
        if b:
            parts = [jnp.exp((injected[a] - reached) + paths[a]) for a in range(b)]
            lead = lead + jnp.sum(functools.reduce(jnp.add, parts), axis=0, keepdims=True)
        sums = jnp.sum(
            jnp.where((block == b) & (lane < 64), lead * forward_inverse, 0.0),
            axis=1,
            keepdims=True,
        )
        here = jnp.broadcast_to(jnp.log(sums) + reached, (8, 128))
        log_sums.append(here)
        injected.append(jump_col[b] + jnp.where(sub == 0, reached, pltpu.roll(here, 1, 0)))
        reached = here[7:8, 0:1]

    row_lane = iota((1, 128), 1)
    row_col = row_lane % 64
    behind_row = jnp.where(row_col == 63, -log_k, NEG)
    back_sums = jnp.zeros((1, 128), F32)
    reached = jnp.zeros((1, 1), F32)
    for b in reversed(range(BLOCKS)):
        lead = jnp.sum(
            jnp.where(lane < 64, jnp.exp(paths[b] + (behind_row - reached)), 0.0),
            axis=1,
            keepdims=True,
        )
        sums = jnp.sum(lead * backward_inverse, axis=0, keepdims=True)
        here = jnp.log(sums) + reached
        back_sums = jnp.where(row_col // 8 == b, here, back_sums)
        if b:
            fresh = pltpu.roll(here + jump_row, 127, 1)
            inside = (row_col >= 8 * b - 1) & (row_col <= 8 * b + 6)
            behind_row = jnp.where(inside, fresh, behind_row)
            reached = here[0:1, 8 * b : 8 * b + 1]
    forward_row = row_of(log_sums)
    return jnp.where(row_lane < 64, forward_row, back_sums)


def by_target(first, second):
    return jnp.where(iota((8, 128), 0) < 4, first, second)


def emission_terms(geno_rows):
    g = by_target(geno_rows[0], geno_rows[1])
    base = jnp.where(g == 2.0, 1.0, jnp.where(g == 1.0, DOWN, UP))
    slope = jnp.where(g == 2.0, 0.0, jnp.where(g == 1.0, UP - DOWN, DOWN - UP))
    return base, slope


def state_terms(solved, rate_row, k):
    lane = iota((8, 128), 1)
    logs = by_target(solved[0], solved[1])
    before = jnp.where(lane == 0, 0.0, pltpu.roll(logs, 1, 1))
    after = jnp.where(lane == 127, 0.0, pltpu.roll(logs, 127, 1))
    over_forward = jnp.exp(before - logs)
    over_backward = pltpu.roll(jnp.exp(after - logs), 64, 1)
    keep = 1.0 - rate_row
    jump = rate_row * (1.0 / k)
    return (
        keep * over_forward,
        jump * over_forward,
        keep * over_backward,
        jnp.broadcast_to(jump, (8, 128)),
    )


def dosage_of(total):
    lane = iota((8, 128), 1)
    sub = iota((8, 128), 0)
    picked = jnp.where((lane // 4) % 2 == sub, total, 0.0)
    src = iota((128, 128), 0)
    dst = iota((128, 128), 1)
    upper = ((src // 8 == dst) & (src < 64)).astype(F32)
    lower = (src // 8 == dst + 8).astype(F32)
    numerator = jnp.dot(picked, upper, precision=HIGHEST, preferred_element_type=F32)
    denominator = jnp.dot(picked, lower, precision=HIGHEST, preferred_element_type=F32)
    return numerator[0:2, 0:8] / denominator[0:2, 0:8]


def kernel(
    n_y, n_z, k,
    panel_ref, rate_ref, geno_ref,
    dosage_ref, like_ref,
    panel_all, meta_all, tiles, emis, fwd, bwd,
    log_send, log_group, log_mid, log_y, log_last, log_z,
    solve_send, solve_recv, sum_send, sum_group, sum_mid, sum_batch,
    own_sem, tile_sem,
    panel_s, panel_r, meta_s, meta_r, group_s, group_r, y_s, y_r, z_s, z_r,
    core_s, core_r, group2_s, group2_r, batch_s, batch_r,
):
    n_group = BLOCKS
    group = lax.axis_index("group")
    batch = lax.axis_index("batch")
    core = group % 2
    y = batch % n_y
    z = batch // n_y
    width = panel_all.shape[2]
    log_k = math.log(k)

    def in_group(d):
        return (group + d) % n_group

    def group_peer(d):
        return (in_group(d), batch)

    def y_peer(d):
        return (group, z * n_y + (y + d) % n_y)

    def z_peer(d):
        return (group, ((z + d) % n_z) * n_y + y)

    def far_first(n):
        return sorted(range(1, n), key=lambda d: -min(d, n - d))

    barrier = pltpu.get_barrier_semaphore()
    peers = [group_peer(d) for d in far_first(n_group)]
    peers += [z_peer(d) for d in far_first(n_z)]
    peers += [y_peer(d) for d in far_first(n_y)]
    for peer in peers:
        pl.semaphore_signal(barrier, inc=1, device_id=peer, device_id_type=MESH)
    own_panel = pltpu.make_async_copy(
        panel_ref.at[:, pl.ds(pl.multiple_of(group * width, width), width)],
        panel_all.at[group],
        own_sem,
    )
    own_panel.start()
    meta_all[group] = meta_tile(rate_ref[...], geno_ref[...])
    pl.semaphore_wait(barrier, len(peers))

    def remote(src, dst, send, recv, peer):
        return pltpu.make_async_remote_copy(
            src_ref=src, dst_ref=dst, send_sem=send, recv_sem=recv,
            device_id=peer, device_id_type=MESH,
        )

    copies = []
    for d in far_first(n_group):
        start = pl.multiple_of(in_group(d) * width, width)
        copies.append(
            remote(
                panel_ref.at[:, pl.ds(start, width)], panel_all.at[group],
                panel_s.at[d - 1], panel_r.at[d - 1], group_peer(d),
            )
        )
        copies.append(
            remote(
                meta_all.at[group], meta_all.at[group],
                meta_s.at[d - 1], meta_r.at[d - 1], group_peer(d),
            )
        )
    for copy in copies:
        copy.start()
    own_panel.wait()
    for copy in copies:
        copy.wait()

    relayout = []
    for c in range(4):
        for h in range(2):
            copy = pltpu.make_async_copy(
                panel_all.at[:, :, pl.ds(128 * c, 128)],
                tiles.at[:, :, 4 * h + c],
                tile_sem.at[4 * h + c],
            )
            copy.start()
            relayout.append(copy)

    meta = meta_all[...].reshape(MARKERS, 128)
    signs = 2.0 * panel_all[...].reshape(MARKERS, width).astype(F32) - 1.0
    for h in range(2):
        log_send[h] = couplings(signs, meta[:, 1 + h : 2 + h])

    def start_all(n, order, src, slots, send, recv, peer):
        out = [
            remote(src(d), slots.at[d - 1], send.at[d - 1], recv.at[d - 1], peer(d)) for d in order
        ]
        for copy in out:
            copy.start()
        return out

    def finish(copies):
        for copy in copies:
            copy.wait()

    flying = start_all(
        n_group, far_first(n_group), lambda d: log_send.at[in_group(d) % 2],
        log_group, group_s, group_r, group_peer,
    )
    rates = [meta[8 * a : 8 * a + 8, 0:1] for a in range(BLOCKS)]
    terms = rate_terms(rates, log_k)
    rate_row = row_of(rates)
    geno_rows = [
        row_of([meta[8 * a : 8 * a + 8, 1 + h : 2 + h] for a in range(BLOCKS)]) for h in range(2)
    ]
    finish(flying)
    total = log_total([log_send[core]] + [log_group[d] for d in range(n_group - 1)])
    if n_y > 1:
        log_mid[...] = total
        flying = start_all(
            n_y, far_first(n_y), lambda d: log_mid, log_y, y_s, y_r, y_peer
        )
        finish(flying)
        total = log_total([total] + [log_y[d] for d in range(n_y - 1)])
    base, slope = emission_terms(geno_rows)

    def emissions():
        finish(relayout)
        for t in range(MARKERS):
            allele = tiles[t // 8, t % 8].astype(F32)
            emis[t] = base[:, t : t + 1] + slope[:, t : t + 1] * allele

    if n_z > 1:
        log_last[...] = total
        flying = start_all(
            n_z, far_first(n_z), lambda d: log_last, log_z, z_s, z_r, z_peer
        )
        emissions()
        finish(flying)
        total = log_total([total] + [log_z[d] for d in range(n_z - 1)])
    else:
        emissions()

    mine = solve(total, terms, log_k)
    solve_send[...] = mine
    partner = (group + 1 - 2 * core, batch)
    swap = remote(solve_send, solve_recv, core_s, core_r, partner)
    swap.start()
    swap.wait()
    theirs = solve_recv[...]
    solved = [jnp.where(core == 0, mine, theirs), jnp.where(core == 0, theirs, mine)]

    lane_row = iota((1, 128), 1)
    likes = []
    for h in range(2):
        seen = jnp.sum(
            jnp.where((lane_row < 64) & (geno_rows[h] != 2.0), LOG_CENTRE, 0.0),
            axis=1, keepdims=True,
        )
        likes.append((solved[h][:, 63:64] + seen) * (1.0 / MARKERS))
    like_ref[...] = jnp.where(lane_row == 0, likes[0], likes[1])[:, 0:2]

    keep_f, jump_f, keep_b, jump_b = state_terms(solved, rate_row, float(k))
    ahead = jnp.full((8, 128), 1.0 / k, F32)
    behind = jnp.full((8, 128), 1.0 / k, F32)
    for i in range(MARKERS):
        ahead = emis[i] * (keep_f[:, i : i + 1] * ahead + jump_f[:, i : i + 1])
        fwd[i] = ahead
        t = MARKERS - 1 - i
        bwd[t] = behind
        behind = keep_b[:, t : t + 1] * (emis[t] * behind) + jump_b[:, t : t + 1]

    ones = jnp.ones((8, 128), BF16)
    for a in range(BLOCKS):
        both = fwd[8 * a : 8 * a + 8] * bwd[8 * a : 8 * a + 8]
        carrying = both * tiles[a].astype(F32)
        stacked = jnp.concatenate([carrying.reshape(64, 128), both.reshape(64, 128)], axis=0)
        coarse = stacked.astype(BF16)
        fine = (stacked - coarse.astype(F32)).astype(BF16)
        sums = dot_nt(ones, coarse) + dot_nt(ones, fine)
        sum_send[a] = sums[0:1]

    flying = start_all(
        n_group, far_first(n_group), lambda d: sum_send.at[in_group(d)],
        sum_group, group2_s, group2_r, group_peer,
    )
    finish(flying)
    total = functools.reduce(
        jnp.add, [sum_send[group]] + [sum_group[d] for d in range(n_group - 1)]
    )
    n_batch = n_y * n_z
    sum_mid[...] = total
    flying = [
        remote(
            sum_mid, sum_batch.at[pl.ds(d - 1, 1)], batch_s.at[d - 1], batch_r.at[d - 1],
            (group, (batch + d) % n_batch),
        )
        for d in range(1, n_batch)
    ]
    for copy in flying:
        copy.start()
    sum_batch[n_batch - 1 : n_batch] = total
    finish(flying)
    total = jnp.sum(sum_batch[...], axis=0, keepdims=True)
    dosage_ref[...] = dosage_of(total)


def on_device(n_y, panel, rates, genotypes):
    n_batch = lax.axis_size("batch")
    n_group = lax.axis_size("group")
    n_z = n_batch // n_y
    width = panel.shape[1] // n_group
    k = panel.shape[1] * n_batch
    dma = pltpu.SemaphoreType.DMA
    vmem = pltpu.VMEM
    g1, y1, z1 = n_group - 1, max(n_y - 1, 1), max(n_z - 1, 1)
    scratch = [
        vmem((BLOCKS, BLOCK, width), jnp.int32),
        vmem((BLOCKS, BLOCK, 128), F32),
        vmem((BLOCKS, BLOCK, 8, 128), jnp.int32),
        vmem((MARKERS, 8, 128), F32),
        vmem((MARKERS, 8, 128), F32),
        vmem((MARKERS, 8, 128), F32),
        vmem((2, 24, 128), F32),
        vmem((g1, 24, 128), F32),
        vmem((24, 128), F32),
        vmem((y1, 24, 128), F32),
        vmem((24, 128), F32),
        vmem((z1, 24, 128), F32),
        vmem((1, 128), F32),
        vmem((1, 128), F32),
        vmem((BLOCKS, 1, 128), F32),
        vmem((g1, 1, 128), F32),
        vmem((1, 128), F32),
        vmem((n_batch, 128), F32),
        dma,
        dma((8,)),
        dma((g1,)), dma((g1,)), dma((g1,)), dma((g1,)), dma((g1,)), dma((g1,)),
        dma((y1,)), dma((y1,)), dma((z1,)), dma((z1,)),
        dma, dma,
        dma((g1,)), dma((g1,)), dma((n_batch - 1,)), dma((n_batch - 1,)),
    ]
    dosage, like = pl.pallas_call(
        functools.partial(kernel, n_y, n_z, k),
        out_shape=(
            jax.ShapeDtypeStruct((2, BLOCK), F32),
            jax.ShapeDtypeStruct((1, 2), F32),
        ),
        in_specs=[
            pl.BlockSpec(memory_space=pl.ANY),
            pl.BlockSpec(memory_space=pltpu.VMEM),
            pl.BlockSpec(memory_space=pltpu.VMEM),
        ],
        out_specs=(
            pl.BlockSpec(memory_space=pltpu.VMEM),
            pl.BlockSpec(memory_space=pltpu.VMEM),
        ),
        scratch_shapes=scratch,
        compiler_params=pltpu.CompilerParams(collective_id=0, has_side_effects=True),
    )(panel, rates.reshape(1, BLOCK), genotypes)
    return dosage, like.reshape(2)


def solution(mesh, n_y=4):
    placed = (P("group", "batch"), P("group"), P(None, "group"))
    return jax.shard_map(
        functools.partial(on_device, n_y),
        mesh=mesh,
        in_specs=placed,
        out_specs=(P(None, "group"), P()),
        check_vma=False,
    )
```

```python
import functools
import math

import jax
import jax.numpy as jnp
from jax import lax
from jax.experimental import pallas as pl
from jax.experimental.pallas import tpu as pltpu
from jax.sharding import PartitionSpec as P

HIGHEST = lax.Precision.HIGHEST
MESH = pl.DeviceIdType.MESH

MISMATCH = 0.05
STEP = 0.5 * math.log((1.0 - MISMATCH) / MISMATCH)
LOG_CENTRE = 0.5 * math.log((1.0 - MISMATCH) * MISMATCH)
UP = math.exp(STEP)
DOWN = math.exp(-STEP)
NEG = -1e30
F32 = jnp.float32
BF16 = jnp.bfloat16

MARKERS = 64
BLOCK = 8
BLOCKS = 8


def iota(shape, axis):
    return lax.broadcasted_iota(jnp.int32, shape, axis)


def dot_nt(a, b, precision=None):
    return lax.dot_general(
        a, b, (((1,), (1,)), ((), ())), precision=precision, preferred_element_type=F32
    )


def low_half(x):
    return jnp.where(iota(x.shape, 1) < 64, x, pltpu.roll(x, 64, 1))


def high_half(x):
    return jnp.where(iota(x.shape, 1) < 64, pltpu.roll(x, 64, 1), x)


def meta_tile(rate_row, geno_rows):
    eye = iota((8, 8), 0) == iota((8, 8), 1)
    lane = iota((8, 128), 1)

    def column(row):
        return jnp.sum(jnp.where(eye, jnp.broadcast_to(row, (8, 8)), 0.0), axis=1, keepdims=True)

    rate = column(rate_row)
    first = column(geno_rows[0:1].astype(F32))
    second = column(geno_rows[1:2].astype(F32))
    return jnp.where(lane == 0, rate, jnp.where(lane == 1, first, second))


def anchor_matrix():
    row = iota((128, 64), 0)
    col = iota((128, 64), 1)
    s = row
    t = row - 64
    upper = jnp.where((col >= s) & (col <= 31), 1.0, jnp.where((col >= 32) & (col < s), -1.0, 0.0))
    lower = jnp.where((col >= 32) & (col <= t), 1.0, jnp.where((col > t) & (col <= 31), -1.0, 0.0))
    return jnp.where(row < 64, upper, lower).astype(BF16)


def couplings(signs, genotype):
    width = signs.shape[1]
    sign = jnp.where(genotype == 2.0, 0.0, 2.0 * genotype - 1.0)
    steps = jnp.dot(anchor_matrix(), (signs * sign).astype(BF16), preferred_element_type=F32)
    from_s, to_t = steps[:64], steps[64:]
    u = jnp.exp(STEP * from_s)
    v = jnp.exp(STEP * to_t)
    full = jnp.log(dot_nt(u, jnp.concatenate([v, v], axis=0), HIGHEST))
    left, right = from_s[16:17], to_t[47:48]
    middle = left + right
    top = jnp.max(middle, axis=1, keepdims=True)
    begin = jnp.exp(STEP * (from_s[:16] - left + (middle - top)))
    end = jnp.exp(STEP * (to_t[48:] - right))
    blank = jnp.zeros((48, width), F32)
    corner = jnp.log(dot_nt(begin, jnp.concatenate([blank, end, blank, end], axis=0), HIGHEST))
    corner = corner + STEP * top
    return pack(full, corner)


def pack(full, corner):
    lane = iota((8, 128), 1)
    sub = iota((8, 128), 0)
    col = lane % 64
    rows = [full[8 * a : 8 * a + 8] for a in range(BLOCKS)]
    for a in range(2):
        rows[a] = jnp.where(col >= 48, corner[8 * a : 8 * a + 8], rows[a])
    diagonal = rows[0]
    for a in range(1, BLOCKS):
        diagonal = jnp.where(col // 8 == a, rows[a], diagonal)
    diagonal = jnp.where(col % 8 >= sub, diagonal, 0.0)
    pairs = []
    for a in range(4):
        other = rows[7 - a] if a == 0 else pltpu.roll(rows[7 - a], 8 * a, 1)
        pairs.append(
            jnp.where(col >= 8 * (a + 1), rows[a], jnp.where(col < 8 * a, other, 0.0))
        )
    first = jnp.where(lane < 64, pairs[0], pairs[1])
    second = jnp.where(lane < 64, pairs[2], pairs[3])
    return jnp.concatenate([first, second, diagonal], axis=0)


def unpack(packed):
    first, second, diagonal = packed[0:8], packed[8:16], packed[16:24]
    pairs = [low_half(first), high_half(first), low_half(second), high_half(second)]
    rows = [None] * BLOCKS
    for a in range(4):
        rows[a] = pairs[a]
        rows[7 - a] = pairs[a] if a == 0 else pltpu.roll(pairs[a], 128 - 8 * a, 1)
    col = iota((8, 128), 1) % 64
    return [jnp.where(col // 8 == a, diagonal, rows[a]) for a in range(BLOCKS)], diagonal


def log_total(items):
    top = functools.reduce(jnp.maximum, items)
    return top + jnp.log(functools.reduce(jnp.add, [jnp.exp(x - top) for x in items]))


def row_of(columns):
    col = iota((8, 128), 1) % 64
    sub = iota((8, 128), 0)
    total = None
    for a, column in enumerate(columns):
        part = jnp.where(col == 8 * a + sub, column, 0.0)
        total = part if total is None else total + part
    return jnp.sum(total, axis=0, keepdims=True)


def rate_terms(rates, log_k):
    lane = iota((8, 128), 1)
    col = lane % 64
    sub = iota((8, 128), 0)
    stay = [jnp.log(1.0 - r) for r in rates]
    stay_row = row_of(stay)
    sums = None
    for a in range(BLOCKS):
        part = jnp.where(8 * a + sub <= col, stay[a], 0.0)
        sums = part if sums is None else sums + part
    reach_row = jnp.sum(sums, axis=0, keepdims=True)
    reach_col = [
        jnp.sum(jnp.where((lane < 64) & (col <= 8 * a + sub), stay_row, 0.0), axis=1, keepdims=True)
        for a in range(BLOCKS)
    ]
    jump_col = [jnp.log(r) - log_k for r in rates]
    jump_row = row_of(jump_col)
    start = jnp.full((8, 1), -log_k, F32)
    jump_col[0] = jnp.where(iota((8, 1), 0) == 0, start, jump_col[0])
    return reach_row, reach_col, jump_row, jump_col


def solve(packed, terms, log_k):
    reach_row, reach_col, jump_row, jump_col = terms
    lane = iota((8, 128), 1)
    sub = iota((8, 128), 0)
    col = lane % 64
    block = col // 8
    within = col % 8
    rows, diagonal = unpack(packed)
    paths = [
        jnp.where(col >= 8 * a + sub, rows[a] + (reach_row - reach_col[a]), NEG)
        for a in range(BLOCKS)
    ]
    reach_diag = jnp.broadcast_to(reach_col[0], (8, 128))
    jump_diag = jnp.broadcast_to(jump_col[0], (8, 128))
    for a in range(1, BLOCKS):
        reach_diag = jnp.where(block == a, reach_col[a], reach_diag)
        jump_diag = jnp.where(block == a, jump_col[a], jump_diag)
    path_diag = diagonal + (reach_row - reach_diag)
    ahead = pltpu.roll(path_diag + jump_diag, 7, 0)
    behind = pltpu.roll(path_diag, 1, 1) + jump_row
    inner = jnp.exp(jnp.where(within > sub, jnp.where(lane < 64, ahead, behind), NEG))
    spread = jnp.concatenate(
        [jnp.where(lane % 8 == sub, inner[m : m + 1], 0.0) for m in range(8)], axis=0
    )
    same = (iota((128, 128), 0) // 8 == iota((128, 128), 1) // 8).astype(BF16)
    coarse = spread.astype(BF16)
    fine = (spread - coarse.astype(F32)).astype(BF16)
    columns = jnp.dot(coarse, same, preferred_element_type=F32)
    columns = columns + jnp.dot(fine, same, preferred_element_type=F32)
    inverse = jnp.where(within == sub, 1.0, 0.0)
    for m in range(7):
        inverse = inverse + columns[8 * m : 8 * m + 8] * inverse[m : m + 1]
    forward_inverse = jnp.where(lane < 64, inverse, 0.0)
    backward_inverse = high_half(inverse)

    offset = jnp.broadcast_to(paths[0][7:8], (8, 128))
    for a in range(1, BLOCKS):
        offset = jnp.where(sub == a, paths[a][7:8], offset)
    offset = jnp.where((within == 0) & (block > sub), offset, 0.0)
    for step in (1, 2, 4):
        offset = offset + pltpu.roll(offset, step, 1)
    factors = [jnp.exp(paths[a] - offset[a : a + 1]) for a in range(BLOCKS)]
    jumps = [jnp.broadcast_to(jnp.exp(j), (8, 128)) for j in jump_col]
    jumps_row = jnp.exp(jump_row)

    row_lane = iota((1, 128), 1)
    row_col = row_lane % 64
    zero = jnp.zeros((1, 128), F32)

    sums = []
    scales = [zero, zero]
    last = jnp.ones((1, 128), F32)
    spent = jnp.zeros((8, 128), F32)
    scale_col = jnp.zeros((8, 128), F32)

    back = zero
    back_scales = [zero, zero]
    back_scale_row = zero
    back_sums = zero
    behind_row = jnp.where(row_lane == 63, math.exp(-log_k), 0.0)

    for b in range(BLOCKS):
        entering = last * jumps[b][0:1]
        lead = entering * factors[b][0:1]
        if b:
            weight = jnp.where(sub < b, jnp.exp(offset + scale_col - scales[b]), 0.0)
            lead = lead + jnp.sum(weight * spent, axis=0, keepdims=True)
        here = jnp.sum(
            jnp.where(block == b, lead * forward_inverse, 0.0), axis=1, keepdims=True
        )
        here = jnp.broadcast_to(here, (8, 128))
        sums.append(here)
        injected = jumps[b] * jnp.where(sub == 0, last, pltpu.roll(here, 1, 0))
        if b < BLOCKS - 1:
            spent = jnp.where(
                sub == b, jnp.sum(injected * factors[b], axis=0, keepdims=True), spent
            )
            scale_col = jnp.where(sub == b, scales[b], scale_col)
            last = here[7:8] * jnp.exp(scales[b] - scales[b + 1])
            scales.append(jnp.log(here[7:8]) + scales[b])

        c = BLOCKS - 1 - b
        weight = jnp.exp(offset[c : c + 1] + back_scale_row - back_scales[b])
        weight = jnp.where((row_lane >= 8 * c + 7) & (row_lane < 64), weight * behind_row, 0.0)
        lead = jnp.sum(factors[c] * weight, axis=1, keepdims=True)
        back = jnp.sum(lead * backward_inverse, axis=0, keepdims=True)
        back_sums = jnp.where(row_col // 8 == c, jnp.log(back) + back_scales[b], back_sums)
        if c:
            fresh = pltpu.roll(back * jumps_row, 127, 1)
            inside = (row_lane >= 8 * c - 1) & (row_lane <= 8 * c + 6)
            behind_row = jnp.where(inside, fresh, behind_row)
            back_scale_row = jnp.where(inside, back_scales[b], back_scale_row)
            first = jnp.sum(
                jnp.where(row_lane == 8 * c, back, 0.0), axis=1, keepdims=True
            )
            back_scales.append(jnp.log(first) + back_scales[b])

    scale_row = zero
    for b in range(BLOCKS):
        scale_row = jnp.where(row_col // 8 == b, scales[b], scale_row)
    forward_row = jnp.log(row_of(sums)) + scale_row
    return jnp.where(row_lane < 64, forward_row, back_sums)


def by_target(first, second):
    return jnp.where(iota((8, 128), 0) < 4, first, second)


def emission_terms(geno_rows):
    g = by_target(geno_rows[0], geno_rows[1])
    base = jnp.where(g == 2.0, 1.0, jnp.where(g == 1.0, DOWN, UP))
    slope = jnp.where(g == 2.0, 0.0, jnp.where(g == 1.0, UP - DOWN, DOWN - UP))
    return base, slope


def state_terms(solved, rate_row, k):
    lane = iota((8, 128), 1)
    logs = by_target(solved[0], solved[1])
    before = jnp.where(lane == 0, 0.0, pltpu.roll(logs, 1, 1))
    after = jnp.where(lane == 127, 0.0, pltpu.roll(logs, 127, 1))
    over_forward = jnp.exp(before - logs)
    over_backward = pltpu.roll(jnp.exp(after - logs), 64, 1)
    keep = 1.0 - rate_row
    jump = rate_row * (1.0 / k)
    return (
        keep * over_forward,
        jump * over_forward,
        keep * over_backward,
        jnp.broadcast_to(jump, (8, 128)),
    )


def dosage_of(total):
    lane = iota((8, 128), 1)
    sub = iota((8, 128), 0)
    picked = jnp.where((lane // 4) % 2 == sub, total, 0.0)
    src = iota((128, 128), 0)
    dst = iota((128, 128), 1)
    upper = ((src // 8 == dst) & (src < 64)).astype(F32)
    lower = (src // 8 == dst + 8).astype(F32)
    numerator = jnp.dot(picked, upper, precision=HIGHEST, preferred_element_type=F32)
    denominator = jnp.dot(picked, lower, precision=HIGHEST, preferred_element_type=F32)
    return numerator[0:2, 0:8] / denominator[0:2, 0:8]


def kernel(
    n_y, n_z, k,
    panel_ref, rate_ref, geno_ref,
    dosage_ref, like_ref,
    panel_all, meta_all, tiles, emis, fwd, bwd,
    log_send, log_group, log_mid, log_y, log_last, log_z,
    solve_send, solve_recv, sum_send, sum_group, sum_mid, sum_batch,
    own_sem, tile_sem,
    panel_s, panel_r, meta_s, meta_r, group_s, group_r, y_s, y_r, z_s, z_r,
    core_s, core_r, group2_s, group2_r, batch_s, batch_r,
):
    n_group = BLOCKS
    group = lax.axis_index("group")
    batch = lax.axis_index("batch")
    core = group % 2
    y = batch % n_y
    z = batch // n_y
    width = panel_all.shape[2]
    log_k = math.log(k)

    def in_group(d):
        return (group + d) % n_group

    def group_peer(d):
        return (in_group(d), batch)

    def y_peer(d):
        return (group, z * n_y + (y + d) % n_y)

    def z_peer(d):
        return (group, ((z + d) % n_z) * n_y + y)

    def far_first(n):
        return sorted(range(1, n), key=lambda d: -min(d, n - d))

    barrier = pltpu.get_barrier_semaphore()
    peers = [group_peer(d) for d in far_first(n_group)]
    peers += [z_peer(d) for d in far_first(n_z)]
    peers += [y_peer(d) for d in far_first(n_y)]
    for peer in peers:
        pl.semaphore_signal(barrier, inc=1, device_id=peer, device_id_type=MESH)
    own_panel = pltpu.make_async_copy(
        panel_ref.at[:, pl.ds(pl.multiple_of(group * width, width), width)],
        panel_all.at[group],
        own_sem,
    )
    own_panel.start()
    meta_all[group] = meta_tile(rate_ref[...], geno_ref[...])
    pl.semaphore_wait(barrier, len(peers))

    def remote(src, dst, send, recv, peer):
        return pltpu.make_async_remote_copy(
            src_ref=src, dst_ref=dst, send_sem=send, recv_sem=recv,
            device_id=peer, device_id_type=MESH,
        )

    copies = []
    for d in far_first(n_group):
        start = pl.multiple_of(in_group(d) * width, width)
        copies.append(
            remote(
                panel_ref.at[:, pl.ds(start, width)], panel_all.at[group],
                panel_s.at[d - 1], panel_r.at[d - 1], group_peer(d),
            )
        )
        copies.append(
            remote(
                meta_all.at[group], meta_all.at[group],
                meta_s.at[d - 1], meta_r.at[d - 1], group_peer(d),
            )
        )
    for copy in copies:
        copy.start()
    own_panel.wait()
    for copy in copies:
        copy.wait()

    relayout = []
    for c in range(4):
        for h in range(2):
            copy = pltpu.make_async_copy(
                panel_all.at[:, :, pl.ds(128 * c, 128)],
                tiles.at[:, :, 4 * h + c],
                tile_sem.at[4 * h + c],
            )
            copy.start()
            relayout.append(copy)

    meta = meta_all[...].reshape(MARKERS, 128)
    signs = 2.0 * panel_all[...].reshape(MARKERS, width).astype(F32) - 1.0
    for h in range(2):
        log_send[h] = couplings(signs, meta[:, 1 + h : 2 + h])

    def start_all(n, order, src, slots, send, recv, peer):
        out = [
            remote(src(d), slots.at[d - 1], send.at[d - 1], recv.at[d - 1], peer(d)) for d in order
        ]
        for copy in out:
            copy.start()
        return out

    def finish(copies):
        for copy in copies:
            copy.wait()

    flying = start_all(
        n_group, far_first(n_group), lambda d: log_send.at[in_group(d) % 2],
        log_group, group_s, group_r, group_peer,
    )
    rates = [meta[8 * a : 8 * a + 8, 0:1] for a in range(BLOCKS)]
    terms = rate_terms(rates, log_k)
    rate_row = row_of(rates)
    geno_rows = [
        row_of([meta[8 * a : 8 * a + 8, 1 + h : 2 + h] for a in range(BLOCKS)]) for h in range(2)
    ]
    finish(flying)
    total = log_total([log_send[core]] + [log_group[d] for d in range(n_group - 1)])
    if n_y > 1:
        log_mid[...] = total
        flying = start_all(
            n_y, far_first(n_y), lambda d: log_mid, log_y, y_s, y_r, y_peer
        )
        finish(flying)
        total = log_total([total] + [log_y[d] for d in range(n_y - 1)])
    base, slope = emission_terms(geno_rows)

    def emissions():
        finish(relayout)
        for t in range(MARKERS):
            allele = tiles[t // 8, t % 8].astype(F32)
            emis[t] = base[:, t : t + 1] + slope[:, t : t + 1] * allele

    if n_z > 1:
        log_last[...] = total
        flying = start_all(
            n_z, far_first(n_z), lambda d: log_last, log_z, z_s, z_r, z_peer
        )
        emissions()
        finish(flying)
        total = log_total([total] + [log_z[d] for d in range(n_z - 1)])
    else:
        emissions()

    mine = solve(total, terms, log_k)
    solve_send[...] = mine
    partner = (group + 1 - 2 * core, batch)
    swap = remote(solve_send, solve_recv, core_s, core_r, partner)
    swap.start()
    swap.wait()
    theirs = solve_recv[...]
    solved = [jnp.where(core == 0, mine, theirs), jnp.where(core == 0, theirs, mine)]

    lane_row = iota((1, 128), 1)
    likes = []
    for h in range(2):
        seen = jnp.sum(
            jnp.where((lane_row < 64) & (geno_rows[h] != 2.0), LOG_CENTRE, 0.0),
            axis=1, keepdims=True,
        )
        likes.append((solved[h][:, 63:64] + seen) * (1.0 / MARKERS))
    like_ref[...] = jnp.where(lane_row == 0, likes[0], likes[1])[:, 0:2]

    keep_f, jump_f, keep_b, jump_b = state_terms(solved, rate_row, float(k))
    ahead = jnp.full((8, 128), 1.0 / k, F32)
    behind = jnp.full((8, 128), 1.0 / k, F32)
    for i in range(MARKERS):
        ahead = emis[i] * (keep_f[:, i : i + 1] * ahead + jump_f[:, i : i + 1])
        fwd[i] = ahead
        t = MARKERS - 1 - i
        bwd[t] = behind
        behind = keep_b[:, t : t + 1] * (emis[t] * behind) + jump_b[:, t : t + 1]

    ones = jnp.ones((8, 128), BF16)
    for a in range(BLOCKS):
        both = fwd[8 * a : 8 * a + 8] * bwd[8 * a : 8 * a + 8]
        carrying = both * tiles[a].astype(F32)
        stacked = jnp.concatenate([carrying.reshape(64, 128), both.reshape(64, 128)], axis=0)
        coarse = stacked.astype(BF16)
        fine = (stacked - coarse.astype(F32)).astype(BF16)
        sums = dot_nt(ones, coarse) + dot_nt(ones, fine)
        sum_send[a] = sums[0:1]

    flying = start_all(
        n_group, far_first(n_group), lambda d: sum_send.at[in_group(d)],
        sum_group, group2_s, group2_r, group_peer,
    )
    finish(flying)
    total = functools.reduce(
        jnp.add, [sum_send[group]] + [sum_group[d] for d in range(n_group - 1)]
    )
    n_batch = n_y * n_z
    sum_mid[...] = total
    flying = [
        remote(
            sum_mid, sum_batch.at[pl.ds(d - 1, 1)], batch_s.at[d - 1], batch_r.at[d - 1],
            (group, (batch + d) % n_batch),
        )
        for d in range(1, n_batch)
    ]
    for copy in flying:
        copy.start()
    sum_batch[n_batch - 1 : n_batch] = total
    finish(flying)
    total = jnp.sum(sum_batch[...], axis=0, keepdims=True)
    dosage_ref[...] = dosage_of(total)


def on_device(n_y, panel, rates, genotypes):
    n_batch = lax.axis_size("batch")
    n_group = lax.axis_size("group")
    n_z = n_batch // n_y
    width = panel.shape[1] // n_group
    k = panel.shape[1] * n_batch
    dma = pltpu.SemaphoreType.DMA
    vmem = pltpu.VMEM
    g1, y1, z1 = n_group - 1, max(n_y - 1, 1), max(n_z - 1, 1)
    scratch = [
        vmem((BLOCKS, BLOCK, width), jnp.int32),
        vmem((BLOCKS, BLOCK, 128), F32),
        vmem((BLOCKS, BLOCK, 8, 128), jnp.int32),
        vmem((MARKERS, 8, 128), F32),
        vmem((MARKERS, 8, 128), F32),
        vmem((MARKERS, 8, 128), F32),
        vmem((2, 24, 128), F32),
        vmem((g1, 24, 128), F32),
        vmem((24, 128), F32),
        vmem((y1, 24, 128), F32),
        vmem((24, 128), F32),
        vmem((z1, 24, 128), F32),
        vmem((1, 128), F32),
        vmem((1, 128), F32),
        vmem((BLOCKS, 1, 128), F32),
        vmem((g1, 1, 128), F32),
        vmem((1, 128), F32),
        vmem((n_batch, 128), F32),
        dma,
        dma((8,)),
        dma((g1,)), dma((g1,)), dma((g1,)), dma((g1,)), dma((g1,)), dma((g1,)),
        dma((y1,)), dma((y1,)), dma((z1,)), dma((z1,)),
        dma, dma,
        dma((g1,)), dma((g1,)), dma((n_batch - 1,)), dma((n_batch - 1,)),
    ]
    dosage, like = pl.pallas_call(
        functools.partial(kernel, n_y, n_z, k),
        out_shape=(
            pltpu.VMEM((2, BLOCK), F32),
            pltpu.VMEM((1, 2), F32),
        ),
        in_specs=[
            pl.BlockSpec(memory_space=pl.ANY),
            pl.BlockSpec(memory_space=pltpu.VMEM),
            pl.BlockSpec(memory_space=pltpu.VMEM),
        ],
        out_specs=(
            pl.BlockSpec(memory_space=pltpu.VMEM),
            pl.BlockSpec(memory_space=pltpu.VMEM),
        ),
        scratch_shapes=scratch,
        compiler_params=pltpu.CompilerParams(collective_id=0, has_side_effects=True),
    )(panel, rates.reshape(1, BLOCK), genotypes)
    return dosage, like.reshape(2)


def solution(mesh, n_y=4):
    placed = (P("group", "batch"), P("group"), P(None, "group"))
    return jax.shard_map(
        functools.partial(on_device, n_y),
        mesh=mesh,
        in_specs=placed,
        out_specs=(P(None, "group"), P()),
        check_vma=False,
    )
```

```python
import functools
import math

import jax
import jax.numpy as jnp
from jax import lax
from jax.experimental import pallas as pl
from jax.experimental.pallas import tpu as pltpu
from jax.sharding import PartitionSpec as P

HIGHEST = lax.Precision.HIGHEST
MESH = pl.DeviceIdType.MESH

MISMATCH = 0.05
STEP = 0.5 * math.log((1.0 - MISMATCH) / MISMATCH)
LOG_CENTRE = 0.5 * math.log((1.0 - MISMATCH) * MISMATCH)
UP = math.exp(STEP)
DOWN = math.exp(-STEP)
NEG = -1e30
F32 = jnp.float32
BF16 = jnp.bfloat16

MARKERS = 64
BLOCK = 8
BLOCKS = 8


def iota(shape, axis):
    return lax.broadcasted_iota(jnp.int32, shape, axis)


def dot_nt(a, b, precision=None):
    return lax.dot_general(
        a, b, (((1,), (1,)), ((), ())), precision=precision, preferred_element_type=F32
    )


def low_half(x):
    return jnp.where(iota(x.shape, 1) < 64, x, pltpu.roll(x, 64, 1))


def high_half(x):
    return jnp.where(iota(x.shape, 1) < 64, pltpu.roll(x, 64, 1), x)


def meta_tile(rate_row, geno_rows):
    eye = iota((8, 8), 0) == iota((8, 8), 1)
    lane = iota((8, 128), 1)

    def column(row):
        return jnp.sum(jnp.where(eye, jnp.broadcast_to(row, (8, 8)), 0.0), axis=1, keepdims=True)

    rate = column(rate_row)
    first = column(geno_rows[0:1].astype(F32))
    second = column(geno_rows[1:2].astype(F32))
    return jnp.where(lane == 0, rate, jnp.where(lane == 1, first, second))


def anchor_matrix():
    row = iota((128, 64), 0)
    col = iota((128, 64), 1)
    s = row
    t = row - 64
    upper = jnp.where((col >= s) & (col <= 31), 1.0, jnp.where((col >= 32) & (col < s), -1.0, 0.0))
    lower = jnp.where((col >= 32) & (col <= t), 1.0, jnp.where((col > t) & (col <= 31), -1.0, 0.0))
    return jnp.where(row < 64, upper, lower).astype(BF16)


def product(a, b):
    a_top, b_top = a.astype(BF16), b.astype(BF16)
    a_rest = (a - a_top.astype(F32)).astype(BF16)
    b_rest = (b - b_top.astype(F32)).astype(BF16)
    return dot_nt(a_top, b_top) + (dot_nt(a_rest, b_top) + dot_nt(a_top, b_rest))


def couplings(signs, genotype):
    width = signs.shape[1]
    sign = jnp.where(genotype == 2.0, 0.0, 2.0 * genotype - 1.0)
    steps = jnp.dot(anchor_matrix(), (signs * sign).astype(BF16), preferred_element_type=F32)
    from_s, to_t = steps[:64], steps[64:]
    u = jnp.exp(STEP * from_s)
    v = jnp.exp(STEP * to_t)
    full = jnp.log(product(u, jnp.concatenate([v, v], axis=0)))
    left, right = from_s[16:17], to_t[47:48]
    middle = left + right
    top = jnp.max(middle, axis=1, keepdims=True)
    begin = jnp.exp(STEP * (from_s[:16] - left + (middle - top)))
    end = jnp.exp(STEP * (to_t[48:] - right))
    blank = jnp.zeros((48, width), F32)
    corner = jnp.log(product(begin, jnp.concatenate([blank, end, blank, end], axis=0)))
    corner = corner + STEP * top
    return pack(full, corner)


def pack(full, corner):
    lane = iota((8, 128), 1)
    sub = iota((8, 128), 0)
    col = lane % 64
    rows = [full[8 * a : 8 * a + 8] for a in range(BLOCKS)]
    for a in range(2):
        rows[a] = jnp.where(col >= 48, corner[8 * a : 8 * a + 8], rows[a])
    diagonal = rows[0]
    for a in range(1, BLOCKS):
        diagonal = jnp.where(col // 8 == a, rows[a], diagonal)
    diagonal = jnp.where(col % 8 >= sub, diagonal, 0.0)
    pairs = []
    for a in range(4):
        other = rows[7 - a] if a == 0 else pltpu.roll(rows[7 - a], 8 * a, 1)
        pairs.append(
            jnp.where(col >= 8 * (a + 1), rows[a], jnp.where(col < 8 * a, other, 0.0))
        )
    first = jnp.where(lane < 64, pairs[0], pairs[1])
    second = jnp.where(lane < 64, pairs[2], pairs[3])
    halves = jnp.where(lane < 64, diagonal, pltpu.roll(diagonal, 4, 0))
    return jnp.concatenate([first, second, halves], axis=0)


def unpack(packed):
    first, second, halves = packed[0:8], packed[8:16], packed[16:24]
    diagonal = jnp.where(
        iota((8, 128), 0) < 4, low_half(halves), pltpu.roll(high_half(halves), 4, 0)
    )
    pairs = [low_half(first), high_half(first), low_half(second), high_half(second)]
    rows = [None] * BLOCKS
    for a in range(4):
        rows[a] = pairs[a]
        rows[7 - a] = pairs[a] if a == 0 else pltpu.roll(pairs[a], 128 - 8 * a, 1)
    col = iota((8, 128), 1) % 64
    return [jnp.where(col // 8 == a, diagonal, rows[a]) for a in range(BLOCKS)], diagonal


def log_total(items):
    top = functools.reduce(jnp.maximum, items)
    return top + jnp.log(functools.reduce(jnp.add, [jnp.exp(x - top) for x in items]))


def row_of(columns):
    col = iota((8, 128), 1) % 64
    sub = iota((8, 128), 0)
    total = None
    for a, column in enumerate(columns):
        part = jnp.where(col == 8 * a + sub, column, 0.0)
        total = part if total is None else total + part
    return jnp.sum(total, axis=0, keepdims=True)


def rate_terms(rates, log_k):
    lane = iota((8, 128), 1)
    col = lane % 64
    sub = iota((8, 128), 0)
    stay = [jnp.log(1.0 - r) for r in rates]
    stay_row = row_of(stay)
    sums = None
    for a in range(BLOCKS):
        part = jnp.where(8 * a + sub <= col, stay[a], 0.0)
        sums = part if sums is None else sums + part
    reach_row = jnp.sum(sums, axis=0, keepdims=True)
    reach_col = [
        jnp.sum(jnp.where((lane < 64) & (col <= 8 * a + sub), stay_row, 0.0), axis=1, keepdims=True)
        for a in range(BLOCKS)
    ]
    jump_col = [jnp.log(r) - log_k for r in rates]
    jump_row = row_of(jump_col)
    start = jnp.full((8, 1), -log_k, F32)
    jump_col[0] = jnp.where(iota((8, 1), 0) == 0, start, jump_col[0])
    return reach_row, reach_col, jump_row, jump_col


def solve(packed, terms, log_k):
    reach_row, reach_col, jump_row, jump_col = terms
    lane = iota((8, 128), 1)
    sub = iota((8, 128), 0)
    col = lane % 64
    block = col // 8
    within = col % 8
    rows, diagonal = unpack(packed)
    paths = [
        jnp.where(col >= 8 * a + sub, rows[a] + (reach_row - reach_col[a]), NEG)
        for a in range(BLOCKS)
    ]
    reach_diag = jnp.broadcast_to(reach_col[0], (8, 128))
    jump_diag = jnp.broadcast_to(jump_col[0], (8, 128))
    for a in range(1, BLOCKS):
        reach_diag = jnp.where(block == a, reach_col[a], reach_diag)
        jump_diag = jnp.where(block == a, jump_col[a], jump_diag)
    path_diag = diagonal + (reach_row - reach_diag)
    ahead = pltpu.roll(path_diag + jump_diag, 7, 0)
    behind = pltpu.roll(path_diag, 1, 1) + jump_row
    inner = jnp.exp(jnp.where(within > sub, jnp.where(lane < 64, ahead, behind), NEG))
    spread = jnp.concatenate(
        [jnp.where(lane % 8 == sub, inner[m : m + 1], 0.0) for m in range(8)], axis=0
    )
    same = (iota((128, 128), 0) // 8 == iota((128, 128), 1) // 8).astype(BF16)
    coarse = spread.astype(BF16)
    fine = (spread - coarse.astype(F32)).astype(BF16)
    columns = jnp.dot(coarse, same, preferred_element_type=F32)
    columns = columns + jnp.dot(fine, same, preferred_element_type=F32)
    inverse = jnp.where(within == sub, 1.0, 0.0)
    for m in range(7):
        inverse = inverse + columns[8 * m : 8 * m + 8] * inverse[m : m + 1]
    forward_inverse = jnp.where(lane < 64, inverse, 0.0)
    backward_inverse = high_half(inverse)

    offset = jnp.broadcast_to(paths[0][7:8], (8, 128))
    for a in range(1, BLOCKS):
        offset = jnp.where(sub == a, paths[a][7:8], offset)
    offset = jnp.where((within == 0) & (block > sub), offset, 0.0)
    for step in (1, 2, 4):
        offset = offset + pltpu.roll(offset, step, 1)
    factors = [jnp.exp(paths[a] - offset[a : a + 1]) for a in range(BLOCKS)]
    jumps = [jnp.broadcast_to(jnp.exp(j), (8, 128)) for j in jump_col]
    jumps_row = jnp.exp(jump_row)

    row_lane = iota((1, 128), 1)
    row_col = row_lane % 64
    zero = jnp.zeros((1, 128), F32)

    sums = []
    scales = [zero, zero]
    last = jnp.ones((1, 128), F32)
    spent = jnp.zeros((8, 128), F32)
    scale_col = jnp.zeros((8, 128), F32)

    back = zero
    back_scales = [zero, zero]
    back_scale_row = zero
    back_sums = zero
    behind_row = jnp.where(row_lane == 63, math.exp(-log_k), 0.0)

    for b in range(BLOCKS):
        entering = last * jumps[b][0:1]
        lead = entering * factors[b][0:1]
        if b:
            weight = jnp.where(sub < b, jnp.exp(offset + scale_col - scales[b]), 0.0)
            lead = lead + jnp.sum(weight * spent, axis=0, keepdims=True)
        here = jnp.sum(
            jnp.where(block == b, lead * forward_inverse, 0.0), axis=1, keepdims=True
        )
        here = jnp.broadcast_to(here, (8, 128))
        sums.append(here)
        injected = jumps[b] * jnp.where(sub == 0, last, pltpu.roll(here, 1, 0))
        if b < BLOCKS - 1:
            spent = jnp.where(
                sub == b, jnp.sum(injected * factors[b], axis=0, keepdims=True), spent
            )
            scale_col = jnp.where(sub == b, scales[b], scale_col)
            last = here[7:8] * jnp.exp(scales[b] - scales[b + 1])
            scales.append(jnp.log(here[7:8]) + scales[b])

        c = BLOCKS - 1 - b
        weight = jnp.exp(offset[c : c + 1] + back_scale_row - back_scales[b])
        weight = jnp.where((row_lane >= 8 * c + 7) & (row_lane < 64), weight * behind_row, 0.0)
        lead = jnp.sum(factors[c] * weight, axis=1, keepdims=True)
        back = jnp.sum(lead * backward_inverse, axis=0, keepdims=True)
        back_sums = jnp.where(row_col // 8 == c, jnp.log(back) + back_scales[b], back_sums)
        if c:
            fresh = pltpu.roll(back * jumps_row, 127, 1)
            inside = (row_lane >= 8 * c - 1) & (row_lane <= 8 * c + 6)
            behind_row = jnp.where(inside, fresh, behind_row)
            back_scale_row = jnp.where(inside, back_scales[b], back_scale_row)
            first = jnp.sum(
                jnp.where(row_lane == 8 * c, back, 0.0), axis=1, keepdims=True
            )
            back_scales.append(jnp.log(first) + back_scales[b])

    scale_row = zero
    for b in range(BLOCKS):
        scale_row = jnp.where(row_col // 8 == b, scales[b], scale_row)
    forward_row = jnp.log(row_of(sums)) + scale_row
    return jnp.where(row_lane < 64, forward_row, back_sums)


def emission_terms(geno_row):
    g = geno_row
    base = jnp.where(g == 2.0, 1.0, jnp.where(g == 1.0, DOWN, UP))
    slope = jnp.where(g == 2.0, 0.0, jnp.where(g == 1.0, UP - DOWN, DOWN - UP))
    return base, slope


def state_terms(logs, rate_row, k):
    lane = iota((1, 128), 1)
    before = jnp.where(lane == 0, 0.0, pltpu.roll(logs, 1, 1))
    after = jnp.where(lane == 127, 0.0, pltpu.roll(logs, 127, 1))
    over_forward = jnp.exp(before - logs)
    over_backward = pltpu.roll(jnp.exp(after - logs), 64, 1)
    keep = 1.0 - rate_row
    jump = rate_row * (1.0 / k)
    rows = (keep * over_forward, jump * over_forward, keep * over_backward, jump)
    return [jnp.broadcast_to(row, (8, 128)) for row in rows]


def interleave(first, second):
    lane = iota((1, 128), 1)
    first = first + pltpu.roll(first, 127, 1)
    second = second + pltpu.roll(second, 127, 1)
    return jnp.where(lane % 2 == 0, first, pltpu.roll(second, 1, 1))


def dosage_of(total):
    lane = iota((8, 128), 1)
    sub = iota((8, 128), 0)
    picked = jnp.where(lane % 2 == sub, total, 0.0)
    src = iota((128, 128), 0)
    dst = iota((128, 128), 1)
    upper = ((src // 8 == dst) & (src < 64)).astype(F32)
    lower = (src // 8 == dst + 8).astype(F32)
    numerator = jnp.dot(picked, upper, precision=HIGHEST, preferred_element_type=F32)
    denominator = jnp.dot(picked, lower, precision=HIGHEST, preferred_element_type=F32)
    return numerator[0:2, 0:8] / denominator[0:2, 0:8]


def far_first(n):
    return sorted(range(1, n), key=lambda d: -min(d, n - d))


def kernel(
    n_y, n_z, k,
    panel_ref, rate_ref, geno_ref,
    dosage_ref, like_ref,
    panel_own, panel_all, meta_all, tiles, emis, fwd, bwd,
    log_send, log_plane, log_mid, log_z, log_last,
    solve_send, solve_recv, sum_send, sum_group, sum_mid, sum_batch,
    load_sem, own_sem, tile_sem, known,
    panel_s, panel_r, meta_s, meta_r, plane_s, plane_r, z_s, z_r,
    core_s, core_r, group_s, group_r, batch_s, batch_r,
):
    n_group = BLOCKS
    n_x = n_group // 2
    group = lax.axis_index("group")
    batch = lax.axis_index("batch")
    core = group % 2
    x = group // 2
    y = batch % n_y
    z = batch // n_y
    width = panel_all.shape[2]
    log_k = math.log(k)

    def in_group(d):
        return (group + d) % n_group

    def group_peer(d):
        return (in_group(d), batch)

    def y_peer(d):
        return (group, z * n_y + (y + d) % n_y)

    def z_peer(d):
        return (group, ((z + d) % n_z) * n_y + y)

    def plane_peer(dx, dy):
        return (((x + dx) % n_x) * 2 + core, z * n_y + (y + dy) % n_y)

    def remote(src, dst, send, recv, peer):
        return pltpu.make_async_remote_copy(
            src_ref=src, dst_ref=dst, send_sem=send, recv_sem=recv,
            device_id=peer, device_id_type=MESH,
        )

    def finish(copies):
        for copy in copies:
            copy.wait()

    load = pltpu.make_async_copy(panel_ref, panel_own, load_sem)
    load.start()
    own = pltpu.make_async_copy(
        panel_ref.at[:, pl.ds(pl.multiple_of(x * width, width), width)],
        panel_all.at[group],
        own_sem,
    )
    own.start()
    barrier = pltpu.get_barrier_semaphore()
    near_y = [y_peer(d) for d in sorted({1, n_y - 1}) if 0 < d < n_y]
    near_z = [z_peer(d) for d in sorted({1, n_z - 1}) if 0 < d < n_z]
    peers = [group_peer(d) for d in far_first(n_group)] + near_y + near_z
    for peer in peers:
        pl.semaphore_signal(barrier, inc=1, device_id=peer, device_id_type=MESH)
    meta_all[group] = meta_tile(rate_ref[...], geno_ref[...])
    load.wait()
    pl.semaphore_wait(barrier, len(peers))

    copies = []
    for d in far_first(n_group):
        start = pl.multiple_of(in_group(d) // 2 * width, width)
        copies.append(
            remote(
                panel_own.at[:, pl.ds(start, width)], panel_all.at[group],
                panel_s.at[d - 1], panel_r.at[d - 1], group_peer(d),
            )
        )
    for d in far_first(n_group):
        copies.append(
            remote(
                meta_all.at[group], meta_all.at[group],
                meta_s.at[d - 1], meta_r.at[d - 1], group_peer(d),
            )
        )
    for copy in copies:
        copy.start()
    for turn, near in enumerate([near_y + near_z, near_y + near_z, near_z]):
        for peer in near:
            pl.semaphore_signal(known.at[turn], inc=1, device_id=peer, device_id_type=MESH)
        if near:
            pl.semaphore_wait(known.at[turn], len(near))
    own.wait()
    finish(copies)

    relayout = []
    for c in range(8):
        copy = pltpu.make_async_copy(
            panel_all.at[:, :, pl.ds(128 * c, 128)], tiles.at[:, :, c], tile_sem.at[c]
        )
        copy.start()
        relayout.append(copy)

    meta = meta_all[...].reshape(MARKERS, 128)
    signs = 2.0 * panel_all[...].reshape(MARKERS, width).astype(F32) - 1.0
    genotype = jnp.where(core == 0, meta[:, 1:2], meta[:, 2:3])
    log_send[...] = couplings(signs, genotype)
    sent = pl.ds(0, 20)

    plane = [(dx, dy) for dx in range(n_x) for dy in range(n_y) if dx or dy]
    plane.sort(key=lambda p: -(min(p[0], n_x - p[0]) + min(p[1], n_y - p[1])))
    flying = [
        remote(
            log_send.at[sent], log_plane.at[i], plane_s.at[i], plane_r.at[i], plane_peer(dx, dy)
        )
        for i, (dx, dy) in enumerate(plane)
    ]
    for copy in flying:
        copy.start()
    rates = [meta[8 * a : 8 * a + 8, 0:1] for a in range(BLOCKS)]
    terms = rate_terms(rates, log_k)
    rate_row = row_of(rates)
    geno_row = row_of([genotype[8 * a : 8 * a + 8] for a in range(BLOCKS)])
    base, slope = emission_terms(geno_row)
    log_mid[...] = jnp.zeros((24, 128), F32)
    log_last[...] = jnp.zeros((24, 128), F32)
    finish(flying)
    total = log_total([log_send[0:20]] + [log_plane[i] for i in range(len(plane))])
    log_mid[0:20] = total

    flying = [
        remote(log_mid.at[sent], log_z.at[d - 1], z_s.at[d - 1], z_r.at[d - 1], z_peer(d))
        for d in far_first(n_z)
    ]
    for copy in flying:
        copy.start()
    finish(relayout)
    for t in range(MARKERS):
        allele = tiles[t // 8, t % 8].astype(F32)
        emis[t] = base[:, t : t + 1] + slope[:, t : t + 1] * allele
    finish(flying)
    log_last[0:20] = log_total([total] + [log_z[d] for d in range(n_z - 1)])

    solved = solve(log_last[...], terms, log_k)

    lane_row = iota((1, 128), 1)
    seen = jnp.sum(
        jnp.where((lane_row < 64) & (geno_row != 2.0), LOG_CENTRE, 0.0), axis=1, keepdims=True
    )
    like = jnp.broadcast_to((solved[:, 63:64] + seen) * (1.0 / MARKERS), (1, 128))
    solve_send[...] = like
    partner = (group + 1 - 2 * core, batch)
    swap = remote(solve_send, solve_recv, core_s, core_r, partner)
    swap.start()

    keep_f, jump_f, keep_b, jump_b = state_terms(solved, rate_row, float(k))
    ahead = jnp.full((8, 128), 1.0 / k, F32)
    behind = jnp.full((8, 128), 1.0 / k, F32)
    for i in range(MARKERS):
        ahead = emis[i] * (keep_f[:, i : i + 1] * ahead + jump_f[:, i : i + 1])
        fwd[i] = ahead
        t = MARKERS - 1 - i
        bwd[t] = behind
        behind = keep_b[:, t : t + 1] * (emis[t] * behind) + jump_b[:, t : t + 1]

    ones = jnp.ones((8, 128), BF16)
    for a in range(BLOCKS):
        both = fwd[8 * a : 8 * a + 8] * bwd[8 * a : 8 * a + 8]
        carrying = both * tiles[a].astype(F32)
        stacked = jnp.concatenate([carrying.reshape(64, 128), both.reshape(64, 128)], axis=0)
        coarse = stacked.astype(BF16)
        fine = (stacked - coarse.astype(F32)).astype(BF16)
        sums = dot_nt(ones, coarse) + dot_nt(ones, fine)
        sum_send[a] = sums[0:1]

    flying = [
        remote(
            sum_send.at[in_group(d)], sum_group.at[d - 1],
            group_s.at[d - 1], group_r.at[d - 1], group_peer(d),
        )
        for d in far_first(n_group)
    ]
    for copy in flying:
        copy.start()
    finish(flying)
    mine = functools.reduce(jnp.add, [sum_send[group]] + [sum_group[d - 1] for d in (2, 4, 6)])
    theirs = functools.reduce(jnp.add, [sum_group[d - 1] for d in (1, 3, 5, 7)])
    total = interleave(
        jnp.where(core == 0, mine, theirs), jnp.where(core == 0, theirs, mine)
    )

    n_batch = n_y * n_z
    sum_mid[...] = total
    flying = [
        remote(
            sum_mid, sum_batch.at[pl.ds(d - 1, 1)], batch_s.at[d - 1], batch_r.at[d - 1],
            (group, (batch + d) % n_batch),
        )
        for d in range(1, n_batch)
    ]
    for copy in flying:
        copy.start()
    sum_batch[n_batch - 1 : n_batch] = total
    swap.wait()
    other = solve_recv[...]
    like_ref[...] = jnp.where(
        lane_row == 0, jnp.where(core == 0, like, other), jnp.where(core == 0, other, like)
    )[:, 0:2]
    finish(flying)
    total = jnp.sum(sum_batch[...], axis=0, keepdims=True)
    dosage_ref[...] = dosage_of(total)


def on_device(n_y, panel, rates, genotypes):
    n_batch = lax.axis_size("batch")
    n_group = lax.axis_size("group")
    n_z = n_batch // n_y
    held = panel.shape[1]
    width = held // (n_group // 2)
    k = held * n_batch
    dma = pltpu.SemaphoreType.DMA
    vmem = pltpu.VMEM
    g1, z1, p1 = n_group - 1, max(n_z - 1, 1), n_group // 2 * n_y - 1
    scratch = [
        vmem((BLOCK, held), jnp.int32),
        vmem((BLOCKS, BLOCK, width), jnp.int32),
        vmem((BLOCKS, BLOCK, 128), F32),
        vmem((BLOCKS, BLOCK, 8, 128), jnp.int32),
        vmem((MARKERS, 8, 128), F32),
        vmem((MARKERS, 8, 128), F32),
        vmem((MARKERS, 8, 128), F32),
        vmem((24, 128), F32),
        vmem((p1, 20, 128), F32),
        vmem((24, 128), F32),
        vmem((z1, 20, 128), F32),
        vmem((24, 128), F32),
        vmem((1, 128), F32),
        vmem((1, 128), F32),
        vmem((BLOCKS, 1, 128), F32),
        vmem((g1, 1, 128), F32),
        vmem((1, 128), F32),
        vmem((n_batch, 128), F32),
        dma,
        dma,
        dma((8,)),
        pltpu.SemaphoreType.REGULAR((3,)),
        dma((g1,)), dma((g1,)), dma((g1,)), dma((g1,)), dma((p1,)), dma((p1,)),
        dma((z1,)), dma((z1,)),
        dma, dma,
        dma((g1,)), dma((g1,)), dma((n_batch - 1,)), dma((n_batch - 1,)),
    ]
    dosage, like = pl.pallas_call(
        functools.partial(kernel, n_y, n_z, k),
        out_shape=(
            pltpu.VMEM((2, BLOCK), F32),
            pltpu.VMEM((1, 2), F32),
        ),
        in_specs=[
            pl.BlockSpec(memory_space=pl.ANY),
            pl.BlockSpec(memory_space=pltpu.VMEM),
            pl.BlockSpec(memory_space=pltpu.VMEM),
        ],
        out_specs=(
            pl.BlockSpec(memory_space=pltpu.VMEM),
            pl.BlockSpec(memory_space=pltpu.VMEM),
        ),
        scratch_shapes=scratch,
        compiler_params=pltpu.CompilerParams(collective_id=0, has_side_effects=True),
    )(panel, rates.reshape(1, BLOCK), genotypes)
    return dosage, like.reshape(2)


def solution(mesh, n_y=4):
    placed = (P("group", "batch"), P("group"), P(None, "group"))
    return jax.shard_map(
        functools.partial(on_device, n_y),
        mesh=mesh,
        in_specs=placed,
        out_specs=(P(None, "group"), P()),
        check_vma=False,
    )
```

```python
import functools
import math

import jax
import jax.numpy as jnp
from jax import lax
from jax.experimental import pallas as pl
from jax.experimental.pallas import tpu as pltpu
from jax.sharding import PartitionSpec as P

HIGHEST = lax.Precision.HIGHEST
MESH = pl.DeviceIdType.MESH

MISMATCH = 0.05
STEP = 0.5 * math.log((1.0 - MISMATCH) / MISMATCH)
LOG_CENTRE = 0.5 * math.log((1.0 - MISMATCH) * MISMATCH)
UP = math.exp(STEP)
DOWN = math.exp(-STEP)
NEG = -1e30
F32 = jnp.float32
BF16 = jnp.bfloat16

MARKERS = 64
BLOCK = 8
BLOCKS = 8


def iota(shape, axis):
    return lax.broadcasted_iota(jnp.int32, shape, axis)


def dot_nt(a, b, precision=None):
    return lax.dot_general(
        a, b, (((1,), (1,)), ((), ())), precision=precision, preferred_element_type=F32
    )


def low_half(x):
    return jnp.where(iota(x.shape, 1) < 64, x, pltpu.roll(x, 64, 1))


def high_half(x):
    return jnp.where(iota(x.shape, 1) < 64, pltpu.roll(x, 64, 1), x)


def meta_tile(rate_row, geno_rows):
    eye = iota((8, 8), 0) == iota((8, 8), 1)
    lane = iota((8, 128), 1)

    def column(row):
        return jnp.sum(jnp.where(eye, jnp.broadcast_to(row, (8, 8)), 0.0), axis=1, keepdims=True)

    rate = column(rate_row)
    first = column(geno_rows[0:1].astype(F32))
    second = column(geno_rows[1:2].astype(F32))
    return jnp.where(lane == 0, rate, jnp.where(lane == 1, first, second))


def anchor_matrix():
    row = iota((128, 64), 0)
    col = iota((128, 64), 1)
    s = row
    t = row - 64
    upper = jnp.where((col >= s) & (col <= 31), 1.0, jnp.where((col >= 32) & (col < s), -1.0, 0.0))
    lower = jnp.where((col >= 32) & (col <= t), 1.0, jnp.where((col > t) & (col <= 31), -1.0, 0.0))
    return jnp.where(row < 64, upper, lower).astype(BF16)


def product(a, b):
    a_top, b_top = a.astype(BF16), b.astype(BF16)
    a_rest = (a - a_top.astype(F32)).astype(BF16)
    b_rest = (b - b_top.astype(F32)).astype(BF16)
    return dot_nt(a_top, b_top) + (dot_nt(a_rest, b_top) + dot_nt(a_top, b_rest))


def couplings(signs, genotype):
    width = signs.shape[1]
    sign = jnp.where(genotype == 2.0, 0.0, 2.0 * genotype - 1.0)
    steps = jnp.dot(anchor_matrix(), (signs * sign).astype(BF16), preferred_element_type=F32)
    from_s, to_t = steps[:64], steps[64:]
    u = jnp.exp(STEP * from_s)
    v = jnp.exp(STEP * to_t)
    full = jnp.log(product(u, jnp.concatenate([v, v], axis=0)))
    left, right = from_s[16:17], to_t[47:48]
    middle = left + right
    top = jnp.max(middle, axis=1, keepdims=True)
    begin = jnp.exp(STEP * (from_s[:16] - left + (middle - top)))
    end = jnp.exp(STEP * (to_t[48:] - right))
    blank = jnp.zeros((48, width), F32)
    corner = jnp.log(product(begin, jnp.concatenate([blank, end, blank, end], axis=0)))
    corner = corner + STEP * top
    return pack(full, corner)


def pack(full, corner):
    lane = iota((8, 128), 1)
    sub = iota((8, 128), 0)
    col = lane % 64
    rows = [full[8 * a : 8 * a + 8] for a in range(BLOCKS)]
    for a in range(2):
        rows[a] = jnp.where(col >= 48, corner[8 * a : 8 * a + 8], rows[a])
    diagonal = rows[0]
    for a in range(1, BLOCKS):
        diagonal = jnp.where(col // 8 == a, rows[a], diagonal)
    diagonal = jnp.where(col % 8 >= sub, diagonal, 0.0)
    pairs = []
    for a in range(4):
        other = rows[7 - a] if a == 0 else pltpu.roll(rows[7 - a], 8 * a, 1)
        pairs.append(
            jnp.where(col >= 8 * (a + 1), rows[a], jnp.where(col < 8 * a, other, 0.0))
        )
    first = jnp.where(lane < 64, pairs[0], pairs[1])
    second = jnp.where(lane < 64, pairs[2], pairs[3])
    halves = jnp.where(lane < 64, diagonal, pltpu.roll(diagonal, 4, 0))
    return jnp.concatenate([first, second, halves], axis=0)


def unpack(packed):
    first, second, halves = packed[0:8], packed[8:16], packed[16:24]
    diagonal = jnp.where(
        iota((8, 128), 0) < 4, low_half(halves), pltpu.roll(high_half(halves), 4, 0)
    )
    pairs = [low_half(first), high_half(first), low_half(second), high_half(second)]
    rows = [None] * BLOCKS
    for a in range(4):
        rows[a] = pairs[a]
        rows[7 - a] = pairs[a] if a == 0 else pltpu.roll(pairs[a], 128 - 8 * a, 1)
    col = iota((8, 128), 1) % 64
    return [jnp.where(col // 8 == a, diagonal, rows[a]) for a in range(BLOCKS)], diagonal


def log_total(items):
    top = functools.reduce(jnp.maximum, items)
    return top + jnp.log(functools.reduce(jnp.add, [jnp.exp(x - top) for x in items]))


def row_of(columns):
    col = iota((8, 128), 1) % 64
    sub = iota((8, 128), 0)
    total = None
    for a, column in enumerate(columns):
        part = jnp.where(col == 8 * a + sub, column, 0.0)
        total = part if total is None else total + part
    return jnp.sum(total, axis=0, keepdims=True)


def rate_terms(rates, log_k):
    lane = iota((8, 128), 1)
    col = lane % 64
    sub = iota((8, 128), 0)
    stay = [jnp.log(1.0 - r) for r in rates]
    stay_row = row_of(stay)
    sums = None
    for a in range(BLOCKS):
        part = jnp.where(8 * a + sub <= col, stay[a], 0.0)
        sums = part if sums is None else sums + part
    reach_row = jnp.sum(sums, axis=0, keepdims=True)
    reach_col = [
        jnp.sum(jnp.where((lane < 64) & (col <= 8 * a + sub), stay_row, 0.0), axis=1, keepdims=True)
        for a in range(BLOCKS)
    ]
    jump_col = [jnp.log(r) - log_k for r in rates]
    jump_row = row_of(jump_col)
    start = jnp.full((8, 1), -log_k, F32)
    jump_col[0] = jnp.where(iota((8, 1), 0) == 0, start, jump_col[0])
    return reach_row, reach_col, jump_row, jump_col


def solve(packed, terms, log_k):
    reach_row, reach_col, jump_row, jump_col = terms
    lane = iota((8, 128), 1)
    sub = iota((8, 128), 0)
    col = lane % 64
    block = col // 8
    within = col % 8
    rows, diagonal = unpack(packed)
    paths = [
        jnp.where(col >= 8 * a + sub, rows[a] + (reach_row - reach_col[a]), NEG)
        for a in range(BLOCKS)
    ]
    reach_diag = jnp.broadcast_to(reach_col[0], (8, 128))
    jump_diag = jnp.broadcast_to(jump_col[0], (8, 128))
    for a in range(1, BLOCKS):
        reach_diag = jnp.where(block == a, reach_col[a], reach_diag)
        jump_diag = jnp.where(block == a, jump_col[a], jump_diag)
    path_diag = diagonal + (reach_row - reach_diag)
    ahead = pltpu.roll(path_diag + jump_diag, 7, 0)
    behind = pltpu.roll(path_diag, 1, 1) + jump_row
    inner = jnp.exp(jnp.where(within > sub, jnp.where(lane < 64, ahead, behind), NEG))
    spread = jnp.concatenate(
        [jnp.where(lane % 8 == sub, inner[m : m + 1], 0.0) for m in range(8)], axis=0
    )
    same = (iota((128, 128), 0) // 8 == iota((128, 128), 1) // 8).astype(BF16)
    coarse = spread.astype(BF16)
    fine = (spread - coarse.astype(F32)).astype(BF16)
    columns = jnp.dot(coarse, same, preferred_element_type=F32)
    columns = columns + jnp.dot(fine, same, preferred_element_type=F32)
    inverse = jnp.where(within == sub, 1.0, 0.0)
    for m in range(7):
        inverse = inverse + columns[8 * m : 8 * m + 8] * inverse[m : m + 1]
    forward_inverse = jnp.where(lane < 64, inverse, 0.0)
    backward_inverse = high_half(inverse)

    offset = jnp.broadcast_to(paths[0][7:8], (8, 128))
    for a in range(1, BLOCKS):
        offset = jnp.where(sub == a, paths[a][7:8], offset)
    offset = jnp.where((within == 0) & (block > sub), offset, 0.0)
    for step in (1, 2, 4):
        offset = offset + pltpu.roll(offset, step, 1)
    factors = [jnp.exp(paths[a] - offset[a : a + 1]) for a in range(BLOCKS)]
    jumps = [jnp.broadcast_to(jnp.exp(j), (8, 128)) for j in jump_col]
    jumps_row = jnp.exp(jump_row)

    row_lane = iota((1, 128), 1)
    row_col = row_lane % 64
    zero = jnp.zeros((1, 128), F32)

    sums = []
    scales = [zero, zero]
    last = jnp.ones((1, 128), F32)
    spent = jnp.zeros((8, 128), F32)
    scale_col = jnp.zeros((8, 128), F32)

    back = zero
    back_scales = [zero, zero]
    back_scale_row = zero
    back_sums = zero
    behind_row = jnp.where(row_lane == 63, math.exp(-log_k), 0.0)

    for b in range(BLOCKS):
        entering = last * jumps[b][0:1]
        lead = entering * factors[b][0:1]
        if b:
            weight = jnp.where(sub < b, jnp.exp(offset + scale_col - scales[b]), 0.0)
            lead = lead + jnp.sum(weight * spent, axis=0, keepdims=True)
        here = jnp.sum(
            jnp.where(block == b, lead * forward_inverse, 0.0), axis=1, keepdims=True
        )
        here = jnp.broadcast_to(here, (8, 128))
        sums.append(here)
        injected = jumps[b] * jnp.where(sub == 0, last, pltpu.roll(here, 1, 0))
        if b < BLOCKS - 1:
            spent = jnp.where(
                sub == b, jnp.sum(injected * factors[b], axis=0, keepdims=True), spent
            )
            scale_col = jnp.where(sub == b, scales[b], scale_col)
            last = here[7:8] * jnp.exp(scales[b] - scales[b + 1])
            scales.append(jnp.log(here[7:8]) + scales[b])

        c = BLOCKS - 1 - b
        weight = jnp.exp(offset[c : c + 1] + back_scale_row - back_scales[b])
        weight = jnp.where((row_lane >= 8 * c + 7) & (row_lane < 64), weight * behind_row, 0.0)
        lead = jnp.sum(factors[c] * weight, axis=1, keepdims=True)
        back = jnp.sum(lead * backward_inverse, axis=0, keepdims=True)
        back_sums = jnp.where(row_col // 8 == c, jnp.log(back) + back_scales[b], back_sums)
        if c:
            fresh = pltpu.roll(back * jumps_row, 127, 1)
            inside = (row_lane >= 8 * c - 1) & (row_lane <= 8 * c + 6)
            behind_row = jnp.where(inside, fresh, behind_row)
            back_scale_row = jnp.where(inside, back_scales[b], back_scale_row)
            first = jnp.sum(
                jnp.where(row_lane == 8 * c, back, 0.0), axis=1, keepdims=True
            )
            back_scales.append(jnp.log(first) + back_scales[b])

    scale_row = zero
    for b in range(BLOCKS):
        scale_row = jnp.where(row_col // 8 == b, scales[b], scale_row)
    forward_row = jnp.log(row_of(sums)) + scale_row
    return jnp.where(row_lane < 64, forward_row, back_sums)


def emission_terms(geno_row):
    g = geno_row
    base = jnp.where(g == 2.0, 1.0, jnp.where(g == 1.0, DOWN, UP))
    slope = jnp.where(g == 2.0, 0.0, jnp.where(g == 1.0, UP - DOWN, DOWN - UP))
    return base, slope


def state_terms(logs, rate_row, k):
    lane = iota((1, 128), 1)
    before = jnp.where(lane == 0, 0.0, pltpu.roll(logs, 1, 1))
    after = jnp.where(lane == 127, 0.0, pltpu.roll(logs, 127, 1))
    over_forward = jnp.exp(before - logs)
    over_backward = pltpu.roll(jnp.exp(after - logs), 64, 1)
    keep = 1.0 - rate_row
    jump = rate_row * (1.0 / k)
    rows = (keep * over_forward, jump * over_forward, keep * over_backward, jump)
    return [jnp.broadcast_to(row, (8, 128)) for row in rows]


def gather_sublanes(tiles):
    sub = iota((8, 128), 0)
    step = 4
    while len(tiles) > 1:
        half = len(tiles) // 2
        low = sub & step == 0
        merged = []
        for i in range(half):
            first, second = tiles[i], tiles[i + half]
            kept = jnp.where(low, first, second)
            moved = jnp.where(low, second, first)
            merged.append(kept + pltpu.roll(moved, step, 0) if step == 4 else kept + swap_by(moved, step))
        tiles = merged
        step //= 2
    return tiles[0]


def swap_by(x, step):
    low = iota((8, 128), 0) & step == 0
    return jnp.where(low, pltpu.roll(x, 8 - step, 0), pltpu.roll(x, step, 0))


def far_first(n):
    return sorted(range(1, n), key=lambda d: -min(d, n - d))


def kernel(
    n_y, n_z, k,
    panel_ref, rate_ref, geno_ref,
    dosage_ref, like_ref,
    rate_own, geno_own, panel_own, panel_all, meta_all, tiles, emis, fwd, bwd,
    log_send, log_plane, log_mid, log_z, log_last,
    solve_send, solve_recv, sum_send, sum_all, dose_send, dose_recv,
    load_sem, own_sem, tile_sem, known,
    panel_s, panel_r, meta_s, meta_r, plane_s, plane_r, z_s, z_r,
    core_s, core_r, all_s, all_r, dose_s, dose_r,
):
    n_group = BLOCKS
    n_x = n_group // 2
    group = lax.axis_index("group")
    batch = lax.axis_index("batch")
    core = group % 2
    x = group // 2
    y = batch % n_y
    z = batch // n_y
    width = panel_all.shape[2]
    log_k = math.log(k)

    def in_group(d):
        return (group + d) % n_group

    def group_peer(d):
        return (in_group(d), batch)

    def y_peer(d):
        return (group, z * n_y + (y + d) % n_y)

    def z_peer(d):
        return (group, ((z + d) % n_z) * n_y + y)

    def plane_peer(dx, dy):
        return (((x + dx) % n_x) * 2 + core, z * n_y + (y + dy) % n_y)

    def remote(src, dst, send, recv, peer):
        return pltpu.make_async_remote_copy(
            src_ref=src, dst_ref=dst, send_sem=send, recv_sem=recv,
            device_id=peer, device_id_type=MESH,
        )

    def finish(copies):
        for copy in copies:
            copy.wait()

    loads = [
        pltpu.make_async_copy(rate_ref, rate_own, load_sem.at[0]),
        pltpu.make_async_copy(geno_ref, geno_own, load_sem.at[1]),
        pltpu.make_async_copy(panel_ref, panel_own, load_sem.at[2]),
    ]
    own = pltpu.make_async_copy(
        panel_ref.at[:, pl.ds(pl.multiple_of(x * width, width), width)],
        panel_all.at[group],
        own_sem,
    )
    for load in loads:
        load.start()
    own.start()
    barrier = pltpu.get_barrier_semaphore()
    near_y = [y_peer(d) for d in sorted({1, n_y - 1}) if 0 < d < n_y]
    near_z = [z_peer(d) for d in sorted({1, n_z - 1}) if 0 < d < n_z]
    peers = [group_peer(d) for d in far_first(n_group)] + near_y + near_z
    for peer in peers:
        pl.semaphore_signal(barrier, inc=1, device_id=peer, device_id_type=MESH)
    finish(loads)
    meta_all[group] = meta_tile(rate_own[...], geno_own[...])
    pl.semaphore_wait(barrier, len(peers))

    copies = []
    for d in far_first(n_group):
        start = pl.multiple_of(in_group(d) // 2 * width, width)
        copies.append(
            remote(
                panel_own.at[:, pl.ds(start, width)], panel_all.at[group],
                panel_s.at[d - 1], panel_r.at[d - 1], group_peer(d),
            )
        )
    for d in far_first(n_group):
        copies.append(
            remote(
                meta_all.at[group], meta_all.at[group],
                meta_s.at[d - 1], meta_r.at[d - 1], group_peer(d),
            )
        )
    for copy in copies:
        copy.start()
    for turn, near in enumerate([near_y + near_z, near_y + near_z, near_z]):
        for peer in near:
            pl.semaphore_signal(known.at[turn], inc=1, device_id=peer, device_id_type=MESH)
        if near:
            pl.semaphore_wait(known.at[turn], len(near))
    own.wait()
    finish(copies)

    relayout = []
    for c in range(8):
        copy = pltpu.make_async_copy(
            panel_all.at[:, :, pl.ds(128 * c, 128)], tiles.at[:, :, c], tile_sem.at[c]
        )
        copy.start()
        relayout.append(copy)

    meta = meta_all[...].reshape(MARKERS, 128)
    signs = 2.0 * panel_all[...].reshape(MARKERS, width).astype(F32) - 1.0
    genotype = jnp.where(core == 0, meta[:, 1:2], meta[:, 2:3])
    log_send[...] = couplings(signs, genotype)
    sent = pl.ds(0, 20)

    plane = [(dx, dy) for dx in range(n_x) for dy in range(n_y) if dx or dy]
    plane.sort(key=lambda p: -(min(p[0], n_x - p[0]) + min(p[1], n_y - p[1])))
    flying = [
        remote(
            log_send.at[sent], log_plane.at[i], plane_s.at[i], plane_r.at[i], plane_peer(dx, dy)
        )
        for i, (dx, dy) in enumerate(plane)
    ]
    for copy in flying:
        copy.start()
    rates = [meta[8 * a : 8 * a + 8, 0:1] for a in range(BLOCKS)]
    terms = rate_terms(rates, log_k)
    rate_row = row_of(rates)
    geno_row = row_of([genotype[8 * a : 8 * a + 8] for a in range(BLOCKS)])
    base, slope = emission_terms(geno_row)
    log_mid[...] = jnp.zeros((24, 128), F32)
    log_last[...] = jnp.zeros((24, 128), F32)
    finish(flying)
    total = log_total([log_send[0:20]] + [log_plane[i] for i in range(len(plane))])
    log_mid[0:20] = total

    flying = [
        remote(log_mid.at[sent], log_z.at[d - 1], z_s.at[d - 1], z_r.at[d - 1], z_peer(d))
        for d in far_first(n_z)
    ]
    for copy in flying:
        copy.start()
    finish(relayout)
    for t in range(MARKERS):
        allele = tiles[t // 8, t % 8].astype(F32)
        emis[t] = base[:, t : t + 1] + slope[:, t : t + 1] * allele
    finish(flying)
    log_last[0:20] = log_total([total] + [log_z[d] for d in range(n_z - 1)])

    solved = solve(log_last[...], terms, log_k)

    lane_row = iota((1, 128), 1)
    seen = jnp.sum(
        jnp.where((lane_row < 64) & (geno_row != 2.0), LOG_CENTRE, 0.0), axis=1, keepdims=True
    )
    like = jnp.broadcast_to((solved[:, 63:64] + seen) * (1.0 / MARKERS), (1, 128))
    solve_send[...] = like
    partner = (group + 1 - 2 * core, batch)
    swap = remote(solve_send, solve_recv, core_s, core_r, partner)
    swap.start()

    keep_f, jump_f, keep_b, jump_b = state_terms(solved, rate_row, float(k))
    ahead = jnp.full((8, 128), 1.0 / k, F32)
    behind = jnp.full((8, 128), 1.0 / k, F32)
    for i in range(MARKERS):
        ahead = emis[i] * (keep_f[:, i : i + 1] * ahead + jump_f[:, i : i + 1])
        fwd[i] = ahead
        t = MARKERS - 1 - i
        bwd[t] = behind
        behind = keep_b[:, t : t + 1] * (emis[t] * behind) + jump_b[:, t : t + 1]

    over_k = []
    for which in range(2):
        for a in range(BLOCKS):
            both = fwd[8 * a : 8 * a + 8] * bwd[8 * a : 8 * a + 8]
            if which == 0:
                both = both * tiles[a].astype(F32)
            over_k.append(gather_sublanes([both[i] for i in range(8)]))
    stacked = jnp.concatenate(over_k, axis=0)
    ones = jnp.ones((8, 128), BF16)
    coarse = stacked.astype(BF16)
    fine = (stacked - coarse.astype(F32)).astype(BF16)
    total = (dot_nt(ones, coarse) + dot_nt(ones, fine))[0:1]

    everyone = [
        (dx, dy, dz) for dx in range(n_x) for dy in range(n_y) for dz in range(n_z)
        if dx or dy or dz
    ]
    everyone.sort(
        key=lambda p: -(min(p[0], n_x - p[0]) + min(p[1], n_y - p[1]) + min(p[2], n_z - p[2]))
    )
    others = len(everyone)
    sum_send[...] = total
    for i, (dx, dy, dz) in enumerate(everyone):
        peer = (
            ((x + dx) % n_x) * 2 + core,
            ((z + dz) % n_z) * n_y + (y + dy) % n_y,
        )
        remote(sum_send, sum_all.at[pl.ds(i, 1)], all_s, all_r, peer).start()
    sum_all[others : others + 1] = total
    swap.wait()
    other = solve_recv[...]
    like_ref[...] = jnp.where(
        lane_row == 0, jnp.where(core == 0, like, other), jnp.where(core == 0, other, like)
    )[:, 0:2]
    rest = pl.ds(0, others)
    remote(sum_all.at[rest], sum_all.at[rest], all_s, all_r, partner).wait()
    total = jnp.sum(sum_all[...], axis=0, keepdims=True)
    share = total / pltpu.roll(total, 64, 1)
    dose_send[...] = share
    trade = remote(dose_send, dose_recv, dose_s, dose_r, partner)
    trade.start()
    shift = (128 - 8 * group) % 128
    mine = pltpu.roll(share, shift, 1)
    trade.wait()
    theirs = pltpu.roll(dose_recv[...], shift, 1)
    dosage_ref[0:1] = jnp.where(core == 0, mine, theirs)[:, 0:8]
    dosage_ref[1:2] = jnp.where(core == 0, theirs, mine)[:, 0:8]


def on_device(n_y, panel, rates, genotypes):
    n_batch = lax.axis_size("batch")
    n_group = lax.axis_size("group")
    n_z = n_batch // n_y
    held = panel.shape[1]
    width = held // (n_group // 2)
    k = held * n_batch
    dma = pltpu.SemaphoreType.DMA
    vmem = pltpu.VMEM
    g1, z1, p1 = n_group - 1, max(n_z - 1, 1), n_group // 2 * n_y - 1
    scratch = [
        vmem((1, BLOCK), F32),
        vmem((2, BLOCK), jnp.int32),
        vmem((BLOCK, held), jnp.int32),
        vmem((BLOCKS, BLOCK, width), jnp.int32),
        vmem((BLOCKS, BLOCK, 128), F32),
        vmem((BLOCKS, BLOCK, 8, 128), jnp.int32),
        vmem((MARKERS, 8, 128), F32),
        vmem((MARKERS, 8, 128), F32),
        vmem((MARKERS, 8, 128), F32),
        vmem((24, 128), F32),
        vmem((p1, 20, 128), F32),
        vmem((24, 128), F32),
        vmem((z1, 20, 128), F32),
        vmem((24, 128), F32),
        vmem((1, 128), F32),
        vmem((1, 128), F32),
        vmem((1, 128), F32),
        vmem((n_group // 2 * n_batch, 128), F32),
        vmem((1, 128), F32),
        vmem((1, 128), F32),
        dma((3,)),
        dma,
        dma((8,)),
        pltpu.SemaphoreType.REGULAR((3,)),
        dma((g1,)), dma((g1,)), dma((g1,)), dma((g1,)), dma((p1,)), dma((p1,)),
        dma((z1,)), dma((z1,)),
        dma, dma,
        dma, dma, dma, dma,
    ]
    dosage, like = pl.pallas_call(
        functools.partial(kernel, n_y, n_z, k),
        out_shape=(
            pltpu.VMEM((2, BLOCK), F32),
            pltpu.VMEM((1, 2), F32),
        ),
        in_specs=[
            pl.BlockSpec(memory_space=pl.ANY),
            pl.BlockSpec(memory_space=pl.ANY),
            pl.BlockSpec(memory_space=pl.ANY),
        ],
        out_specs=(
            pl.BlockSpec(memory_space=pltpu.VMEM),
            pl.BlockSpec(memory_space=pltpu.VMEM),
        ),
        scratch_shapes=scratch,
        compiler_params=pltpu.CompilerParams(collective_id=0, has_side_effects=True),
    )(panel, rates.reshape(1, BLOCK), genotypes)
    return dosage, like.reshape(2)


def solution(mesh, n_y=4):
    placed = (P("group", "batch"), P("group"), P(None, "group"))
    return jax.shard_map(
        functools.partial(on_device, n_y),
        mesh=mesh,
        in_specs=placed,
        out_specs=(P(None, "group"), P()),
        check_vma=False,
    )
```

```python
import functools
import math

import jax
import jax.numpy as jnp
from jax import lax
from jax.experimental import pallas as pl
from jax.experimental.pallas import tpu as pltpu
from jax.sharding import PartitionSpec as P

HIGHEST = lax.Precision.HIGHEST
MESH = pl.DeviceIdType.MESH

MISMATCH = 0.05
STEP = 0.5 * math.log((1.0 - MISMATCH) / MISMATCH)
LOG_CENTRE = 0.5 * math.log((1.0 - MISMATCH) * MISMATCH)
UP = math.exp(STEP)
DOWN = math.exp(-STEP)
NEG = -1e30
F32 = jnp.float32
BF16 = jnp.bfloat16

MARKERS = 64
BLOCK = 8
BLOCKS = 8


def iota(shape, axis):
    return lax.broadcasted_iota(jnp.int32, shape, axis)


def dot_nt(a, b, precision=None):
    return lax.dot_general(
        a, b, (((1,), (1,)), ((), ())), precision=precision, preferred_element_type=F32
    )


def low_half(x):
    return jnp.where(iota(x.shape, 1) < 64, x, pltpu.roll(x, 64, 1))


def high_half(x):
    return jnp.where(iota(x.shape, 1) < 64, pltpu.roll(x, 64, 1), x)


def meta_tile(rate_row, geno_rows):
    eye = iota((8, 8), 0) == iota((8, 8), 1)
    lane = iota((8, 128), 1)

    def column(row):
        return jnp.sum(jnp.where(eye, jnp.broadcast_to(row, (8, 8)), 0.0), axis=1, keepdims=True)

    rate = column(rate_row)
    first = column(geno_rows[0:1].astype(F32))
    second = column(geno_rows[1:2].astype(F32))
    return jnp.where(lane == 0, rate, jnp.where(lane == 1, first, second))


def anchor_matrix():
    row = iota((128, 64), 0)
    col = iota((128, 64), 1)
    s = row
    t = row - 64
    upper = jnp.where((col >= s) & (col <= 31), 1.0, jnp.where((col >= 32) & (col < s), -1.0, 0.0))
    lower = jnp.where((col >= 32) & (col <= t), 1.0, jnp.where((col > t) & (col <= 31), -1.0, 0.0))
    return jnp.where(row < 64, upper, lower).astype(BF16)


def product(a, b):
    a_top, b_top = a.astype(BF16), b.astype(BF16)
    a_rest = (a - a_top.astype(F32)).astype(BF16)
    b_rest = (b - b_top.astype(F32)).astype(BF16)
    return dot_nt(a_top, b_top) + (dot_nt(a_rest, b_top) + dot_nt(a_top, b_rest))


def couplings(signs, genotype):
    width = signs.shape[1]
    sign = jnp.where(genotype == 2.0, 0.0, 2.0 * genotype - 1.0)
    steps = jnp.dot(anchor_matrix(), (signs * sign).astype(BF16), preferred_element_type=F32)
    from_s, to_t = steps[:64], steps[64:]
    u = jnp.exp(STEP * from_s)
    v = jnp.exp(STEP * to_t)
    full = jnp.log(product(u, jnp.concatenate([v, v], axis=0)))
    left, right = from_s[16:17], to_t[47:48]
    middle = left + right
    top = jnp.max(middle, axis=1, keepdims=True)
    begin = jnp.exp(STEP * (from_s[:16] - left + (middle - top)))
    end = jnp.exp(STEP * (to_t[48:] - right))
    blank = jnp.zeros((48, width), F32)
    corner = jnp.log(product(begin, jnp.concatenate([blank, end, blank, end], axis=0)))
    corner = corner + STEP * top
    return pack(full, corner)


def pack(full, corner):
    lane = iota((8, 128), 1)
    sub = iota((8, 128), 0)
    col = lane % 64
    rows = [full[8 * a : 8 * a + 8] for a in range(BLOCKS)]
    for a in range(2):
        rows[a] = jnp.where(col >= 48, corner[8 * a : 8 * a + 8], rows[a])
    diagonal = rows[0]
    for a in range(1, BLOCKS):
        diagonal = jnp.where(col // 8 == a, rows[a], diagonal)
    diagonal = jnp.where(col % 8 >= sub, diagonal, 0.0)
    pairs = []
    for a in range(4):
        other = rows[7 - a] if a == 0 else pltpu.roll(rows[7 - a], 8 * a, 1)
        pairs.append(
            jnp.where(col >= 8 * (a + 1), rows[a], jnp.where(col < 8 * a, other, 0.0))
        )
    first = jnp.where(lane < 64, pairs[0], pairs[1])
    second = jnp.where(lane < 64, pairs[2], pairs[3])
    halves = jnp.where(lane < 64, diagonal, pltpu.roll(diagonal, 4, 0))
    return jnp.concatenate([first, second, halves], axis=0)


def unpack(packed):
    first, second, halves = packed[0:8], packed[8:16], packed[16:24]
    diagonal = jnp.where(
        iota((8, 128), 0) < 4, low_half(halves), pltpu.roll(high_half(halves), 4, 0)
    )
    pairs = [low_half(first), high_half(first), low_half(second), high_half(second)]
    rows = [None] * BLOCKS
    for a in range(4):
        rows[a] = pairs[a]
        rows[7 - a] = pairs[a] if a == 0 else pltpu.roll(pairs[a], 128 - 8 * a, 1)
    col = iota((8, 128), 1) % 64
    return [jnp.where(col // 8 == a, diagonal, rows[a]) for a in range(BLOCKS)], diagonal


def log_total(items):
    top = functools.reduce(jnp.maximum, items)
    return top + jnp.log(functools.reduce(jnp.add, [jnp.exp(x - top) for x in items]))


def row_of(columns):
    col = iota((8, 128), 1) % 64
    sub = iota((8, 128), 0)
    total = None
    for a, column in enumerate(columns):
        part = jnp.where(col == 8 * a + sub, column, 0.0)
        total = part if total is None else total + part
    return jnp.sum(total, axis=0, keepdims=True)


def rate_terms(rates, log_k):
    lane = iota((8, 128), 1)
    col = lane % 64
    sub = iota((8, 128), 0)
    stay = [jnp.log(1.0 - r) for r in rates]
    stay_row = row_of(stay)
    sums = None
    for a in range(BLOCKS):
        part = jnp.where(8 * a + sub <= col, stay[a], 0.0)
        sums = part if sums is None else sums + part
    reach_row = jnp.sum(sums, axis=0, keepdims=True)
    reach_col = [
        jnp.sum(jnp.where((lane < 64) & (col <= 8 * a + sub), stay_row, 0.0), axis=1, keepdims=True)
        for a in range(BLOCKS)
    ]
    jump_col = [jnp.log(r) - log_k for r in rates]
    jump_row = row_of(jump_col)
    start = jnp.full((8, 1), -log_k, F32)
    jump_col[0] = jnp.where(iota((8, 1), 0) == 0, start, jump_col[0])
    return reach_row, reach_col, jump_row, jump_col


def solve(packed, terms, log_k):
    reach_row, reach_col, jump_row, jump_col = terms
    lane = iota((8, 128), 1)
    sub = iota((8, 128), 0)
    col = lane % 64
    block = col // 8
    within = col % 8
    rows, diagonal = unpack(packed)
    paths = [
        jnp.where(col >= 8 * a + sub, rows[a] + (reach_row - reach_col[a]), NEG)
        for a in range(BLOCKS)
    ]
    reach_diag = jnp.broadcast_to(reach_col[0], (8, 128))
    jump_diag = jnp.broadcast_to(jump_col[0], (8, 128))
    for a in range(1, BLOCKS):
        reach_diag = jnp.where(block == a, reach_col[a], reach_diag)
        jump_diag = jnp.where(block == a, jump_col[a], jump_diag)
    path_diag = diagonal + (reach_row - reach_diag)
    ahead = pltpu.roll(path_diag + jump_diag, 7, 0)
    behind = pltpu.roll(path_diag, 1, 1) + jump_row
    inner = jnp.exp(jnp.where(within > sub, jnp.where(lane < 64, ahead, behind), NEG))
    spread = jnp.concatenate(
        [jnp.where(lane % 8 == sub, inner[m : m + 1], 0.0) for m in range(8)], axis=0
    )
    same = (iota((128, 128), 0) // 8 == iota((128, 128), 1) // 8).astype(BF16)
    coarse = spread.astype(BF16)
    fine = (spread - coarse.astype(F32)).astype(BF16)
    columns = jnp.dot(coarse, same, preferred_element_type=F32)
    columns = columns + jnp.dot(fine, same, preferred_element_type=F32)
    inverse = jnp.where(within == sub, 1.0, 0.0)
    for m in range(7):
        inverse = inverse + columns[8 * m : 8 * m + 8] * inverse[m : m + 1]
    forward_inverse = jnp.where(lane < 64, inverse, 0.0)
    backward_inverse = high_half(inverse)

    offset = jnp.broadcast_to(paths[0][7:8], (8, 128))
    for a in range(1, BLOCKS):
        offset = jnp.where(sub == a, paths[a][7:8], offset)
    offset = jnp.where((within == 0) & (block > sub), offset, 0.0)
    for step in (1, 2, 4):
        offset = offset + pltpu.roll(offset, step, 1)
    factors = [jnp.exp(paths[a] - offset[a : a + 1]) for a in range(BLOCKS)]
    injectors = [jnp.exp(j) * f for j, f in zip(jump_col, factors)]
    row_lane = iota((1, 128), 1)
    row_col = row_lane % 64
    jumps_row = jnp.where(row_lane == 64, math.exp(-log_k), jnp.exp(jump_row))
    shifted = [pltpu.roll(f, 1, 1) * jumps_row for f in factors]
    shifted_offset = pltpu.roll(offset, 1, 1)
    inverses = [jnp.where(block == b, forward_inverse, 0.0) for b in range(BLOCKS)]

    zero = jnp.zeros((1, 128), F32)
    sums = []
    scales = [zero, zero]
    last = jnp.ones((1, 128), F32)
    spent = jnp.zeros((8, 128), F32)
    scale_col = jnp.zeros((8, 128), F32)
    newest = None

    back_scales = [zero, zero]
    back_scale_row = zero
    back_sums = zero
    behind_row = jnp.where(row_lane == 64, 1.0, 0.0)

    for b in range(BLOCKS):
        lead = last * injectors[b][0:1]
        if b > 1:
            weight = jnp.exp(offset + scale_col - scales[b])
            weight = jnp.where((sub < b - 1) & (block == b), weight, 0.0)
            lead = lead + jnp.sum(weight * spent, axis=0, keepdims=True)
        if b:
            weight = jnp.exp(offset[b - 1 : b] + (scales[b - 1] - scales[b]))
            weight = jnp.where(row_col // 8 == b, weight, 0.0)
            lead = lead + weight * newest
        here = jnp.sum(lead * inverses[b], axis=1, keepdims=True)
        here = jnp.broadcast_to(here, (8, 128))
        sums.append(here)
        if b < BLOCKS - 1:
            before = jnp.where(sub == 0, last, pltpu.roll(here, 1, 0))
            newest = jnp.sum(before * injectors[b], axis=0, keepdims=True)
            spent = jnp.where(sub == b, newest, spent)
            scale_col = jnp.where(sub == b, scales[b], scale_col)
            last = here[7:8] * jnp.exp(scales[b] - scales[b + 1])
            scales.append(jnp.log(here[7:8]) + scales[b])

        c = BLOCKS - 1 - b
        weight = jnp.exp(shifted_offset[c : c + 1] + (back_scale_row - back_scales[b]))
        weight = jnp.where((row_lane >= 8 * c + 8) & (row_lane <= 64), weight, 0.0)
        pulled = shifted[c] * weight
        lead = jnp.sum(pulled * behind_row, axis=1, keepdims=True)
        back = jnp.sum(lead * backward_inverse, axis=0, keepdims=True)
        inside = (row_lane >= 8 * c) & (row_lane < 8 * c + 8)
        back_sums = jnp.where(row_col // 8 == c, jnp.log(back) + back_scales[b], back_sums)
        if c:
            behind_row = jnp.where(inside, back, behind_row)
            back_scale_row = jnp.where(inside, back_scales[b], back_scale_row)
            first = jnp.sum(
                jnp.where(row_lane == 8 * c, back, 0.0), axis=1, keepdims=True
            )
            back_scales.append(jnp.log(first) + back_scales[b])

    scale_row = zero
    for b in range(BLOCKS):
        scale_row = jnp.where(row_col // 8 == b, scales[b], scale_row)
    forward_row = jnp.log(row_of(sums)) + scale_row
    return jnp.where(row_lane < 64, forward_row, back_sums)


def emission_terms(geno_row):
    g = geno_row
    base = jnp.where(g == 2.0, 1.0, jnp.where(g == 1.0, DOWN, UP))
    slope = jnp.where(g == 2.0, 0.0, jnp.where(g == 1.0, UP - DOWN, DOWN - UP))
    return base, slope


def state_terms(logs, rate_row, k):
    lane = iota((1, 128), 1)
    before = jnp.where(lane == 0, 0.0, pltpu.roll(logs, 1, 1))
    after = jnp.where(lane == 127, 0.0, pltpu.roll(logs, 127, 1))
    over_forward = jnp.exp(before - logs)
    over_backward = pltpu.roll(jnp.exp(after - logs), 64, 1)
    keep = 1.0 - rate_row
    jump = rate_row * (1.0 / k)
    rows = (keep * over_forward, jump * over_forward, keep * over_backward, jump)
    return [jnp.broadcast_to(row, (8, 128)) for row in rows]


def gather_sublanes(tiles):
    sub = iota((8, 128), 0)
    step = 4
    while len(tiles) > 1:
        half = len(tiles) // 2
        low = sub & step == 0
        merged = []
        for i in range(half):
            first, second = tiles[i], tiles[i + half]
            kept = jnp.where(low, first, second)
            moved = jnp.where(low, second, first)
            merged.append(kept + pltpu.roll(moved, step, 0) if step == 4 else kept + swap_by(moved, step))
        tiles = merged
        step //= 2
    return tiles[0]


def swap_by(x, step):
    low = iota((8, 128), 0) & step == 0
    return jnp.where(low, pltpu.roll(x, 8 - step, 0), pltpu.roll(x, step, 0))


def far_first(n):
    return sorted(range(1, n), key=lambda d: -min(d, n - d))


def kernel(
    n_y, n_z, k,
    panel_ref, rate_ref, geno_ref,
    dosage_ref, like_ref,
    rate_own, geno_own, panel_own, panel_all, meta_all, tiles, emis, fwd, bwd,
    log_send, log_plane, log_mid, log_z, log_last,
    solve_send, solve_recv, sum_send, sum_all, dose_send, dose_recv,
    load_sem, own_sem, tile_sem, known,
    panel_s, panel_r, meta_s, meta_r, plane_s, plane_r, z_s, z_r,
    core_s, core_r, all_s, all_r, dose_s, dose_r,
):
    n_group = BLOCKS
    n_x = n_group // 2
    group = lax.axis_index("group")
    batch = lax.axis_index("batch")
    core = group % 2
    x = group // 2
    y = batch % n_y
    z = batch // n_y
    width = panel_all.shape[2]
    log_k = math.log(k)

    def in_group(d):
        return (group + d) % n_group

    def group_peer(d):
        return (in_group(d), batch)

    def y_peer(d):
        return (group, z * n_y + (y + d) % n_y)

    def z_peer(d):
        return (group, ((z + d) % n_z) * n_y + y)

    def plane_peer(dx, dy):
        return (((x + dx) % n_x) * 2 + core, z * n_y + (y + dy) % n_y)

    def remote(src, dst, send, recv, peer):
        return pltpu.make_async_remote_copy(
            src_ref=src, dst_ref=dst, send_sem=send, recv_sem=recv,
            device_id=peer, device_id_type=MESH,
        )

    def finish(copies):
        for copy in copies:
            copy.wait()

    loads = [
        pltpu.make_async_copy(rate_ref, rate_own, load_sem.at[0]),
        pltpu.make_async_copy(geno_ref, geno_own, load_sem.at[1]),
        pltpu.make_async_copy(panel_ref, panel_own, load_sem.at[2]),
    ]
    own = pltpu.make_async_copy(
        panel_ref.at[:, pl.ds(pl.multiple_of(x * width, width), width)],
        panel_all.at[group],
        own_sem,
    )
    for load in loads:
        load.start()
    own.start()
    barrier = pltpu.get_barrier_semaphore()
    near_y = [y_peer(d) for d in sorted({1, n_y - 1}) if 0 < d < n_y]
    near_z = [z_peer(d) for d in sorted({1, n_z - 1}) if 0 < d < n_z]
    peers = [group_peer(d) for d in far_first(n_group)] + near_y + near_z
    for peer in peers:
        pl.semaphore_signal(barrier, inc=1, device_id=peer, device_id_type=MESH)
    finish(loads)
    meta_all[group] = meta_tile(rate_own[...], geno_own[...])
    pl.semaphore_wait(barrier, len(peers))

    copies = []
    for d in far_first(n_group):
        start = pl.multiple_of(in_group(d) // 2 * width, width)
        copies.append(
            remote(
                panel_own.at[:, pl.ds(start, width)], panel_all.at[group],
                panel_s.at[d - 1], panel_r.at[d - 1], group_peer(d),
            )
        )
    for d in far_first(n_group):
        copies.append(
            remote(
                meta_all.at[group], meta_all.at[group],
                meta_s.at[d - 1], meta_r.at[d - 1], group_peer(d),
            )
        )
    for copy in copies:
        copy.start()
    for turn, near in enumerate([near_y + near_z, near_y + near_z, near_z]):
        for peer in near:
            pl.semaphore_signal(known.at[turn], inc=1, device_id=peer, device_id_type=MESH)
        if near:
            pl.semaphore_wait(known.at[turn], len(near))
    own.wait()
    finish(copies)

    relayout = []
    for c in range(8):
        copy = pltpu.make_async_copy(
            panel_all.at[:, :, pl.ds(128 * c, 128)], tiles.at[:, :, c], tile_sem.at[c]
        )
        copy.start()
        relayout.append(copy)

    meta = meta_all[...].reshape(MARKERS, 128)
    signs = 2.0 * panel_all[...].reshape(MARKERS, width).astype(F32) - 1.0
    genotype = jnp.where(core == 0, meta[:, 1:2], meta[:, 2:3])
    log_send[...] = couplings(signs, genotype)
    sent = pl.ds(0, 20)

    plane = [(dx, dy) for dx in range(n_x) for dy in range(n_y) if dx or dy]
    plane.sort(key=lambda p: -(min(p[0], n_x - p[0]) + min(p[1], n_y - p[1])))
    flying = [
        remote(
            log_send.at[sent], log_plane.at[i], plane_s.at[i], plane_r.at[i], plane_peer(dx, dy)
        )
        for i, (dx, dy) in enumerate(plane)
    ]
    for copy in flying:
        copy.start()
    rates = [meta[8 * a : 8 * a + 8, 0:1] for a in range(BLOCKS)]
    terms = rate_terms(rates, log_k)
    rate_row = row_of(rates)
    geno_row = row_of([genotype[8 * a : 8 * a + 8] for a in range(BLOCKS)])
    base, slope = emission_terms(geno_row)
    log_mid[...] = jnp.zeros((24, 128), F32)
    log_last[...] = jnp.zeros((24, 128), F32)
    finish(flying)
    total = log_total([log_send[0:20]] + [log_plane[i] for i in range(len(plane))])
    log_mid[0:20] = total

    flying = [
        remote(log_mid.at[sent], log_z.at[d - 1], z_s.at[d - 1], z_r.at[d - 1], z_peer(d))
        for d in far_first(n_z)
    ]
    for copy in flying:
        copy.start()
    finish(relayout)
    for t in range(MARKERS):
        allele = tiles[t // 8, t % 8].astype(F32)
        emis[t] = base[:, t : t + 1] + slope[:, t : t + 1] * allele
    finish(flying)
    log_last[0:20] = log_total([total] + [log_z[d] for d in range(n_z - 1)])

    solved = solve(log_last[...], terms, log_k)

    lane_row = iota((1, 128), 1)
    seen = jnp.sum(
        jnp.where((lane_row < 64) & (geno_row != 2.0), LOG_CENTRE, 0.0), axis=1, keepdims=True
    )
    like = jnp.broadcast_to((solved[:, 63:64] + seen) * (1.0 / MARKERS), (1, 128))
    solve_send[...] = like
    partner = (group + 1 - 2 * core, batch)
    swap = remote(solve_send, solve_recv, core_s, core_r, partner)
    swap.start()

    keep_f, jump_f, keep_b, jump_b = state_terms(solved, rate_row, float(k))
    ahead = jnp.full((8, 128), 1.0 / k, F32)
    behind = jnp.full((8, 128), 1.0 / k, F32)
    for i in range(MARKERS):
        kept, added = emis[i] * keep_f[:, i : i + 1], emis[i] * jump_f[:, i : i + 1]
        ahead = kept * ahead + added
        fwd[i] = ahead
        t = MARKERS - 1 - i
        bwd[t] = behind
        behind = (keep_b[:, t : t + 1] * emis[t]) * behind + jump_b[:, t : t + 1]

    over_k = []
    for which in range(2):
        for a in range(BLOCKS):
            both = fwd[8 * a : 8 * a + 8] * bwd[8 * a : 8 * a + 8]
            if which == 0:
                both = both * tiles[a].astype(F32)
            over_k.append(gather_sublanes([both[i] for i in range(8)]))
    stacked = jnp.concatenate(over_k, axis=0)
    ones = jnp.ones((8, 128), BF16)
    coarse = stacked.astype(BF16)
    fine = (stacked - coarse.astype(F32)).astype(BF16)
    total = (dot_nt(ones, coarse) + dot_nt(ones, fine))[0:1]

    everyone = [
        (dx, dy, dz) for dx in range(n_x) for dy in range(n_y) for dz in range(n_z)
        if dx or dy or dz
    ]
    everyone.sort(
        key=lambda p: -(min(p[0], n_x - p[0]) + min(p[1], n_y - p[1]) + min(p[2], n_z - p[2]))
    )
    others = len(everyone)
    sum_send[...] = total
    for i, (dx, dy, dz) in enumerate(everyone):
        peer = (
            ((x + dx) % n_x) * 2 + core,
            ((z + dz) % n_z) * n_y + (y + dy) % n_y,
        )
        remote(sum_send, sum_all.at[pl.ds(i, 1)], all_s, all_r, peer).start()
    sum_all[others : others + 1] = total
    swap.wait()
    other = solve_recv[...]
    like_ref[...] = jnp.where(
        lane_row == 0, jnp.where(core == 0, like, other), jnp.where(core == 0, other, like)
    )[:, 0:2]
    rest = pl.ds(0, others)
    remote(sum_all.at[rest], sum_all.at[rest], all_s, all_r, partner).wait()
    total = jnp.sum(sum_all[...], axis=0, keepdims=True)
    share = total / pltpu.roll(total, 64, 1)
    dose_send[...] = share
    trade = remote(dose_send, dose_recv, dose_s, dose_r, partner)
    trade.start()
    shift = (128 - 8 * group) % 128
    mine = pltpu.roll(share, shift, 1)
    trade.wait()
    theirs = pltpu.roll(dose_recv[...], shift, 1)
    dosage_ref[0:1] = jnp.where(core == 0, mine, theirs)[:, 0:8]
    dosage_ref[1:2] = jnp.where(core == 0, theirs, mine)[:, 0:8]


def on_device(n_y, panel, rates, genotypes):
    n_batch = lax.axis_size("batch")
    n_group = lax.axis_size("group")
    n_z = n_batch // n_y
    held = panel.shape[1]
    width = held // (n_group // 2)
    k = held * n_batch
    dma = pltpu.SemaphoreType.DMA
    vmem = pltpu.VMEM
    g1, z1, p1 = n_group - 1, max(n_z - 1, 1), n_group // 2 * n_y - 1
    scratch = [
        vmem((1, BLOCK), F32),
        vmem((2, BLOCK), jnp.int32),
        vmem((BLOCK, held), jnp.int32),
        vmem((BLOCKS, BLOCK, width), jnp.int32),
        vmem((BLOCKS, BLOCK, 128), F32),
        vmem((BLOCKS, BLOCK, 8, 128), jnp.int32),
        vmem((MARKERS, 8, 128), F32),
        vmem((MARKERS, 8, 128), F32),
        vmem((MARKERS, 8, 128), F32),
        vmem((24, 128), F32),
        vmem((p1, 20, 128), F32),
        vmem((24, 128), F32),
        vmem((z1, 20, 128), F32),
        vmem((24, 128), F32),
        vmem((1, 128), F32),
        vmem((1, 128), F32),
        vmem((1, 128), F32),
        vmem((n_group // 2 * n_batch, 128), F32),
        vmem((1, 128), F32),
        vmem((1, 128), F32),
        dma((3,)),
        dma,
        dma((8,)),
        pltpu.SemaphoreType.REGULAR((3,)),
        dma((g1,)), dma((g1,)), dma((g1,)), dma((g1,)), dma((p1,)), dma((p1,)),
        dma((z1,)), dma((z1,)),
        dma, dma,
        dma, dma, dma, dma,
    ]
    dosage, like = pl.pallas_call(
        functools.partial(kernel, n_y, n_z, k),
        out_shape=(
            pltpu.VMEM((2, BLOCK), F32),
            pltpu.VMEM((1, 2), F32),
        ),
        in_specs=[
            pl.BlockSpec(memory_space=pl.ANY),
            pl.BlockSpec(memory_space=pl.ANY),
            pl.BlockSpec(memory_space=pl.ANY),
        ],
        out_specs=(
            pl.BlockSpec(memory_space=pltpu.VMEM),
            pl.BlockSpec(memory_space=pltpu.VMEM),
        ),
        scratch_shapes=scratch,
        compiler_params=pltpu.CompilerParams(collective_id=0, has_side_effects=True),
    )(panel, rates.reshape(1, BLOCK), genotypes)
    return dosage, like.reshape(2)


def solution(mesh, n_y=4):
    placed = (P("group", "batch"), P("group"), P(None, "group"))
    return jax.shard_map(
        functools.partial(on_device, n_y),
        mesh=mesh,
        in_specs=placed,
        out_specs=(P(None, "group"), P()),
        check_vma=False,
    )
```

```python
import functools
import math

import jax
import jax.numpy as jnp
from jax import lax
from jax.experimental import pallas as pl
from jax.experimental.pallas import tpu as pltpu
from jax.sharding import PartitionSpec as P

HIGHEST = lax.Precision.HIGHEST
MESH = pl.DeviceIdType.MESH

MISMATCH = 0.05
STEP = 0.5 * math.log((1.0 - MISMATCH) / MISMATCH)
LOG_CENTRE = 0.5 * math.log((1.0 - MISMATCH) * MISMATCH)
UP = math.exp(STEP)
DOWN = math.exp(-STEP)
NEG = -1e30
F32 = jnp.float32
BF16 = jnp.bfloat16

MARKERS = 64
BLOCK = 8
BLOCKS = 8


def iota(shape, axis):
    return lax.broadcasted_iota(jnp.int32, shape, axis)


def dot_nt(a, b, precision=None):
    return lax.dot_general(
        a, b, (((1,), (1,)), ((), ())), precision=precision, preferred_element_type=F32
    )


def low_half(x):
    return jnp.where(iota(x.shape, 1) < 64, x, pltpu.roll(x, 64, 1))


def high_half(x):
    return jnp.where(iota(x.shape, 1) < 64, pltpu.roll(x, 64, 1), x)


def meta_tile(rate_row, geno_rows):
    eye = iota((8, 8), 0) == iota((8, 8), 1)
    lane = iota((8, 128), 1)

    def column(row):
        return jnp.sum(jnp.where(eye, jnp.broadcast_to(row, (8, 8)), 0.0), axis=1, keepdims=True)

    rate = column(rate_row)
    first = column(geno_rows[0:1].astype(F32))
    second = column(geno_rows[1:2].astype(F32))
    return jnp.where(lane == 0, rate, jnp.where(lane == 1, first, second))


def anchor_matrix():
    row = iota((128, 64), 0)
    col = iota((128, 64), 1)
    s = row
    t = row - 64
    upper = jnp.where((col >= s) & (col <= 31), 1.0, jnp.where((col >= 32) & (col < s), -1.0, 0.0))
    lower = jnp.where((col >= 32) & (col <= t), 1.0, jnp.where((col > t) & (col <= 31), -1.0, 0.0))
    return jnp.where(row < 64, upper, lower).astype(BF16)


def product(a, b):
    a_top, b_top = a.astype(BF16), b.astype(BF16)
    a_rest = (a - a_top.astype(F32)).astype(BF16)
    b_rest = (b - b_top.astype(F32)).astype(BF16)
    return dot_nt(a_top, b_top) + (dot_nt(a_rest, b_top) + dot_nt(a_top, b_rest))


def couplings(signs, genotype):
    width = signs.shape[1]
    sign = jnp.where(genotype == 2.0, 0.0, 2.0 * genotype - 1.0)
    steps = jnp.dot(anchor_matrix(), (signs * sign).astype(BF16), preferred_element_type=F32)
    from_s, to_t = steps[:64], steps[64:]
    u = jnp.exp(STEP * from_s)
    v = jnp.exp(STEP * to_t)
    full = jnp.log(product(u, jnp.concatenate([v, v], axis=0)))
    left, right = from_s[16:17], to_t[47:48]
    middle = left + right
    top = jnp.max(middle, axis=1, keepdims=True)
    begin = jnp.exp(STEP * (from_s[:16] - left + (middle - top)))
    end = jnp.exp(STEP * (to_t[48:] - right))
    blank = jnp.zeros((48, width), F32)
    corner = jnp.log(product(begin, jnp.concatenate([blank, end, blank, end], axis=0)))
    corner = corner + STEP * top
    return pack(full, corner)


def pack(full, corner):
    lane = iota((8, 128), 1)
    sub = iota((8, 128), 0)
    col = lane % 64
    rows = [full[8 * a : 8 * a + 8] for a in range(BLOCKS)]
    for a in range(2):
        rows[a] = jnp.where(col >= 48, corner[8 * a : 8 * a + 8], rows[a])
    diagonal = rows[0]
    for a in range(1, BLOCKS):
        diagonal = jnp.where(col // 8 == a, rows[a], diagonal)
    diagonal = jnp.where(col % 8 >= sub, diagonal, 0.0)
    pairs = []
    for a in range(4):
        other = rows[7 - a] if a == 0 else pltpu.roll(rows[7 - a], 8 * a, 1)
        pairs.append(
            jnp.where(col >= 8 * (a + 1), rows[a], jnp.where(col < 8 * a, other, 0.0))
        )
    first = jnp.where(lane < 64, pairs[0], pairs[1])
    second = jnp.where(lane < 64, pairs[2], pairs[3])
    halves = jnp.where(lane < 64, diagonal, pltpu.roll(diagonal, 4, 0))
    return jnp.concatenate([first, second, halves], axis=0)


def unpack(packed):
    first, second, halves = packed[0:8], packed[8:16], packed[16:24]
    diagonal = jnp.where(
        iota((8, 128), 0) < 4, low_half(halves), pltpu.roll(high_half(halves), 4, 0)
    )
    pairs = [low_half(first), high_half(first), low_half(second), high_half(second)]
    rows = [None] * BLOCKS
    for a in range(4):
        rows[a] = pairs[a]
        rows[7 - a] = pairs[a] if a == 0 else pltpu.roll(pairs[a], 128 - 8 * a, 1)
    col = iota((8, 128), 1) % 64
    return [jnp.where(col // 8 == a, diagonal, rows[a]) for a in range(BLOCKS)], diagonal


def log_total(items):
    top = functools.reduce(jnp.maximum, items)
    return top + jnp.log(functools.reduce(jnp.add, [jnp.exp(x - top) for x in items]))


def row_of(columns):
    col = iota((8, 128), 1) % 64
    sub = iota((8, 128), 0)
    total = None
    for a, column in enumerate(columns):
        part = jnp.where(col == 8 * a + sub, column, 0.0)
        total = part if total is None else total + part
    return jnp.sum(total, axis=0, keepdims=True)


def rate_terms(rates, log_k):
    lane = iota((8, 128), 1)
    col = lane % 64
    sub = iota((8, 128), 0)
    stay = [jnp.log(1.0 - r) for r in rates]
    stay_row = row_of(stay)
    sums = None
    for a in range(BLOCKS):
        part = jnp.where(8 * a + sub <= col, stay[a], 0.0)
        sums = part if sums is None else sums + part
    reach_row = jnp.sum(sums, axis=0, keepdims=True)
    reach_col = [
        jnp.sum(jnp.where((lane < 64) & (col <= 8 * a + sub), stay_row, 0.0), axis=1, keepdims=True)
        for a in range(BLOCKS)
    ]
    jump_col = [jnp.log(r) - log_k for r in rates]
    jump_row = row_of(jump_col)
    start = jnp.full((8, 1), -log_k, F32)
    jump_col[0] = jnp.where(iota((8, 1), 0) == 0, start, jump_col[0])
    return reach_row, reach_col, jump_row, jump_col


def solve(packed, terms, log_k):
    reach_row, reach_col, jump_row, jump_col = terms
    lane = iota((8, 128), 1)
    sub = iota((8, 128), 0)
    col = lane % 64
    block = col // 8
    within = col % 8
    rows, diagonal = unpack(packed)
    paths = [
        jnp.where(col >= 8 * a + sub, rows[a] + (reach_row - reach_col[a]), NEG)
        for a in range(BLOCKS)
    ]
    reach_diag = jnp.broadcast_to(reach_col[0], (8, 128))
    jump_diag = jnp.broadcast_to(jump_col[0], (8, 128))
    for a in range(1, BLOCKS):
        reach_diag = jnp.where(block == a, reach_col[a], reach_diag)
        jump_diag = jnp.where(block == a, jump_col[a], jump_diag)
    path_diag = diagonal + (reach_row - reach_diag)
    ahead = pltpu.roll(path_diag + jump_diag, 7, 0)
    behind = pltpu.roll(path_diag, 1, 1) + jump_row
    inner = jnp.exp(jnp.where(within > sub, jnp.where(lane < 64, ahead, behind), NEG))
    spread = jnp.concatenate(
        [jnp.where(lane % 8 == sub, inner[m : m + 1], 0.0) for m in range(8)], axis=0
    )
    same = (iota((128, 128), 0) // 8 == iota((128, 128), 1) // 8).astype(BF16)
    coarse = spread.astype(BF16)
    fine = (spread - coarse.astype(F32)).astype(BF16)
    columns = jnp.dot(coarse, same, preferred_element_type=F32)
    columns = columns + jnp.dot(fine, same, preferred_element_type=F32)
    inverse = jnp.where(within == sub, 1.0, 0.0)
    for m in range(7):
        inverse = inverse + columns[8 * m : 8 * m + 8] * inverse[m : m + 1]
    forward_inverse = jnp.where(lane < 64, inverse, 0.0)
    backward_inverse = high_half(inverse)

    offset = jnp.broadcast_to(paths[0][7:8], (8, 128))
    for a in range(1, BLOCKS):
        offset = jnp.where(sub == a, paths[a][7:8], offset)
    offset = jnp.where((within == 0) & (block > sub), offset, 0.0)
    for step in (1, 2, 4):
        offset = offset + pltpu.roll(offset, step, 1)
    factors = [jnp.exp(paths[a] - offset[a : a + 1]) for a in range(BLOCKS)]
    injectors = [jnp.exp(j) * f for j, f in zip(jump_col, factors)]
    row_lane = iota((1, 128), 1)
    row_col = row_lane % 64
    jumps_row = jnp.where(row_lane == 64, math.exp(-log_k), jnp.exp(jump_row))
    shifted = [pltpu.roll(f, 1, 1) * jumps_row for f in factors]
    shifted_offset = pltpu.roll(offset, 1, 1)
    inverses = [jnp.where(block == b, forward_inverse, 0.0) for b in range(BLOCKS)]

    zero = jnp.zeros((1, 128), F32)
    sums = []
    scales = [zero, zero]
    last = jnp.ones((1, 128), F32)
    spent = jnp.zeros((8, 128), F32)
    scale_col = jnp.zeros((8, 128), F32)
    newest = None

    back_scales = [zero, zero]
    back_scale_row = zero
    back_sums = zero
    behind_row = jnp.where(row_lane == 64, 1.0, 0.0)

    for b in range(BLOCKS):
        lead = last * injectors[b][0:1]
        if b > 1:
            weight = jnp.exp(offset + scale_col - scales[b])
            weight = jnp.where((sub < b - 1) & (block == b), weight, 0.0)
            lead = lead + jnp.sum(weight * spent, axis=0, keepdims=True)
        if b:
            weight = jnp.exp(offset[b - 1 : b] + (scales[b - 1] - scales[b]))
            weight = jnp.where(row_col // 8 == b, weight, 0.0)
            lead = lead + weight * newest
        here = jnp.sum(lead * inverses[b], axis=1, keepdims=True)
        here = jnp.broadcast_to(here, (8, 128))
        sums.append(here)
        if b < BLOCKS - 1:
            before = jnp.where(sub == 0, last, pltpu.roll(here, 1, 0))
            newest = jnp.sum(before * injectors[b], axis=0, keepdims=True)
            spent = jnp.where(sub == b, newest, spent)
            scale_col = jnp.where(sub == b, scales[b], scale_col)
            last = here[7:8] * jnp.exp(scales[b] - scales[b + 1])
            scales.append(jnp.log(here[7:8]) + scales[b])

        c = BLOCKS - 1 - b
        weight = jnp.exp(shifted_offset[c : c + 1] + (back_scale_row - back_scales[b]))
        weight = jnp.where((row_lane >= 8 * c + 8) & (row_lane <= 64), weight, 0.0)
        pulled = shifted[c] * weight
        lead = jnp.sum(pulled * behind_row, axis=1, keepdims=True)
        back = jnp.sum(lead * backward_inverse, axis=0, keepdims=True)
        inside = (row_lane >= 8 * c) & (row_lane < 8 * c + 8)
        back_sums = jnp.where(row_col // 8 == c, jnp.log(back) + back_scales[b], back_sums)
        if c:
            behind_row = jnp.where(inside, back, behind_row)
            back_scale_row = jnp.where(inside, back_scales[b], back_scale_row)
            first = jnp.sum(
                jnp.where(row_lane == 8 * c, back, 0.0), axis=1, keepdims=True
            )
            back_scales.append(jnp.log(first) + back_scales[b])

    scale_row = zero
    for b in range(BLOCKS):
        scale_row = jnp.where(row_col // 8 == b, scales[b], scale_row)
    forward_row = jnp.log(row_of(sums)) + scale_row
    return jnp.where(row_lane < 64, forward_row, back_sums)


def emission_terms(geno_row):
    g = geno_row
    base = jnp.where(g == 2.0, 1.0, jnp.where(g == 1.0, DOWN, UP))
    slope = jnp.where(g == 2.0, 0.0, jnp.where(g == 1.0, UP - DOWN, DOWN - UP))
    return base, slope


def state_terms(logs, rate_row, k):
    lane = iota((1, 128), 1)
    before = jnp.where(lane == 0, 0.0, pltpu.roll(logs, 1, 1))
    after = jnp.where(lane == 127, 0.0, pltpu.roll(logs, 127, 1))
    over_forward = jnp.exp(before - logs)
    over_backward = pltpu.roll(jnp.exp(after - logs), 64, 1)
    keep = 1.0 - rate_row
    jump = rate_row * (1.0 / k)
    rows = (keep * over_forward, jump * over_forward, keep * over_backward, jump)
    return [jnp.broadcast_to(row, (8, 128)) for row in rows]


def gather_sublanes(tiles):
    sub = iota((8, 128), 0)
    step = 4
    while len(tiles) > 1:
        half = len(tiles) // 2
        low = sub & step == 0
        merged = []
        for i in range(half):
            first, second = tiles[i], tiles[i + half]
            kept = jnp.where(low, first, second)
            moved = jnp.where(low, second, first)
            merged.append(kept + pltpu.roll(moved, step, 0) if step == 4 else kept + swap_by(moved, step))
        tiles = merged
        step //= 2
    return tiles[0]


def swap_by(x, step):
    low = iota((8, 128), 0) & step == 0
    return jnp.where(low, pltpu.roll(x, 8 - step, 0), pltpu.roll(x, step, 0))


def far_first(n):
    return sorted(range(1, n), key=lambda d: -min(d, n - d))


def kernel(
    n_y, n_z, k,
    panel_ref, rate_ref, geno_ref,
    out_ref,
    rate_own, geno_own, panel_own, panel_all, meta_all, tiles, emis, fwd, bwd,
    log_send, log_plane, log_mid, log_z, log_last,
    solve_send, solve_recv, sum_send, sum_all, dose_send, dose_recv,
    load_sem, own_sem, tile_sem, known,
    panel_s, panel_r, meta_s, meta_r, plane_s, plane_r, z_s, z_r,
    core_s, core_r, all_s, all_r, dose_s, dose_r,
):
    n_group = BLOCKS
    n_x = n_group // 2
    group = lax.axis_index("group")
    batch = lax.axis_index("batch")
    core = group % 2
    x = group // 2
    y = batch % n_y
    z = batch // n_y
    partner = (group + 1 - 2 * core, batch)
    width = panel_all.shape[2]
    log_k = math.log(k)

    def in_group(d):
        return (group + d) % n_group

    def group_peer(d):
        return (in_group(d), batch)

    def y_peer(d):
        return (group, z * n_y + (y + d) % n_y)

    def z_peer(d):
        return (group, ((z + d) % n_z) * n_y + y)

    def plane_peer(dx, dy):
        return (((x + dx) % n_x) * 2 + core, z * n_y + (y + dy) % n_y)

    def remote(src, dst, send, recv, peer):
        return pltpu.make_async_remote_copy(
            src_ref=src, dst_ref=dst, send_sem=send, recv_sem=recv,
            device_id=peer, device_id_type=MESH,
        )

    def finish(copies):
        for copy in copies:
            copy.wait()

    def hear(near, turn):
        for peer in near:
            pl.semaphore_signal(known.at[turn], inc=1, device_id=peer, device_id_type=MESH)
        if near:
            pl.semaphore_wait(known.at[turn], len(near))

    loads = [
        pltpu.make_async_copy(rate_ref, rate_own, load_sem.at[0]),
        pltpu.make_async_copy(geno_ref, geno_own, load_sem.at[1]),
        pltpu.make_async_copy(panel_ref, panel_own, load_sem.at[2]),
    ]
    own = pltpu.make_async_copy(
        panel_ref.at[:, pl.ds(pl.multiple_of(x * width, width), width)],
        panel_all.at[group],
        own_sem,
    )
    for load in loads:
        load.start()
    own.start()
    barrier = pltpu.get_barrier_semaphore()
    near_y = [y_peer(d) for d in sorted({1, n_y - 1}) if 0 < d < n_y]
    near_z = [z_peer(d) for d in sorted({1, n_z - 1}) if 0 < d < n_z]
    peers = [group_peer(d) for d in far_first(n_group)] + near_y + near_z
    for peer in peers:
        pl.semaphore_signal(barrier, inc=1, device_id=peer, device_id_type=MESH)
    finish(loads)
    meta_all[group] = meta_tile(rate_own[...], geno_own[...])
    pl.semaphore_wait(barrier, len(peers))

    copies = []
    for d in far_first(n_group):
        start = pl.multiple_of(in_group(d) // 2 * width, width)
        copies.append(
            remote(
                panel_own.at[:, pl.ds(start, width)], panel_all.at[group],
                panel_s, panel_r, group_peer(d),
            )
        )
    for d in far_first(n_group):
        copies.append(
            remote(
                meta_all.at[group], meta_all.at[group],
                meta_s, meta_r, group_peer(d),
            )
        )
    for copy in copies:
        copy.start()
    hear(near_y + near_z, 0)
    hear(near_y + near_z, 1)
    hear(near_z, 2)
    own.wait()
    most = pl.ds(0, n_group - 1)
    remote(meta_all.at[most], meta_all.at[most], meta_s, meta_r, partner).wait()
    remote(panel_all.at[most], panel_all.at[most], panel_s, panel_r, partner).wait()

    relayout = []
    for c in range(8):
        copy = pltpu.make_async_copy(
            panel_all.at[:, :, pl.ds(128 * c, 128)], tiles.at[:, :, c], tile_sem.at[c]
        )
        copy.start()
        relayout.append(copy)

    meta = meta_all[...].reshape(MARKERS, 128)
    signs = 2.0 * panel_all[...].reshape(MARKERS, width).astype(F32) - 1.0
    genotype = jnp.where(core == 0, meta[:, 1:2], meta[:, 2:3])
    log_send[...] = couplings(signs, genotype)
    sent = pl.ds(0, 20)

    plane = [(dx, dy) for dx in range(n_x) for dy in range(n_y) if dx or dy]
    plane.sort(key=lambda p: -(min(p[0], n_x - p[0]) + min(p[1], n_y - p[1])))
    flying = [
        remote(
            log_send.at[sent], log_plane.at[i], plane_s, plane_r, plane_peer(dx, dy)
        )
        for i, (dx, dy) in enumerate(plane)
    ]
    for copy in flying:
        copy.start()
    rates = [meta[8 * a : 8 * a + 8, 0:1] for a in range(BLOCKS)]
    terms = rate_terms(rates, log_k)
    rate_row = row_of(rates)
    geno_row = row_of([genotype[8 * a : 8 * a + 8] for a in range(BLOCKS)])
    base, slope = emission_terms(geno_row)
    log_mid[...] = jnp.zeros((24, 128), F32)
    log_last[...] = jnp.zeros((24, 128), F32)
    remote(log_plane, log_plane, plane_s, plane_r, partner).wait()
    total = log_total([log_send[0:20]] + [log_plane[i] for i in range(len(plane))])
    log_mid[0:20] = total

    flying = [
        remote(log_mid.at[sent], log_z.at[d - 1], z_s, z_r, z_peer(d))
        for d in far_first(n_z)
    ]
    for copy in flying:
        copy.start()
    finish(relayout)
    for t in range(MARKERS):
        allele = tiles[t // 8, t % 8].astype(F32)
        emis[t] = base[:, t : t + 1] + slope[:, t : t + 1] * allele
    if n_z > 1:
        remote(log_z, log_z, z_s, z_r, partner).wait()
    log_last[0:20] = log_total([total] + [log_z[d] for d in range(n_z - 1)])

    solved = solve(log_last[...], terms, log_k)

    lane_row = iota((1, 128), 1)
    seen = jnp.sum(
        jnp.where((lane_row < 64) & (geno_row != 2.0), LOG_CENTRE, 0.0), axis=1, keepdims=True
    )
    like = jnp.broadcast_to((solved[:, 63:64] + seen) * (1.0 / MARKERS), (1, 128))
    solve_send[...] = like
    swap = remote(solve_send, solve_recv, core_s, core_r, partner)
    swap.start()

    keep_f, jump_f, keep_b, jump_b = state_terms(solved, rate_row, float(k))
    ahead = jnp.full((8, 128), 1.0 / k, F32)
    behind = jnp.full((8, 128), 1.0 / k, F32)
    for i in range(MARKERS):
        kept, added = emis[i] * keep_f[:, i : i + 1], emis[i] * jump_f[:, i : i + 1]
        ahead = kept * ahead + added
        fwd[i] = ahead
        t = MARKERS - 1 - i
        bwd[t] = behind
        behind = (keep_b[:, t : t + 1] * emis[t]) * behind + jump_b[:, t : t + 1]

    over_k = []
    for which in range(2):
        for a in range(BLOCKS):
            both = fwd[8 * a : 8 * a + 8] * bwd[8 * a : 8 * a + 8]
            if which == 0:
                both = both * tiles[a].astype(F32)
            over_k.append(gather_sublanes([both[i] for i in range(8)]))
    stacked = jnp.concatenate(over_k, axis=0)
    ones = jnp.ones((8, 128), BF16)
    coarse = stacked.astype(BF16)
    fine = (stacked - coarse.astype(F32)).astype(BF16)
    total = (dot_nt(ones, coarse) + dot_nt(ones, fine))[0:1]

    everyone = [
        (dx, dy, dz) for dx in range(n_x) for dy in range(n_y) for dz in range(n_z)
        if dx or dy or dz
    ]
    everyone.sort(
        key=lambda p: -(min(p[0], n_x - p[0]) + min(p[1], n_y - p[1]) + min(p[2], n_z - p[2]))
    )
    others = len(everyone)
    sum_send[...] = total
    for i, (dx, dy, dz) in enumerate(everyone):
        peer = (
            ((x + dx) % n_x) * 2 + core,
            ((z + dz) % n_z) * n_y + (y + dy) % n_y,
        )
        remote(sum_send, sum_all.at[pl.ds(i, 1)], all_s, all_r, peer).start()
    sum_all[others : others + 1] = total
    swap.wait()
    other = solve_recv[...]
    out_ref[2:3, 0:2] = jnp.where(
        lane_row == 0, jnp.where(core == 0, like, other), jnp.where(core == 0, other, like)
    )[:, 0:2]
    rest = pl.ds(0, others)
    remote(sum_all.at[rest], sum_all.at[rest], all_s, all_r, partner).wait()
    total = jnp.sum(sum_all[...], axis=0, keepdims=True)
    share = total / pltpu.roll(total, 64, 1)
    dose_send[...] = share
    trade = remote(dose_send, dose_recv, dose_s, dose_r, partner)
    trade.start()
    shift = (128 - 8 * group) % 128
    mine = pltpu.roll(share, shift, 1)
    trade.wait()
    theirs = pltpu.roll(dose_recv[...], shift, 1)
    out_ref[0:1, 0:8] = jnp.where(core == 0, mine, theirs)[:, 0:8]
    out_ref[1:2, 0:8] = jnp.where(core == 0, theirs, mine)[:, 0:8]


def hand_over(out_ref, dosage_ref, like_ref):
    dosage_ref[...] = out_ref[0:2, 0:8]
    like_ref[...] = out_ref[2:3, 0:2]


def on_device(n_y, panel, rates, genotypes):
    n_batch = lax.axis_size("batch")
    n_group = lax.axis_size("group")
    n_z = n_batch // n_y
    held = panel.shape[1]
    width = held // (n_group // 2)
    k = held * n_batch
    dma = pltpu.SemaphoreType.DMA
    vmem = pltpu.VMEM
    g1, z1, p1 = n_group - 1, max(n_z - 1, 1), n_group // 2 * n_y - 1
    scratch = [
        vmem((1, BLOCK), F32),
        vmem((2, BLOCK), jnp.int32),
        vmem((BLOCK, held), jnp.int32),
        vmem((BLOCKS, BLOCK, width), jnp.int32),
        vmem((BLOCKS, BLOCK, 128), F32),
        vmem((BLOCKS, BLOCK, 8, 128), jnp.int32),
        vmem((MARKERS, 8, 128), F32),
        vmem((MARKERS, 8, 128), F32),
        vmem((MARKERS, 8, 128), F32),
        vmem((24, 128), F32),
        vmem((p1, 20, 128), F32),
        vmem((24, 128), F32),
        vmem((z1, 20, 128), F32),
        vmem((24, 128), F32),
        vmem((1, 128), F32),
        vmem((1, 128), F32),
        vmem((1, 128), F32),
        vmem((n_group // 2 * n_batch, 128), F32),
        vmem((1, 128), F32),
        vmem((1, 128), F32),
        dma((3,)),
        dma,
        dma((8,)),
        pltpu.SemaphoreType.REGULAR((3,)),
        dma, dma, dma, dma, dma, dma,
        dma, dma,
        dma, dma,
        dma, dma, dma, dma,
    ]
    out = pl.pallas_call(
        functools.partial(kernel, n_y, n_z, k),
        out_shape=pltpu.VMEM((8, 128), F32),
        in_specs=[
            pl.BlockSpec(memory_space=pl.ANY),
            pl.BlockSpec(memory_space=pl.ANY),
            pl.BlockSpec(memory_space=pl.ANY),
        ],
        out_specs=pl.BlockSpec(memory_space=pltpu.VMEM),
        scratch_shapes=scratch,
        compiler_params=pltpu.CompilerParams(collective_id=0, has_side_effects=True),
    )(panel, rates.reshape(1, BLOCK), genotypes)
    dosage, like = pl.pallas_call(
        hand_over,
        out_shape=(
            jax.ShapeDtypeStruct((2, BLOCK), F32),
            jax.ShapeDtypeStruct((1, 2), F32),
        ),
    )(pltpu.with_memory_space_constraint(out, pltpu.VMEM))
    return dosage, like.reshape(2)


def solution(mesh, n_y=4):
    placed = (P("group", "batch"), P("group"), P(None, "group"))
    return jax.shard_map(
        functools.partial(on_device, n_y),
        mesh=mesh,
        in_specs=placed,
        out_specs=(P(None, "group"), P()),
        check_vma=False,
    )
```

```python
import functools
import math

import jax
import jax.numpy as jnp
from jax import lax
from jax.experimental import pallas as pl
from jax.experimental.pallas import tpu as pltpu
from jax.sharding import PartitionSpec as P

HIGHEST = lax.Precision.HIGHEST
MESH = pl.DeviceIdType.MESH

MISMATCH = 0.05
STEP = 0.5 * math.log((1.0 - MISMATCH) / MISMATCH)
LOG_CENTRE = 0.5 * math.log((1.0 - MISMATCH) * MISMATCH)
UP = math.exp(STEP)
DOWN = math.exp(-STEP)
NEG = -1e30
F32 = jnp.float32
BF16 = jnp.bfloat16

MARKERS = 64
BLOCK = 8
BLOCKS = 8


def iota(shape, axis):
    return lax.broadcasted_iota(jnp.int32, shape, axis)


def dot_nt(a, b, precision=None):
    return lax.dot_general(
        a, b, (((1,), (1,)), ((), ())), precision=precision, preferred_element_type=F32
    )


def low_half(x):
    return jnp.where(iota(x.shape, 1) < 64, x, pltpu.roll(x, 64, 1))


def high_half(x):
    return jnp.where(iota(x.shape, 1) < 64, pltpu.roll(x, 64, 1), x)


def meta_tile(rate_row, geno_rows):
    eye = iota((8, 8), 0) == iota((8, 8), 1)
    lane = iota((8, 128), 1)

    def column(row):
        return jnp.sum(jnp.where(eye, jnp.broadcast_to(row, (8, 8)), 0.0), axis=1, keepdims=True)

    rate = column(rate_row)
    first = column(geno_rows[0:1].astype(F32))
    second = column(geno_rows[1:2].astype(F32))
    return jnp.where(lane == 0, rate, jnp.where(lane == 1, first, second))


def anchor_matrix():
    row = iota((128, 64), 0)
    col = iota((128, 64), 1)
    s = row
    t = row - 64
    upper = jnp.where((col >= s) & (col <= 31), 1.0, jnp.where((col >= 32) & (col < s), -1.0, 0.0))
    lower = jnp.where((col >= 32) & (col <= t), 1.0, jnp.where((col > t) & (col <= 31), -1.0, 0.0))
    return jnp.where(row < 64, upper, lower).astype(BF16)


def product(a, b):
    a_top, b_top = a.astype(BF16), b.astype(BF16)
    a_rest = (a - a_top.astype(F32)).astype(BF16)
    b_rest = (b - b_top.astype(F32)).astype(BF16)
    return dot_nt(a_top, b_top) + (dot_nt(a_rest, b_top) + dot_nt(a_top, b_rest))


def couplings(signs, genotype):
    width = signs.shape[1]
    sign = jnp.where(genotype == 2.0, 0.0, 2.0 * genotype - 1.0)
    steps = jnp.dot(anchor_matrix(), (signs * sign).astype(BF16), preferred_element_type=F32)
    from_s, to_t = steps[:64], steps[64:]
    u = jnp.exp(STEP * from_s)
    v = jnp.exp(STEP * to_t)
    full = jnp.log(product(u, jnp.concatenate([v, v], axis=0)))
    left, right = from_s[16:17], to_t[47:48]
    middle = left + right
    top = jnp.max(middle, axis=1, keepdims=True)
    begin = jnp.exp(STEP * (from_s[:16] - left + (middle - top)))
    end = jnp.exp(STEP * (to_t[48:] - right))
    blank = jnp.zeros((48, width), F32)
    corner = jnp.log(product(begin, jnp.concatenate([blank, end, blank, end], axis=0)))
    corner = corner + STEP * top
    return pack(full, corner)


def pack(full, corner):
    lane = iota((8, 128), 1)
    sub = iota((8, 128), 0)
    col = lane % 64
    rows = [full[8 * a : 8 * a + 8] for a in range(BLOCKS)]
    for a in range(2):
        rows[a] = jnp.where(col >= 48, corner[8 * a : 8 * a + 8], rows[a])
    diagonal = rows[0]
    for a in range(1, BLOCKS):
        diagonal = jnp.where(col // 8 == a, rows[a], diagonal)
    diagonal = jnp.where(col % 8 >= sub, diagonal, 0.0)
    pairs = []
    for a in range(4):
        other = rows[7 - a] if a == 0 else pltpu.roll(rows[7 - a], 8 * a, 1)
        pairs.append(
            jnp.where(col >= 8 * (a + 1), rows[a], jnp.where(col < 8 * a, other, 0.0))
        )
    first = jnp.where(lane < 64, pairs[0], pairs[1])
    second = jnp.where(lane < 64, pairs[2], pairs[3])
    halves = jnp.where(lane < 64, diagonal, pltpu.roll(diagonal, 4, 0))
    return jnp.concatenate([first, second, halves], axis=0)


def unpack(packed):
    first, second, halves = packed[0:8], packed[8:16], packed[16:24]
    diagonal = jnp.where(
        iota((8, 128), 0) < 4, low_half(halves), pltpu.roll(high_half(halves), 4, 0)
    )
    pairs = [low_half(first), high_half(first), low_half(second), high_half(second)]
    rows = [None] * BLOCKS
    for a in range(4):
        rows[a] = pairs[a]
        rows[7 - a] = pairs[a] if a == 0 else pltpu.roll(pairs[a], 128 - 8 * a, 1)
    col = iota((8, 128), 1) % 64
    return [jnp.where(col // 8 == a, diagonal, rows[a]) for a in range(BLOCKS)], diagonal


def log_total(items):
    top = functools.reduce(jnp.maximum, items)
    return top + jnp.log(functools.reduce(jnp.add, [jnp.exp(x - top) for x in items]))


def row_of(columns):
    col = iota((8, 128), 1) % 64
    sub = iota((8, 128), 0)
    total = None
    for a, column in enumerate(columns):
        part = jnp.where(col == 8 * a + sub, column, 0.0)
        total = part if total is None else total + part
    return jnp.sum(total, axis=0, keepdims=True)


def rate_terms(rates, log_k):
    lane = iota((8, 128), 1)
    col = lane % 64
    sub = iota((8, 128), 0)
    stay = [jnp.log(1.0 - r) for r in rates]
    stay_row = row_of(stay)
    sums = None
    for a in range(BLOCKS):
        part = jnp.where(8 * a + sub <= col, stay[a], 0.0)
        sums = part if sums is None else sums + part
    reach_row = jnp.sum(sums, axis=0, keepdims=True)
    reach_col = [
        jnp.sum(jnp.where((lane < 64) & (col <= 8 * a + sub), stay_row, 0.0), axis=1, keepdims=True)
        for a in range(BLOCKS)
    ]
    jump_col = [jnp.log(r) - log_k for r in rates]
    jump_row = row_of(jump_col)
    start = jnp.full((8, 1), -log_k, F32)
    jump_col[0] = jnp.where(iota((8, 1), 0) == 0, start, jump_col[0])
    return reach_row, reach_col, jump_row, jump_col


def solve(packed, terms, log_k):
    reach_row, reach_col, jump_row, jump_col = terms
    lane = iota((8, 128), 1)
    sub = iota((8, 128), 0)
    col = lane % 64
    block = col // 8
    within = col % 8
    rows, diagonal = unpack(packed)
    paths = [
        jnp.where(col >= 8 * a + sub, rows[a] + (reach_row - reach_col[a]), NEG)
        for a in range(BLOCKS)
    ]
    reach_diag = jnp.broadcast_to(reach_col[0], (8, 128))
    jump_diag = jnp.broadcast_to(jump_col[0], (8, 128))
    for a in range(1, BLOCKS):
        reach_diag = jnp.where(block == a, reach_col[a], reach_diag)
        jump_diag = jnp.where(block == a, jump_col[a], jump_diag)
    path_diag = diagonal + (reach_row - reach_diag)
    ahead = pltpu.roll(path_diag + jump_diag, 7, 0)
    behind = pltpu.roll(path_diag, 1, 1) + jump_row
    inner = jnp.exp(jnp.where(within > sub, jnp.where(lane < 64, ahead, behind), NEG))
    spread = jnp.concatenate(
        [jnp.where(lane % 8 == sub, inner[m : m + 1], 0.0) for m in range(8)], axis=0
    )
    same = (iota((128, 128), 0) // 8 == iota((128, 128), 1) // 8).astype(BF16)
    coarse = spread.astype(BF16)
    fine = (spread - coarse.astype(F32)).astype(BF16)
    columns = jnp.dot(coarse, same, preferred_element_type=F32)
    columns = columns + jnp.dot(fine, same, preferred_element_type=F32)
    inverse = jnp.where(within == sub, 1.0, 0.0)
    for m in range(7):
        inverse = inverse + columns[8 * m : 8 * m + 8] * inverse[m : m + 1]
    forward_inverse = jnp.where(lane < 64, inverse, 0.0)
    backward_inverse = high_half(inverse)

    offset = jnp.broadcast_to(paths[0][7:8], (8, 128))
    for a in range(1, BLOCKS):
        offset = jnp.where(sub == a, paths[a][7:8], offset)
    offset = jnp.where((within == 0) & (block > sub), offset, 0.0)
    for step in (1, 2, 4):
        offset = offset + pltpu.roll(offset, step, 1)
    factors = [jnp.exp(paths[a] - offset[a : a + 1]) for a in range(BLOCKS)]
    injectors = [jnp.exp(j) * f for j, f in zip(jump_col, factors)]
    row_lane = iota((1, 128), 1)
    row_col = row_lane % 64
    jumps_row = jnp.where(row_lane == 64, math.exp(-log_k), jnp.exp(jump_row))
    shifted = [pltpu.roll(f, 1, 1) * jumps_row for f in factors]
    shifted_offset = pltpu.roll(offset, 1, 1)
    inverses = [jnp.where(block == b, forward_inverse, 0.0) for b in range(BLOCKS)]

    zero = jnp.zeros((1, 128), F32)
    sums = []
    scales = [zero, zero]
    last = jnp.ones((1, 128), F32)
    spent = jnp.zeros((8, 128), F32)
    scale_col = jnp.zeros((8, 128), F32)
    newest = None

    back_scales = [zero, zero]
    back_scale_row = zero
    back_sums = zero
    behind_row = jnp.where(row_lane == 64, 1.0, 0.0)

    for b in range(BLOCKS):
        lead = last * injectors[b][0:1]
        if b > 1:
            weight = jnp.exp(offset + scale_col - scales[b])
            weight = jnp.where((sub < b - 1) & (block == b), weight, 0.0)
            lead = lead + jnp.sum(weight * spent, axis=0, keepdims=True)
        if b:
            weight = jnp.exp(offset[b - 1 : b] + (scales[b - 1] - scales[b]))
            weight = jnp.where(row_col // 8 == b, weight, 0.0)
            lead = lead + weight * newest
        here = jnp.sum(lead * inverses[b], axis=1, keepdims=True)
        here = jnp.broadcast_to(here, (8, 128))
        sums.append(here)
        if b < BLOCKS - 1:
            before = jnp.where(sub == 0, last, pltpu.roll(here, 1, 0))
            newest = jnp.sum(before * injectors[b], axis=0, keepdims=True)
            spent = jnp.where(sub == b, newest, spent)
            scale_col = jnp.where(sub == b, scales[b], scale_col)
            last = here[7:8] * jnp.exp(scales[b] - scales[b + 1])
            scales.append(jnp.log(here[7:8]) + scales[b])

        c = BLOCKS - 1 - b
        weight = jnp.exp(shifted_offset[c : c + 1] + (back_scale_row - back_scales[b]))
        weight = jnp.where((row_lane >= 8 * c + 8) & (row_lane <= 64), weight, 0.0)
        pulled = shifted[c] * weight
        lead = jnp.sum(pulled * behind_row, axis=1, keepdims=True)
        back = jnp.sum(lead * backward_inverse, axis=0, keepdims=True)
        inside = (row_lane >= 8 * c) & (row_lane < 8 * c + 8)
        back_sums = jnp.where(row_col // 8 == c, jnp.log(back) + back_scales[b], back_sums)
        if c:
            behind_row = jnp.where(inside, back, behind_row)
            back_scale_row = jnp.where(inside, back_scales[b], back_scale_row)
            first = jnp.sum(
                jnp.where(row_lane == 8 * c, back, 0.0), axis=1, keepdims=True
            )
            back_scales.append(jnp.log(first) + back_scales[b])

    scale_row = zero
    for b in range(BLOCKS):
        scale_row = jnp.where(row_col // 8 == b, scales[b], scale_row)
    forward_row = jnp.log(row_of(sums)) + scale_row
    return jnp.where(row_lane < 64, forward_row, back_sums)


def emission_terms(geno_row):
    g = geno_row
    base = jnp.where(g == 2.0, 1.0, jnp.where(g == 1.0, DOWN, UP))
    slope = jnp.where(g == 2.0, 0.0, jnp.where(g == 1.0, UP - DOWN, DOWN - UP))
    return base, slope


def state_terms(logs, rate_row, k):
    lane = iota((1, 128), 1)
    before = jnp.where(lane == 0, 0.0, pltpu.roll(logs, 1, 1))
    after = jnp.where(lane == 127, 0.0, pltpu.roll(logs, 127, 1))
    over_forward = jnp.exp(before - logs)
    over_backward = pltpu.roll(jnp.exp(after - logs), 64, 1)
    keep = 1.0 - rate_row
    jump = rate_row * (1.0 / k)
    rows = (keep * over_forward, jump * over_forward, keep * over_backward, jump)
    return [jnp.broadcast_to(row, (8, 128)) for row in rows]


def gather_sublanes(tiles):
    sub = iota((8, 128), 0)
    step = 4
    while len(tiles) > 1:
        half = len(tiles) // 2
        low = sub & step == 0
        merged = []
        for i in range(half):
            first, second = tiles[i], tiles[i + half]
            kept = jnp.where(low, first, second)
            moved = jnp.where(low, second, first)
            merged.append(kept + pltpu.roll(moved, step, 0) if step == 4 else kept + swap_by(moved, step))
        tiles = merged
        step //= 2
    return tiles[0]


def swap_by(x, step):
    low = iota((8, 128), 0) & step == 0
    return jnp.where(low, pltpu.roll(x, 8 - step, 0), pltpu.roll(x, step, 0))


def far_first(n):
    return sorted(range(1, n), key=lambda d: -min(d, n - d))


def kernel(
    n_y, n_z, k,
    panel_ref, rate_ref, geno_ref,
    out_ref,
    rate_own, geno_own, panel_own, panel_all, meta_all, tiles, emis, fwd, bwd,
    log_send, log_plane, log_mid, log_z, log_last,
    solve_send, solve_recv, sum_send, sum_all,
    load_sem, own_sem, tile_sem, known,
    panel_s, panel_r, meta_s, meta_r, plane_s, plane_r, z_s, z_r,
    core_s, core_r, all_s, all_r,
):
    n_group = BLOCKS
    n_x = n_group // 2
    group = lax.axis_index("group")
    batch = lax.axis_index("batch")
    core = group % 2
    x = group // 2
    y = batch % n_y
    z = batch // n_y
    partner = (group + 1 - 2 * core, batch)
    width = panel_all.shape[2]
    log_k = math.log(k)

    def in_group(d):
        return (group + d) % n_group

    def group_peer(d):
        return (in_group(d), batch)

    def y_peer(d):
        return (group, z * n_y + (y + d) % n_y)

    def z_peer(d):
        return (group, ((z + d) % n_z) * n_y + y)

    def plane_peer(dx, dy):
        return (((x + dx) % n_x) * 2 + core, z * n_y + (y + dy) % n_y)

    def remote(src, dst, send, recv, peer):
        return pltpu.make_async_remote_copy(
            src_ref=src, dst_ref=dst, send_sem=send, recv_sem=recv,
            device_id=peer, device_id_type=MESH,
        )

    def finish(copies):
        for copy in copies:
            copy.wait()

    def hear(near, turn):
        for peer in near:
            pl.semaphore_signal(known.at[turn], inc=1, device_id=peer, device_id_type=MESH)
        if near:
            pl.semaphore_wait(known.at[turn], len(near))

    loads = [
        pltpu.make_async_copy(rate_ref, rate_own, load_sem.at[0]),
        pltpu.make_async_copy(geno_ref, geno_own, load_sem.at[1]),
        pltpu.make_async_copy(panel_ref, panel_own, load_sem.at[2]),
    ]
    own = pltpu.make_async_copy(
        panel_ref.at[:, pl.ds(pl.multiple_of(x * width, width), width)],
        panel_all.at[group],
        own_sem,
    )
    for load in loads:
        load.start()
    own.start()
    barrier = pltpu.get_barrier_semaphore()
    near_y = [y_peer(d) for d in sorted({1, n_y - 1}) if 0 < d < n_y]
    near_z = [z_peer(d) for d in sorted({1, n_z - 1}) if 0 < d < n_z]
    peers = [group_peer(d) for d in far_first(n_group)] + near_y + near_z
    for peer in peers:
        pl.semaphore_signal(barrier, inc=1, device_id=peer, device_id_type=MESH)
    finish(loads)
    meta_all[group] = meta_tile(rate_own[...], geno_own[...])
    pl.semaphore_wait(barrier, len(peers))

    copies = []
    for d in far_first(n_group):
        start = pl.multiple_of(in_group(d) // 2 * width, width)
        copies.append(
            remote(
                panel_own.at[:, pl.ds(start, width)], panel_all.at[group],
                panel_s, panel_r, group_peer(d),
            )
        )
    for d in far_first(n_group):
        copies.append(
            remote(
                meta_all.at[group], meta_all.at[group],
                meta_s, meta_r, group_peer(d),
            )
        )
    for copy in copies:
        copy.start()
    hear(near_y + near_z, 0)
    hear(near_y + near_z, 1)
    hear(near_z, 2)
    own.wait()
    most = pl.ds(0, n_group - 1)
    remote(meta_all.at[most], meta_all.at[most], meta_s, meta_r, partner).wait()
    remote(panel_all.at[most], panel_all.at[most], panel_s, panel_r, partner).wait()

    relayout = []
    for c in range(8):
        copy = pltpu.make_async_copy(
            panel_all.at[:, :, pl.ds(128 * c, 128)], tiles.at[:, :, c], tile_sem.at[c]
        )
        copy.start()
        relayout.append(copy)

    meta = meta_all[...].reshape(MARKERS, 128)
    signs = 2.0 * panel_all[...].reshape(MARKERS, width).astype(F32) - 1.0
    genotype = jnp.where(core == 0, meta[:, 1:2], meta[:, 2:3])
    log_send[...] = couplings(signs, genotype)
    sent = pl.ds(0, 20)

    plane = [(dx, dy) for dx in range(n_x) for dy in range(n_y) if dx or dy]
    plane.sort(key=lambda p: -(min(p[0], n_x - p[0]) + min(p[1], n_y - p[1])))
    flying = [
        remote(
            log_send.at[sent], log_plane.at[i], plane_s, plane_r, plane_peer(dx, dy)
        )
        for i, (dx, dy) in enumerate(plane)
    ]
    for copy in flying:
        copy.start()
    rates = [meta[8 * a : 8 * a + 8, 0:1] for a in range(BLOCKS)]
    terms = rate_terms(rates, log_k)
    rate_row = row_of(rates)
    geno_row = row_of([genotype[8 * a : 8 * a + 8] for a in range(BLOCKS)])
    base, slope = emission_terms(geno_row)
    log_mid[...] = jnp.zeros((24, 128), F32)
    log_last[...] = jnp.zeros((24, 128), F32)
    remote(log_plane, log_plane, plane_s, plane_r, partner).wait()
    total = log_total([log_send[0:20]] + [log_plane[i] for i in range(len(plane))])
    log_mid[0:20] = total

    flying = [
        remote(log_mid.at[sent], log_z.at[d - 1], z_s, z_r, z_peer(d))
        for d in far_first(n_z)
    ]
    for copy in flying:
        copy.start()
    finish(relayout)
    for t in range(MARKERS):
        allele = tiles[t // 8, t % 8].astype(F32)
        emis[t] = base[:, t : t + 1] + slope[:, t : t + 1] * allele
    if n_z > 1:
        remote(log_z, log_z, z_s, z_r, partner).wait()
    log_last[0:20] = log_total([total] + [log_z[d] for d in range(n_z - 1)])

    solved = solve(log_last[...], terms, log_k)

    lane_row = iota((1, 128), 1)
    seen = jnp.sum(
        jnp.where((lane_row < 64) & (geno_row != 2.0), LOG_CENTRE, 0.0), axis=1, keepdims=True
    )
    like = jnp.broadcast_to((solved[:, 63:64] + seen) * (1.0 / MARKERS), (1, 128))
    solve_send[...] = like
    swap = remote(solve_send, solve_recv, core_s, core_r, partner)
    swap.start()

    keep_f, jump_f, keep_b, jump_b = state_terms(solved, rate_row, float(k))
    ahead = jnp.full((8, 128), 1.0 / k, F32)
    behind = jnp.full((8, 128), 1.0 / k, F32)
    for i in range(MARKERS):
        kept, added = emis[i] * keep_f[:, i : i + 1], emis[i] * jump_f[:, i : i + 1]
        ahead = kept * ahead + added
        fwd[i] = ahead
        t = MARKERS - 1 - i
        bwd[t] = behind
        behind = (keep_b[:, t : t + 1] * emis[t]) * behind + jump_b[:, t : t + 1]

    over_k = []
    for which in range(2):
        for a in range(BLOCKS):
            both = fwd[8 * a : 8 * a + 8] * bwd[8 * a : 8 * a + 8]
            if which == 0:
                both = both * tiles[a].astype(F32)
            over_k.append(gather_sublanes([both[i] for i in range(8)]))
    stacked = jnp.concatenate(over_k, axis=0)
    ones = jnp.ones((8, 128), BF16)
    coarse = stacked.astype(BF16)
    fine = (stacked - coarse.astype(F32)).astype(BF16)
    total = (dot_nt(ones, coarse) + dot_nt(ones, fine))[0:1]

    everyone = [
        (dx, dy, dz, dc) for dx in range(n_x) for dy in range(n_y) for dz in range(n_z)
        for dc in range(2) if dx or dy or dz or dc
    ]
    everyone.sort(
        key=lambda p: -(min(p[0], n_x - p[0]) + min(p[1], n_y - p[1]) + min(p[2], n_z - p[2]))
    )
    others = len(everyone)
    half = (others + 1) // 2
    sum_send[...] = total
    places = [1, half]
    for dx, dy, dz, dc in everyone:
        peer = (
            ((x + dx) % n_x) * 2 + (core + dc) % 2,
            ((z + dz) % n_z) * n_y + (y + dy) % n_y,
        )
        remote(sum_send, sum_all.at[pl.ds(places[dc], 1)], all_s, all_r, peer).start()
        places[dc] += 1
    sum_all[0:1] = total
    swap.wait()
    other = solve_recv[...]
    out_ref[2:3, 0:2] = jnp.where(
        lane_row == 0, jnp.where(core == 0, like, other), jnp.where(core == 0, other, like)
    )[:, 0:2]
    rest = pl.ds(1, others)
    remote(sum_all.at[rest], sum_all.at[rest], all_s, all_r, partner).wait()
    mine = jnp.sum(sum_all[0:half], axis=0, keepdims=True)
    theirs = jnp.sum(sum_all[half:], axis=0, keepdims=True)
    shift = (128 - 8 * group) % 128
    mine = pltpu.roll(mine / pltpu.roll(mine, 64, 1), shift, 1)
    theirs = pltpu.roll(theirs / pltpu.roll(theirs, 64, 1), shift, 1)
    out_ref[0:1, 0:8] = jnp.where(core == 0, mine, theirs)[:, 0:8]
    out_ref[1:2, 0:8] = jnp.where(core == 0, theirs, mine)[:, 0:8]


def hand_over(out_ref, dosage_ref, like_ref):
    dosage_ref[...] = out_ref[0:2, 0:8]
    like_ref[...] = out_ref[2:3, 0:2]


def on_device(n_y, panel, rates, genotypes):
    n_batch = lax.axis_size("batch")
    n_group = lax.axis_size("group")
    n_z = n_batch // n_y
    held = panel.shape[1]
    width = held // (n_group // 2)
    k = held * n_batch
    dma = pltpu.SemaphoreType.DMA
    vmem = pltpu.VMEM
    g1, z1, p1 = n_group - 1, max(n_z - 1, 1), n_group // 2 * n_y - 1
    scratch = [
        vmem((1, BLOCK), F32),
        vmem((2, BLOCK), jnp.int32),
        vmem((BLOCK, held), jnp.int32),
        vmem((BLOCKS, BLOCK, width), jnp.int32),
        vmem((BLOCKS, BLOCK, 128), F32),
        vmem((BLOCKS, BLOCK, 8, 128), jnp.int32),
        vmem((MARKERS, 8, 128), F32),
        vmem((MARKERS, 8, 128), F32),
        vmem((MARKERS, 8, 128), F32),
        vmem((24, 128), F32),
        vmem((p1, 20, 128), F32),
        vmem((24, 128), F32),
        vmem((z1, 20, 128), F32),
        vmem((24, 128), F32),
        vmem((1, 128), F32),
        vmem((1, 128), F32),
        vmem((1, 128), F32),
        vmem((n_group * n_batch, 128), F32),
        dma((3,)),
        dma,
        dma((8,)),
        pltpu.SemaphoreType.REGULAR((3,)),
        dma, dma, dma, dma, dma, dma,
        dma, dma,
        dma, dma,
        dma, dma,
    ]
    out = pl.pallas_call(
        functools.partial(kernel, n_y, n_z, k),
        out_shape=pltpu.VMEM((8, 128), F32),
        in_specs=[
            pl.BlockSpec(memory_space=pl.ANY),
            pl.BlockSpec(memory_space=pl.ANY),
            pl.BlockSpec(memory_space=pl.ANY),
        ],
        out_specs=pl.BlockSpec(memory_space=pltpu.VMEM),
        scratch_shapes=scratch,
        compiler_params=pltpu.CompilerParams(collective_id=0, has_side_effects=True),
    )(panel, rates.reshape(1, BLOCK), genotypes)
    dosage, like = pl.pallas_call(
        hand_over,
        out_shape=(
            jax.ShapeDtypeStruct((2, BLOCK), F32),
            jax.ShapeDtypeStruct((1, 2), F32),
        ),
    )(pltpu.with_memory_space_constraint(out, pltpu.VMEM))
    return dosage, like.reshape(2)


def solution(mesh, n_y=4):
    placed = (P("group", "batch"), P("group"), P(None, "group"))
    return jax.shard_map(
        functools.partial(on_device, n_y),
        mesh=mesh,
        in_specs=placed,
        out_specs=(P(None, "group"), P()),
        check_vma=False,
    )
```

```python
import functools
import math

import jax
import jax.numpy as jnp
from jax import lax
from jax.experimental import pallas as pl
from jax.experimental.pallas import tpu as pltpu
from jax.sharding import PartitionSpec as P

HIGHEST = lax.Precision.HIGHEST
MESH = pl.DeviceIdType.MESH

MISMATCH = 0.05
STEP = 0.5 * math.log((1.0 - MISMATCH) / MISMATCH)
LOG_CENTRE = 0.5 * math.log((1.0 - MISMATCH) * MISMATCH)
UP = math.exp(STEP)
DOWN = math.exp(-STEP)
NEG = -1e30
F32 = jnp.float32
BF16 = jnp.bfloat16

MARKERS = 64
BLOCK = 8
BLOCKS = 8


def iota(shape, axis):
    return lax.broadcasted_iota(jnp.int32, shape, axis)


def dot_nt(a, b, precision=None):
    return lax.dot_general(
        a, b, (((1,), (1,)), ((), ())), precision=precision, preferred_element_type=F32
    )


def low_half(x):
    return jnp.where(iota(x.shape, 1) < 64, x, pltpu.roll(x, 64, 1))


def high_half(x):
    return jnp.where(iota(x.shape, 1) < 64, pltpu.roll(x, 64, 1), x)


def meta_tile(rate_row, geno_rows):
    eye = iota((8, 8), 0) == iota((8, 8), 1)
    lane = iota((8, 128), 1)

    def column(row):
        return jnp.sum(jnp.where(eye, jnp.broadcast_to(row, (8, 8)), 0.0), axis=1, keepdims=True)

    rate = column(rate_row)
    first = column(geno_rows[0:1].astype(F32))
    second = column(geno_rows[1:2].astype(F32))
    return jnp.where(lane == 0, rate, jnp.where(lane == 1, first, second))


def anchor_matrix():
    row = iota((128, 64), 0)
    col = iota((128, 64), 1)
    s = row
    t = row - 64
    upper = jnp.where((col >= s) & (col <= 31), 1.0, jnp.where((col >= 32) & (col < s), -1.0, 0.0))
    lower = jnp.where((col >= 32) & (col <= t), 1.0, jnp.where((col > t) & (col <= 31), -1.0, 0.0))
    return jnp.where(row < 64, upper, lower).astype(BF16)


def product(a, b):
    a_top, b_top = a.astype(BF16), b.astype(BF16)
    a_rest = (a - a_top.astype(F32)).astype(BF16)
    b_rest = (b - b_top.astype(F32)).astype(BF16)
    return dot_nt(a_top, b_top) + (dot_nt(a_rest, b_top) + dot_nt(a_top, b_rest))


def couplings(signs, genotype):
    width = signs.shape[1]
    sign = jnp.where(genotype == 2.0, 0.0, 2.0 * genotype - 1.0)
    steps = jnp.dot(anchor_matrix(), (signs * sign).astype(BF16), preferred_element_type=F32)
    from_s, to_t = steps[:64], steps[64:]
    u = jnp.exp(STEP * from_s)
    v = jnp.exp(STEP * to_t)
    full = jnp.log(product(u, jnp.concatenate([v, v], axis=0)))
    left, right = from_s[16:17], to_t[47:48]
    middle = left + right
    top = jnp.max(middle, axis=1, keepdims=True)
    begin = jnp.exp(STEP * (from_s[:16] - left + (middle - top)))
    end = jnp.exp(STEP * (to_t[48:] - right))
    blank = jnp.zeros((48, width), F32)
    corner = jnp.log(product(begin, jnp.concatenate([blank, end, blank, end], axis=0)))
    corner = corner + STEP * top
    return pack(full, corner)


def pack(full, corner):
    lane = iota((8, 128), 1)
    sub = iota((8, 128), 0)
    col = lane % 64
    rows = [full[8 * a : 8 * a + 8] for a in range(BLOCKS)]
    for a in range(2):
        rows[a] = jnp.where(col >= 48, corner[8 * a : 8 * a + 8], rows[a])
    diagonal = rows[0]
    for a in range(1, BLOCKS):
        diagonal = jnp.where(col // 8 == a, rows[a], diagonal)
    diagonal = jnp.where(col % 8 >= sub, diagonal, 0.0)
    pairs = []
    for a in range(4):
        other = rows[7 - a] if a == 0 else pltpu.roll(rows[7 - a], 8 * a, 1)
        pairs.append(
            jnp.where(col >= 8 * (a + 1), rows[a], jnp.where(col < 8 * a, other, 0.0))
        )
    first = jnp.where(lane < 64, pairs[0], pairs[1])
    second = jnp.where(lane < 64, pairs[2], pairs[3])
    halves = jnp.where(lane < 64, diagonal, pltpu.roll(diagonal, 4, 0))
    return jnp.concatenate([first, second, halves], axis=0)


def unpack(packed):
    first, second, halves = packed[0:8], packed[8:16], packed[16:24]
    diagonal = jnp.where(
        iota((8, 128), 0) < 4, low_half(halves), pltpu.roll(high_half(halves), 4, 0)
    )
    pairs = [low_half(first), high_half(first), low_half(second), high_half(second)]
    rows = [None] * BLOCKS
    for a in range(4):
        rows[a] = pairs[a]
        rows[7 - a] = pairs[a] if a == 0 else pltpu.roll(pairs[a], 128 - 8 * a, 1)
    col = iota((8, 128), 1) % 64
    return [jnp.where(col // 8 == a, diagonal, rows[a]) for a in range(BLOCKS)], diagonal


def log_total(items):
    top = functools.reduce(jnp.maximum, items)
    return top + jnp.log(functools.reduce(jnp.add, [jnp.exp(x - top) for x in items]))


def row_of(columns):
    col = iota((8, 128), 1) % 64
    sub = iota((8, 128), 0)
    total = None
    for a, column in enumerate(columns):
        part = jnp.where(col == 8 * a + sub, column, 0.0)
        total = part if total is None else total + part
    return jnp.sum(total, axis=0, keepdims=True)


def rate_terms(rates, log_k):
    lane = iota((8, 128), 1)
    col = lane % 64
    sub = iota((8, 128), 0)
    stay = [jnp.log(1.0 - r) for r in rates]
    stay_row = row_of(stay)
    sums = None
    for a in range(BLOCKS):
        part = jnp.where(8 * a + sub <= col, stay[a], 0.0)
        sums = part if sums is None else sums + part
    reach_row = jnp.sum(sums, axis=0, keepdims=True)
    reach_col = [
        jnp.sum(jnp.where((lane < 64) & (col <= 8 * a + sub), stay_row, 0.0), axis=1, keepdims=True)
        for a in range(BLOCKS)
    ]
    jump_col = [jnp.log(r) - log_k for r in rates]
    jump_row = row_of(jump_col)
    start = jnp.full((8, 1), -log_k, F32)
    jump_col[0] = jnp.where(iota((8, 1), 0) == 0, start, jump_col[0])
    return reach_row, reach_col, jump_row, jump_col


def solve(packed, terms, log_k):
    reach_row, reach_col, jump_row, jump_col = terms
    lane = iota((8, 128), 1)
    sub = iota((8, 128), 0)
    col = lane % 64
    block = col // 8
    within = col % 8
    rows, diagonal = unpack(packed)
    paths = [
        jnp.where(col >= 8 * a + sub, rows[a] + (reach_row - reach_col[a]), NEG)
        for a in range(BLOCKS)
    ]
    reach_diag = jnp.broadcast_to(reach_col[0], (8, 128))
    jump_diag = jnp.broadcast_to(jump_col[0], (8, 128))
    for a in range(1, BLOCKS):
        reach_diag = jnp.where(block == a, reach_col[a], reach_diag)
        jump_diag = jnp.where(block == a, jump_col[a], jump_diag)
    path_diag = diagonal + (reach_row - reach_diag)
    ahead = pltpu.roll(path_diag + jump_diag, 7, 0)
    behind = pltpu.roll(path_diag, 1, 1) + jump_row
    inner = jnp.exp(jnp.where(within > sub, jnp.where(lane < 64, ahead, behind), NEG))
    spread = jnp.concatenate(
        [jnp.where(lane % 8 == sub, inner[m : m + 1], 0.0) for m in range(8)], axis=0
    )
    same = (iota((128, 128), 0) // 8 == iota((128, 128), 1) // 8).astype(BF16)
    coarse = spread.astype(BF16)
    fine = (spread - coarse.astype(F32)).astype(BF16)
    columns = jnp.dot(coarse, same, preferred_element_type=F32)
    columns = columns + jnp.dot(fine, same, preferred_element_type=F32)
    inverse = jnp.where(within == sub, 1.0, 0.0)
    for m in range(7):
        inverse = inverse + columns[8 * m : 8 * m + 8] * inverse[m : m + 1]
    forward_inverse = jnp.where(lane < 64, inverse, 0.0)
    backward_inverse = high_half(inverse)

    offset = jnp.broadcast_to(paths[0][7:8], (8, 128))
    for a in range(1, BLOCKS):
        offset = jnp.where(sub == a, paths[a][7:8], offset)
    offset = jnp.where((within == 0) & (block > sub), offset, 0.0)
    for step in (1, 2, 4):
        offset = offset + pltpu.roll(offset, step, 1)
    factors = [jnp.exp(paths[a] - offset[a : a + 1]) for a in range(BLOCKS)]
    injectors = [jnp.exp(j) * f for j, f in zip(jump_col, factors)]
    row_lane = iota((1, 128), 1)
    row_col = row_lane % 64
    jumps_row = jnp.where(row_lane == 64, math.exp(-log_k), jnp.exp(jump_row))
    shifted = [pltpu.roll(f, 1, 1) * jumps_row for f in factors]
    shifted_offset = pltpu.roll(offset, 1, 1)
    inverses = [jnp.where(block == b, forward_inverse, 0.0) for b in range(BLOCKS)]

    zero = jnp.zeros((1, 128), F32)
    sums = []
    scales = [zero, zero]
    last = jnp.ones((1, 128), F32)
    spent = jnp.zeros((8, 128), F32)
    scale_col = jnp.zeros((8, 128), F32)
    newest = None

    back_scales = [zero, zero]
    back_scale_row = zero
    back_sums = zero
    behind_row = jnp.where(row_lane == 64, 1.0, 0.0)

    for b in range(BLOCKS):
        lead = last * injectors[b][0:1]
        if b > 1:
            weight = jnp.exp(offset + scale_col - scales[b])
            weight = jnp.where((sub < b - 1) & (block == b), weight, 0.0)
            lead = lead + jnp.sum(weight * spent, axis=0, keepdims=True)
        if b:
            weight = jnp.exp(offset[b - 1 : b] + (scales[b - 1] - scales[b]))
            weight = jnp.where(row_col // 8 == b, weight, 0.0)
            lead = lead + weight * newest
        here = jnp.sum(lead * inverses[b], axis=1, keepdims=True)
        here = jnp.broadcast_to(here, (8, 128))
        sums.append(here)
        if b < BLOCKS - 1:
            before = jnp.where(sub == 0, last, pltpu.roll(here, 1, 0))
            newest = jnp.sum(before * injectors[b], axis=0, keepdims=True)
            spent = jnp.where(sub == b, newest, spent)
            scale_col = jnp.where(sub == b, scales[b], scale_col)
            last = here[7:8] * jnp.exp(scales[b] - scales[b + 1])
            scales.append(jnp.log(here[7:8]) + scales[b])

        c = BLOCKS - 1 - b
        weight = jnp.exp(shifted_offset[c : c + 1] + (back_scale_row - back_scales[b]))
        weight = jnp.where((row_lane >= 8 * c + 8) & (row_lane <= 64), weight, 0.0)
        pulled = shifted[c] * weight
        lead = jnp.sum(pulled * behind_row, axis=1, keepdims=True)
        back = jnp.sum(lead * backward_inverse, axis=0, keepdims=True)
        inside = (row_lane >= 8 * c) & (row_lane < 8 * c + 8)
        back_sums = jnp.where(row_col // 8 == c, jnp.log(back) + back_scales[b], back_sums)
        if c:
            behind_row = jnp.where(inside, back, behind_row)
            back_scale_row = jnp.where(inside, back_scales[b], back_scale_row)
            first = jnp.sum(
                jnp.where(row_lane == 8 * c, back, 0.0), axis=1, keepdims=True
            )
            back_scales.append(jnp.log(first) + back_scales[b])

    scale_row = zero
    for b in range(BLOCKS):
        scale_row = jnp.where(row_col // 8 == b, scales[b], scale_row)
    forward_row = jnp.log(row_of(sums)) + scale_row
    return jnp.where(row_lane < 64, forward_row, back_sums)


def emission_terms(geno_row):
    g = geno_row
    base = jnp.where(g == 2.0, 1.0, jnp.where(g == 1.0, DOWN, UP))
    slope = jnp.where(g == 2.0, 0.0, jnp.where(g == 1.0, UP - DOWN, DOWN - UP))
    return base, slope


def state_terms(logs, rate_row, k):
    lane = iota((1, 128), 1)
    before = jnp.where(lane == 0, 0.0, pltpu.roll(logs, 1, 1))
    after = jnp.where(lane == 127, 0.0, pltpu.roll(logs, 127, 1))
    over_forward = jnp.exp(before - logs)
    over_backward = pltpu.roll(jnp.exp(after - logs), 64, 1)
    keep = 1.0 - rate_row
    jump = rate_row * (1.0 / k)
    rows = (keep * over_forward, jump * over_forward, keep * over_backward, jump)
    return [jnp.broadcast_to(row, (8, 128)) for row in rows]


def gather_sublanes(tiles):
    sub = iota((8, 128), 0)
    step = 4
    while len(tiles) > 1:
        half = len(tiles) // 2
        low = sub & step == 0
        merged = []
        for i in range(half):
            first, second = tiles[i], tiles[i + half]
            kept = jnp.where(low, first, second)
            moved = jnp.where(low, second, first)
            merged.append(kept + pltpu.roll(moved, step, 0) if step == 4 else kept + swap_by(moved, step))
        tiles = merged
        step //= 2
    return tiles[0]


def swap_by(x, step):
    low = iota((8, 128), 0) & step == 0
    return jnp.where(low, pltpu.roll(x, 8 - step, 0), pltpu.roll(x, step, 0))


def far_first(n):
    return sorted(range(1, n), key=lambda d: -min(d, n - d))


def kernel(
    n_y, n_z, k,
    panel_ref, rate_ref, geno_ref,
    out_ref,
    rate_own, geno_own, panel_own, panel_all, meta_all, tiles, emis, fwd, bwd,
    log_send, log_plane, log_mid, log_z, log_last,
    solve_send, solve_recv, sum_send, sum_all,
    load_sem, own_sem, tile_sem, known,
    panel_s, panel_r, meta_s, meta_r, plane_s, plane_r, z_s, z_r,
    core_s, core_r, all_s, all_r,
):
    n_group = BLOCKS
    n_x = n_group // 2
    group = lax.axis_index("group")
    batch = lax.axis_index("batch")
    x = lax.div(group, 2)
    core = group - 2 * x
    z = lax.div(batch, n_y)
    y = batch - n_y * z
    others_core = 1 - core
    partner = (2 * x + others_core, batch)
    width = panel_all.shape[2]
    log_k = math.log(k)
    first_of = [2 * lax.rem(x + d, n_x) for d in range(n_x)]
    groups = [[first + core, first + others_core] for first in first_of]
    ys = [lax.rem(y + d, n_y) for d in range(n_y)]
    zs = [n_y * lax.rem(z + d, n_z) for d in range(n_z)]

    def in_group(d):
        return lax.rem(group + d, n_group)

    def group_peer(d):
        return (in_group(d), batch)

    def y_peer(d):
        return (group, n_y * z + ys[d])

    def z_peer(d):
        return (group, zs[d] + y)

    def plane_peer(dx, dy):
        return (groups[dx][0], n_y * z + ys[dy])

    def remote(src, dst, send, recv, peer):
        return pltpu.make_async_remote_copy(
            src_ref=src, dst_ref=dst, send_sem=send, recv_sem=recv,
            device_id=peer, device_id_type=MESH,
        )

    def finish(copies):
        for copy in copies:
            copy.wait()

    def hear(near, turn):
        for peer in near:
            pl.semaphore_signal(known.at[turn], inc=1, device_id=peer, device_id_type=MESH)
        if near:
            pl.semaphore_wait(known.at[turn], len(near))

    loads = [
        pltpu.make_async_copy(rate_ref, rate_own, load_sem.at[0]),
        pltpu.make_async_copy(geno_ref, geno_own, load_sem.at[1]),
        pltpu.make_async_copy(panel_ref, panel_own, load_sem.at[2]),
    ]
    own = pltpu.make_async_copy(
        panel_ref.at[:, pl.ds(pl.multiple_of(x * width, width), width)],
        panel_all.at[group],
        own_sem,
    )
    for load in loads:
        load.start()
    barrier = pltpu.get_barrier_semaphore()
    near_y = [y_peer(d) for d in sorted({1, n_y - 1}) if 0 < d < n_y]
    near_z = [z_peer(d) for d in sorted({1, n_z - 1}) if 0 < d < n_z]
    peers = [group_peer(d) for d in far_first(n_group)] + near_y + near_z
    for peer in peers:
        pl.semaphore_signal(barrier, inc=1, device_id=peer, device_id_type=MESH)
    own.start()
    finish(loads)
    meta_all[group] = meta_tile(rate_own[...], geno_own[...])
    pl.semaphore_wait(barrier, len(peers))

    copies = []
    for d in far_first(n_group):
        start = pl.multiple_of(lax.div(in_group(d), 2) * width, width)
        copies.append(
            remote(
                panel_own.at[:, pl.ds(start, width)], panel_all.at[group],
                panel_s, panel_r, group_peer(d),
            )
        )
    for d in far_first(n_group):
        copies.append(
            remote(
                meta_all.at[group], meta_all.at[group],
                meta_s, meta_r, group_peer(d),
            )
        )
    for copy in copies:
        copy.start()
    hear(near_y + near_z, 0)
    hear(near_y + near_z, 1)
    hear(near_z, 2)
    own.wait()
    most = pl.ds(0, n_group - 1)
    remote(meta_all.at[most], meta_all.at[most], meta_s, meta_r, partner).wait()
    remote(panel_all.at[most], panel_all.at[most], panel_s, panel_r, partner).wait()

    meta = meta_all[...].reshape(MARKERS, 128)
    signs = 2.0 * panel_all[...].reshape(MARKERS, width).astype(F32) - 1.0
    genotype = jnp.where(core == 0, meta[:, 1:2], meta[:, 2:3])
    log_send[...] = couplings(signs, genotype)
    sent = pl.ds(0, 20)

    plane = [(dx, dy) for dx in range(n_x) for dy in range(n_y) if dx or dy]
    plane.sort(key=lambda p: -(min(p[0], n_x - p[0]) + min(p[1], n_y - p[1])))
    flying = [
        remote(
            log_send.at[sent], log_plane.at[i], plane_s, plane_r, plane_peer(dx, dy)
        )
        for i, (dx, dy) in enumerate(plane)
    ]
    for copy in flying:
        copy.start()
    relayout = []
    for c in range(8):
        copy = pltpu.make_async_copy(
            panel_all.at[:, :, pl.ds(128 * c, 128)], tiles.at[:, :, c], tile_sem.at[c]
        )
        copy.start()
        relayout.append(copy)

    rates = [meta[8 * a : 8 * a + 8, 0:1] for a in range(BLOCKS)]
    terms = rate_terms(rates, log_k)
    rate_row = row_of(rates)
    geno_row = row_of([genotype[8 * a : 8 * a + 8] for a in range(BLOCKS)])
    base, slope = emission_terms(geno_row)
    log_mid[...] = jnp.zeros((24, 128), F32)
    log_last[...] = jnp.zeros((24, 128), F32)
    remote(log_plane, log_plane, plane_s, plane_r, partner).wait()
    total = log_total([log_send[0:20]] + [log_plane[i] for i in range(len(plane))])
    log_mid[0:20] = total

    flying = [
        remote(log_mid.at[sent], log_z.at[d - 1], z_s, z_r, z_peer(d))
        for d in far_first(n_z)
    ]
    for copy in flying:
        copy.start()
    finish(relayout)
    for t in range(MARKERS):
        allele = tiles[t // 8, t % 8].astype(F32)
        emis[t] = base[:, t : t + 1] + slope[:, t : t + 1] * allele
    if n_z > 1:
        remote(log_z, log_z, z_s, z_r, partner).wait()
    log_last[0:20] = log_total([total] + [log_z[d] for d in range(n_z - 1)])

    sum_send[...] = jnp.zeros((1, 128), F32)
    solved = solve(log_last[...], terms, log_k)

    lane_row = iota((1, 128), 1)
    seen = jnp.sum(
        jnp.where((lane_row < 64) & (geno_row != 2.0), LOG_CENTRE, 0.0), axis=1, keepdims=True
    )
    like = jnp.broadcast_to((solved[:, 63:64] + seen) * (1.0 / MARKERS), (1, 128))
    solve_send[...] = like
    swap = remote(solve_send, solve_recv, core_s, core_r, partner)
    swap.start()

    keep_f, jump_f, keep_b, jump_b = state_terms(solved, rate_row, float(k))
    ahead = jnp.full((8, 128), 1.0 / k, F32)
    behind = jnp.full((8, 128), 1.0 / k, F32)
    for i in range(MARKERS):
        kept, added = emis[i] * keep_f[:, i : i + 1], emis[i] * jump_f[:, i : i + 1]
        ahead = kept * ahead + added
        fwd[i] = ahead
        t = MARKERS - 1 - i
        bwd[t] = behind
        behind = (keep_b[:, t : t + 1] * emis[t]) * behind + jump_b[:, t : t + 1]

    over_k = []
    for a in range(BLOCKS):
        both = fwd[8 * a : 8 * a + 8] * bwd[8 * a : 8 * a + 8] * tiles[a].astype(F32)
        over_k.append(gather_sublanes([both[i] for i in range(8)]))
    stacked = jnp.concatenate(over_k, axis=0)
    ones = jnp.ones((8, 128), BF16)
    coarse = stacked.astype(BF16)
    fine = (stacked - coarse.astype(F32)).astype(BF16)
    total = (dot_nt(ones, coarse) + dot_nt(ones, fine))[0:1]
    after = jnp.where(lane_row == 127, 0.0, pltpu.roll(solved, 127, 1))
    inverse = jnp.exp(solved + pltpu.roll(after, 64, 1) - (solved[:, 63:64] - log_k))
    total = total * inverse[:, 0:64]

    everyone = [
        (dx, dy, dz, dc) for dx in range(n_x) for dy in range(n_y) for dz in range(n_z)
        for dc in range(2) if dx or dy or dz or dc
    ]
    everyone.sort(
        key=lambda p: -(min(p[0], n_x - p[0]) + min(p[1], n_y - p[1]) + min(p[2], n_z - p[2]))
    )
    others = len(everyone)
    half = (others + 1) // 2
    sum_send[:, 0:64] = total
    places = [1, half]
    for dx, dy, dz, dc in everyone:
        peer = (groups[dx][dc], zs[dz] + ys[dy])
        remote(sum_send, sum_all.at[pl.ds(places[dc], 1)], all_s, all_r, peer).start()
        places[dc] += 1
    sum_all[0:1, 0:64] = total
    sum_all[0:1, 64:128] = jnp.zeros((1, 64), F32)
    swap.wait()
    other = solve_recv[...]
    out_ref[2:3, 0:2] = jnp.where(
        lane_row == 0, jnp.where(core == 0, like, other), jnp.where(core == 0, other, like)
    )[:, 0:2]
    rest = pl.ds(1, others)
    remote(sum_all.at[rest], sum_all.at[rest], all_s, all_r, partner).wait()
    mine = jnp.sum(sum_all[0:half], axis=0, keepdims=True)
    theirs = jnp.sum(sum_all[half:], axis=0, keepdims=True)
    shift = lax.rem(128 - 8 * group, 128)
    mine = pltpu.roll(mine, shift, 1)
    theirs = pltpu.roll(theirs, shift, 1)
    out_ref[0:1, 0:8] = jnp.where(core == 0, mine, theirs)[:, 0:8]
    out_ref[1:2, 0:8] = jnp.where(core == 0, theirs, mine)[:, 0:8]


def hand_over(out_ref, dosage_ref, like_ref):
    dosage_ref[...] = out_ref[0:2, 0:8]
    like_ref[...] = out_ref[2:3, 0:2]


def on_device(n_y, panel, rates, genotypes):
    n_batch = lax.axis_size("batch")
    n_group = lax.axis_size("group")
    n_z = n_batch // n_y
    held = panel.shape[1]
    width = held // (n_group // 2)
    k = held * n_batch
    dma = pltpu.SemaphoreType.DMA
    vmem = pltpu.VMEM
    g1, z1, p1 = n_group - 1, max(n_z - 1, 1), n_group // 2 * n_y - 1
    scratch = [
        vmem((1, BLOCK), F32),
        vmem((2, BLOCK), jnp.int32),
        vmem((BLOCK, held), jnp.int32),
        vmem((BLOCKS, BLOCK, width), jnp.int32),
        vmem((BLOCKS, BLOCK, 128), F32),
        vmem((BLOCKS, BLOCK, 8, 128), jnp.int32),
        vmem((MARKERS, 8, 128), F32),
        vmem((MARKERS, 8, 128), F32),
        vmem((MARKERS, 8, 128), F32),
        vmem((24, 128), F32),
        vmem((p1, 20, 128), F32),
        vmem((24, 128), F32),
        vmem((z1, 20, 128), F32),
        vmem((24, 128), F32),
        vmem((1, 128), F32),
        vmem((1, 128), F32),
        vmem((1, 128), F32),
        vmem((n_group * n_batch, 128), F32),
        dma((3,)),
        dma,
        dma((8,)),
        pltpu.SemaphoreType.REGULAR((3,)),
        dma, dma, dma, dma, dma, dma,
        dma, dma,
        dma, dma,
        dma, dma,
    ]
    out = pl.pallas_call(
        functools.partial(kernel, n_y, n_z, k),
        out_shape=pltpu.VMEM((8, 128), F32),
        in_specs=[
            pl.BlockSpec(memory_space=pl.ANY),
            pl.BlockSpec(memory_space=pl.ANY),
            pl.BlockSpec(memory_space=pl.ANY),
        ],
        out_specs=pl.BlockSpec(memory_space=pltpu.VMEM),
        scratch_shapes=scratch,
        compiler_params=pltpu.CompilerParams(collective_id=0, has_side_effects=True),
    )(panel, rates.reshape(1, BLOCK), genotypes)
    dosage, like = pl.pallas_call(
        hand_over,
        out_shape=(
            jax.ShapeDtypeStruct((2, BLOCK), F32),
            jax.ShapeDtypeStruct((1, 2), F32),
        ),
    )(pltpu.with_memory_space_constraint(out, pltpu.VMEM))
    return dosage, like.reshape(2)


def solution(mesh, n_y=4):
    placed = (P("group", "batch"), P("group"), P(None, "group"))
    return jax.shard_map(
        functools.partial(on_device, n_y),
        mesh=mesh,
        in_specs=placed,
        out_specs=(P(None, "group"), P()),
        check_vma=False,
    )
```

```python
import functools
import math

import jax
import jax.numpy as jnp
from jax import lax
from jax.experimental import pallas as pl
from jax.experimental.pallas import tpu as pltpu
from jax.sharding import PartitionSpec as P

HIGHEST = lax.Precision.HIGHEST
MESH = pl.DeviceIdType.MESH

MISMATCH = 0.05
STEP = 0.5 * math.log((1.0 - MISMATCH) / MISMATCH)
LOG_CENTRE = 0.5 * math.log((1.0 - MISMATCH) * MISMATCH)
UP = math.exp(STEP)
DOWN = math.exp(-STEP)
NEG = -1e30
F32 = jnp.float32
BF16 = jnp.bfloat16

MARKERS = 64
BLOCK = 8
BLOCKS = 8


def iota(shape, axis):
    return lax.broadcasted_iota(jnp.int32, shape, axis)


def dot_nt(a, b, precision=None):
    return lax.dot_general(
        a, b, (((1,), (1,)), ((), ())), precision=precision, preferred_element_type=F32
    )


def low_half(x):
    return jnp.where(iota(x.shape, 1) < 64, x, pltpu.roll(x, 64, 1))


def high_half(x):
    return jnp.where(iota(x.shape, 1) < 64, pltpu.roll(x, 64, 1), x)


def meta_tile(rate_row, geno_rows):
    eye = iota((8, 8), 0) == iota((8, 8), 1)
    lane = iota((8, 128), 1)

    def column(row):
        return jnp.sum(jnp.where(eye, jnp.broadcast_to(row, (8, 8)), 0.0), axis=1, keepdims=True)

    rate = column(rate_row)
    first = column(geno_rows[0:1].astype(F32))
    second = column(geno_rows[1:2].astype(F32))
    return jnp.where(lane == 0, rate, jnp.where(lane == 1, first, second))


def anchor_matrix():
    row = iota((128, 64), 0)
    col = iota((128, 64), 1)
    s = row
    t = row - 64
    upper = jnp.where((col >= s) & (col <= 31), 1.0, jnp.where((col >= 32) & (col < s), -1.0, 0.0))
    lower = jnp.where((col >= 32) & (col <= t), 1.0, jnp.where((col > t) & (col <= 31), -1.0, 0.0))
    return jnp.where(row < 64, upper, lower).astype(BF16)


def product(a, b):
    a_top, b_top = a.astype(BF16), b.astype(BF16)
    a_rest = (a - a_top.astype(F32)).astype(BF16)
    b_rest = (b - b_top.astype(F32)).astype(BF16)
    return dot_nt(a_top, b_top) + (dot_nt(a_rest, b_top) + dot_nt(a_top, b_rest))


def couplings(signs, genotype):
    width = signs.shape[1]
    sign = jnp.where(genotype == 2.0, 0.0, 2.0 * genotype - 1.0)
    steps = jnp.dot(anchor_matrix(), (signs * sign).astype(BF16), preferred_element_type=F32)
    from_s, to_t = steps[:64], steps[64:]
    u = jnp.exp(STEP * from_s)
    v = jnp.exp(STEP * to_t)
    full = jnp.log(product(u, jnp.concatenate([v, v], axis=0)))
    left, right = from_s[16:17], to_t[47:48]
    middle = left + right
    top = jnp.max(middle, axis=1, keepdims=True)
    begin = jnp.exp(STEP * (from_s[:16] - left + (middle - top)))
    end = jnp.exp(STEP * (to_t[48:] - right))
    blank = jnp.zeros((48, width), F32)
    corner = jnp.log(product(begin, jnp.concatenate([blank, end, blank, end], axis=0)))
    corner = corner + STEP * top
    return pack(full, corner)


def pack(full, corner):
    lane = iota((8, 128), 1)
    sub = iota((8, 128), 0)
    col = lane % 64
    rows = [full[8 * a : 8 * a + 8] for a in range(BLOCKS)]
    for a in range(2):
        rows[a] = jnp.where(col >= 48, corner[8 * a : 8 * a + 8], rows[a])
    diagonal = rows[0]
    for a in range(1, BLOCKS):
        diagonal = jnp.where(col // 8 == a, rows[a], diagonal)
    diagonal = jnp.where(col % 8 >= sub, diagonal, 0.0)
    pairs = []
    for a in range(4):
        other = rows[7 - a] if a == 0 else pltpu.roll(rows[7 - a], 8 * a, 1)
        pairs.append(
            jnp.where(col >= 8 * (a + 1), rows[a], jnp.where(col < 8 * a, other, 0.0))
        )
    first = jnp.where(lane < 64, pairs[0], pairs[1])
    second = jnp.where(lane < 64, pairs[2], pairs[3])
    halves = jnp.where(lane < 64, diagonal, pltpu.roll(diagonal, 4, 0))
    return jnp.concatenate([first, second, halves], axis=0)


def unpack(packed):
    first, second, halves = packed[0:8], packed[8:16], packed[16:24]
    diagonal = jnp.where(
        iota((8, 128), 0) < 4, low_half(halves), pltpu.roll(high_half(halves), 4, 0)
    )
    pairs = [low_half(first), high_half(first), low_half(second), high_half(second)]
    rows = [None] * BLOCKS
    for a in range(4):
        rows[a] = pairs[a]
        rows[7 - a] = pairs[a] if a == 0 else pltpu.roll(pairs[a], 128 - 8 * a, 1)
    col = iota((8, 128), 1) % 64
    return [jnp.where(col // 8 == a, diagonal, rows[a]) for a in range(BLOCKS)], diagonal


def log_total(items):
    top = functools.reduce(jnp.maximum, items)
    return top + jnp.log(functools.reduce(jnp.add, [jnp.exp(x - top) for x in items]))


def row_of(columns):
    col = iota((8, 128), 1) % 64
    sub = iota((8, 128), 0)
    total = None
    for a, column in enumerate(columns):
        part = jnp.where(col == 8 * a + sub, column, 0.0)
        total = part if total is None else total + part
    return jnp.sum(total, axis=0, keepdims=True)


def rate_terms(rates, log_k):
    lane = iota((8, 128), 1)
    col = lane % 64
    sub = iota((8, 128), 0)
    stay = [jnp.log(1.0 - r) for r in rates]
    stay_row = row_of(stay)
    sums = None
    for a in range(BLOCKS):
        part = jnp.where(8 * a + sub <= col, stay[a], 0.0)
        sums = part if sums is None else sums + part
    reach_row = jnp.sum(sums, axis=0, keepdims=True)
    reach_col = [
        jnp.sum(jnp.where((lane < 64) & (col <= 8 * a + sub), stay_row, 0.0), axis=1, keepdims=True)
        for a in range(BLOCKS)
    ]
    jump_col = [jnp.log(r) - log_k for r in rates]
    jump_row = row_of(jump_col)
    start = jnp.full((8, 1), -log_k, F32)
    jump_col[0] = jnp.where(iota((8, 1), 0) == 0, start, jump_col[0])
    return reach_row, reach_col, jump_row, jump_col


def solve(packed, terms, log_k):
    reach_row, reach_col, jump_row, jump_col = terms
    lane = iota((8, 128), 1)
    sub = iota((8, 128), 0)
    col = lane % 64
    block = col // 8
    within = col % 8
    rows, diagonal = unpack(packed)
    paths = [
        jnp.where(col >= 8 * a + sub, rows[a] + (reach_row - reach_col[a]), NEG)
        for a in range(BLOCKS)
    ]
    reach_diag = jnp.broadcast_to(reach_col[0], (8, 128))
    jump_diag = jnp.broadcast_to(jump_col[0], (8, 128))
    for a in range(1, BLOCKS):
        reach_diag = jnp.where(block == a, reach_col[a], reach_diag)
        jump_diag = jnp.where(block == a, jump_col[a], jump_diag)
    path_diag = diagonal + (reach_row - reach_diag)
    ahead = pltpu.roll(path_diag + jump_diag, 7, 0)
    behind = pltpu.roll(path_diag, 1, 1) + jump_row
    inner = jnp.exp(jnp.where(within > sub, jnp.where(lane < 64, ahead, behind), NEG))
    spread = jnp.concatenate(
        [jnp.where(lane % 8 == sub, inner[m : m + 1], 0.0) for m in range(8)], axis=0
    )
    same = (iota((128, 128), 0) // 8 == iota((128, 128), 1) // 8).astype(BF16)
    coarse = spread.astype(BF16)
    fine = (spread - coarse.astype(F32)).astype(BF16)
    columns = jnp.dot(coarse, same, preferred_element_type=F32)
    columns = columns + jnp.dot(fine, same, preferred_element_type=F32)
    inverse = jnp.where(within == sub, 1.0, 0.0)
    for m in range(7):
        inverse = inverse + columns[8 * m : 8 * m + 8] * inverse[m : m + 1]
    forward_inverse = jnp.where(lane < 64, inverse, 0.0)
    backward_inverse = high_half(inverse)

    offset = jnp.broadcast_to(paths[0][7:8], (8, 128))
    for a in range(1, BLOCKS):
        offset = jnp.where(sub == a, paths[a][7:8], offset)
    offset = jnp.where((within == 0) & (block > sub), offset, 0.0)
    for step in (1, 2, 4):
        offset = offset + pltpu.roll(offset, step, 1)
    factors = [jnp.exp(paths[a] - offset[a : a + 1]) for a in range(BLOCKS)]
    injectors = [jnp.exp(j) * f for j, f in zip(jump_col, factors)]
    row_lane = iota((1, 128), 1)
    row_col = row_lane % 64
    jumps_row = jnp.where(row_lane == 64, math.exp(-log_k), jnp.exp(jump_row))
    shifted = [pltpu.roll(f, 1, 1) * jumps_row for f in factors]
    shifted_offset = pltpu.roll(offset, 1, 1)
    inverses = [jnp.where(block == b, forward_inverse, 0.0) for b in range(BLOCKS)]

    zero = jnp.zeros((1, 128), F32)
    sums = []
    scales = [zero, zero]
    last = jnp.ones((1, 128), F32)
    spent = jnp.zeros((8, 128), F32)
    scale_col = jnp.zeros((8, 128), F32)
    newest = None

    back_scales = [zero, zero]
    back_scale_row = zero
    back_sums = zero
    behind_row = jnp.where(row_lane == 64, 1.0, 0.0)

    for b in range(BLOCKS):
        lead = last * injectors[b][0:1]
        if b > 1:
            weight = jnp.exp(offset + scale_col - scales[b])
            weight = jnp.where((sub < b - 1) & (block == b), weight, 0.0)
            lead = lead + jnp.sum(weight * spent, axis=0, keepdims=True)
        if b:
            weight = jnp.exp(offset[b - 1 : b] + (scales[b - 1] - scales[b]))
            weight = jnp.where(row_col // 8 == b, weight, 0.0)
            lead = lead + weight * newest
        here = jnp.sum(lead * inverses[b], axis=1, keepdims=True)
        here = jnp.broadcast_to(here, (8, 128))
        sums.append(here)
        if b < BLOCKS - 1:
            before = jnp.where(sub == 0, last, pltpu.roll(here, 1, 0))
            newest = jnp.sum(before * injectors[b], axis=0, keepdims=True)
            spent = jnp.where(sub == b, newest, spent)
            scale_col = jnp.where(sub == b, scales[b], scale_col)
            last = here[7:8] * jnp.exp(scales[b] - scales[b + 1])
            scales.append(jnp.log(here[7:8]) + scales[b])

        c = BLOCKS - 1 - b
        weight = jnp.exp(shifted_offset[c : c + 1] + (back_scale_row - back_scales[b]))
        weight = jnp.where((row_lane >= 8 * c + 8) & (row_lane <= 64), weight, 0.0)
        pulled = shifted[c] * weight
        lead = jnp.sum(pulled * behind_row, axis=1, keepdims=True)
        back = jnp.sum(lead * backward_inverse, axis=0, keepdims=True)
        inside = (row_lane >= 8 * c) & (row_lane < 8 * c + 8)
        back_sums = jnp.where(row_col // 8 == c, jnp.log(back) + back_scales[b], back_sums)
        if c:
            behind_row = jnp.where(inside, back, behind_row)
            back_scale_row = jnp.where(inside, back_scales[b], back_scale_row)
            first = jnp.sum(
                jnp.where(row_lane == 8 * c, back, 0.0), axis=1, keepdims=True
            )
            back_scales.append(jnp.log(first) + back_scales[b])

    scale_row = zero
    for b in range(BLOCKS):
        scale_row = jnp.where(row_col // 8 == b, scales[b], scale_row)
    forward_row = jnp.log(row_of(sums)) + scale_row
    return jnp.where(row_lane < 64, forward_row, back_sums)


def emission_terms(geno_row):
    g = geno_row
    base = jnp.where(g == 2.0, 1.0, jnp.where(g == 1.0, DOWN, UP))
    slope = jnp.where(g == 2.0, 0.0, jnp.where(g == 1.0, UP - DOWN, DOWN - UP))
    return base, slope


def state_terms(logs, rate_row, k):
    lane = iota((1, 128), 1)
    before = jnp.where(lane == 0, 0.0, pltpu.roll(logs, 1, 1))
    after = jnp.where(lane == 127, 0.0, pltpu.roll(logs, 127, 1))
    over_forward = jnp.exp(before - logs)
    over_backward = pltpu.roll(jnp.exp(after - logs), 64, 1)
    keep = 1.0 - rate_row
    jump = rate_row * (1.0 / k)
    rows = (keep * over_forward, jump * over_forward, keep * over_backward, jump)
    return [jnp.broadcast_to(row, (8, 128)) for row in rows]


def gather_sublanes(tiles):
    sub = iota((8, 128), 0)
    step = 4
    while len(tiles) > 1:
        half = len(tiles) // 2
        low = sub & step == 0
        merged = []
        for i in range(half):
            first, second = tiles[i], tiles[i + half]
            kept = jnp.where(low, first, second)
            moved = jnp.where(low, second, first)
            merged.append(kept + pltpu.roll(moved, step, 0) if step == 4 else kept + swap_by(moved, step))
        tiles = merged
        step //= 2
    return tiles[0]


def swap_by(x, step):
    low = iota((8, 128), 0) & step == 0
    return jnp.where(low, pltpu.roll(x, 8 - step, 0), pltpu.roll(x, step, 0))


def far_first(n):
    return sorted(range(1, n), key=lambda d: -min(d, n - d))


def kernel(
    n_y, n_z, k,
    panel_ref, rate_ref, geno_ref,
    out_ref,
    rate_own, geno_own, panel_own, panel_all, meta_all, tiles, emis, fwd, bwd,
    log_send, log_plane, log_mid, log_z, log_last,
    solve_send, solve_recv, sum_send, sum_all,
    load_sem, own_sem, tile_sem, known,
    panel_s, panel_r, meta_s, meta_r, plane_s, plane_r, z_s, z_r,
    core_s, core_r, all_s, all_r,
):
    n_group = BLOCKS
    n_x = n_group // 2
    group = lax.axis_index("group")
    batch = lax.axis_index("batch")
    x = lax.div(group, 2)
    core = group - 2 * x
    z = lax.div(batch, n_y)
    y = batch - n_y * z
    others_core = 1 - core
    partner = (2 * x + others_core, batch)
    width = panel_all.shape[2]
    log_k = math.log(k)
    first_of = [2 * lax.rem(x + d, n_x) for d in range(n_x)]
    groups = [[first + core, first + others_core] for first in first_of]
    ys = [lax.rem(y + d, n_y) for d in range(n_y)]
    zs = [n_y * lax.rem(z + d, n_z) for d in range(n_z)]

    def in_group(d):
        return lax.rem(group + d, n_group)

    def group_peer(d):
        return (in_group(d), batch)

    def y_peer(d):
        return (group, n_y * z + ys[d])

    def z_peer(d):
        return (group, zs[d] + y)

    def plane_peer(dx, dy):
        return (groups[dx][0], n_y * z + ys[dy])

    def remote(src, dst, send, recv, peer):
        return pltpu.make_async_remote_copy(
            src_ref=src, dst_ref=dst, send_sem=send, recv_sem=recv,
            device_id=peer, device_id_type=MESH,
        )

    def finish(copies):
        for copy in copies:
            copy.wait()

    def hear(near, turn):
        for peer in near:
            pl.semaphore_signal(known.at[turn], inc=1, device_id=peer, device_id_type=MESH)
        if near:
            pl.semaphore_wait(known.at[turn], len(near))

    loads = [
        pltpu.make_async_copy(rate_ref, rate_own, load_sem.at[0]),
        pltpu.make_async_copy(geno_ref, geno_own, load_sem.at[1]),
        pltpu.make_async_copy(panel_ref, panel_own, load_sem.at[2]),
    ]
    own = pltpu.make_async_copy(
        panel_ref.at[:, pl.ds(pl.multiple_of(x * width, width), width)],
        panel_all.at[group],
        own_sem,
    )
    for load in loads:
        load.start()
    barrier = pltpu.get_barrier_semaphore()
    near_y = [y_peer(d) for d in sorted({1, n_y - 1}) if 0 < d < n_y]
    near_z = [z_peer(d) for d in sorted({1, n_z - 1}) if 0 < d < n_z]
    peers = [group_peer(d) for d in far_first(n_group)] + near_y + near_z
    for peer in peers:
        pl.semaphore_signal(barrier, inc=1, device_id=peer, device_id_type=MESH)
    own.start()
    finish(loads)
    meta_all[group] = meta_tile(rate_own[...], geno_own[...])
    pl.semaphore_wait(barrier, len(peers))

    copies = []
    for d in far_first(n_group):
        start = pl.multiple_of(lax.div(in_group(d), 2) * width, width)
        copies.append(
            remote(
                panel_own.at[:, pl.ds(start, width)], panel_all.at[group],
                panel_s, panel_r, group_peer(d),
            )
        )
    for d in far_first(n_group):
        copies.append(
            remote(
                meta_all.at[group], meta_all.at[group],
                meta_s, meta_r, group_peer(d),
            )
        )
    for copy in copies:
        copy.start()
    hear(near_y + near_z, 0)
    hear(near_y + near_z, 1)
    hear(near_z, 2)
    own.wait()
    most = pl.ds(0, n_group - 1)
    remote(meta_all.at[most], meta_all.at[most], meta_s, meta_r, partner).wait()
    remote(panel_all.at[most], panel_all.at[most], panel_s, panel_r, partner).wait()

    meta = meta_all[...].reshape(MARKERS, 128)
    signs = 2.0 * panel_all[...].reshape(MARKERS, width).astype(F32) - 1.0
    genotype = jnp.where(core == 0, meta[:, 1:2], meta[:, 2:3])
    log_send[...] = couplings(signs, genotype)
    sent = pl.ds(0, 20)

    plane = [(dx, dy) for dx in range(n_x) for dy in range(n_y) if dx or dy]
    plane.sort(key=lambda p: -(min(p[0], n_x - p[0]) + min(p[1], n_y - p[1])))
    flying = [
        remote(
            log_send.at[sent], log_plane.at[i], plane_s, plane_r, plane_peer(dx, dy)
        )
        for i, (dx, dy) in enumerate(plane)
    ]
    for copy in flying:
        copy.start()
    relayout = []
    for c in range(8):
        copy = pltpu.make_async_copy(
            panel_all.at[:, :, pl.ds(128 * c, 128)], tiles.at[:, :, c], tile_sem.at[c]
        )
        copy.start()
        relayout.append(copy)

    rates = [meta[8 * a : 8 * a + 8, 0:1] for a in range(BLOCKS)]
    terms = rate_terms(rates, log_k)
    rate_row = row_of(rates)
    geno_row = row_of([genotype[8 * a : 8 * a + 8] for a in range(BLOCKS)])
    base, slope = emission_terms(geno_row)
    log_mid[...] = jnp.zeros((24, 128), F32)
    log_last[...] = jnp.zeros((24, 128), F32)
    remote(log_plane, log_plane, plane_s, plane_r, partner).wait()
    total = log_total([log_send[0:20]] + [log_plane[i] for i in range(len(plane))])
    log_mid[0:20] = total

    flying = [
        remote(log_mid.at[sent], log_z.at[d - 1], z_s, z_r, z_peer(d))
        for d in far_first(n_z)
    ]
    for copy in flying:
        copy.start()
    finish(relayout)
    for t in range(MARKERS):
        allele = tiles[t // 8, t % 8].astype(F32)
        emis[t] = base[:, t : t + 1] + slope[:, t : t + 1] * allele
    if n_z > 1:
        remote(log_z, log_z, z_s, z_r, partner).wait()
    log_last[0:20] = log_total([total] + [log_z[d] for d in range(n_z - 1)])

    sum_send[...] = jnp.zeros((1, 128), F32)
    solved = solve(log_last[...], terms, log_k)

    lane_row = iota((1, 128), 1)
    seen = jnp.sum(
        jnp.where((lane_row < 64) & (geno_row != 2.0), LOG_CENTRE, 0.0), axis=1, keepdims=True
    )
    like = jnp.broadcast_to((solved[:, 63:64] + seen) * (1.0 / MARKERS), (1, 128))
    solve_send[...] = like
    swap = remote(solve_send, solve_recv, core_s, core_r, partner)
    swap.start()

    keep_f, jump_f, keep_b, jump_b = state_terms(solved, rate_row, float(k))
    ahead = jnp.full((8, 128), 1.0 / k, F32)
    behind = jnp.full((8, 128), 1.0 / k, F32)
    for i in range(MARKERS):
        kept, added = emis[i] * keep_f[:, i : i + 1], emis[i] * jump_f[:, i : i + 1]
        ahead = kept * ahead + added
        fwd[i] = ahead
        t = MARKERS - 1 - i
        bwd[t] = behind
        behind = (keep_b[:, t : t + 1] * emis[t]) * behind + jump_b[:, t : t + 1]

    over_k = []
    for a in range(BLOCKS):
        both = fwd[8 * a : 8 * a + 8] * bwd[8 * a : 8 * a + 8] * tiles[a].astype(F32)
        over_k.append(gather_sublanes([both[i] for i in range(8)]))
    stacked = jnp.concatenate(over_k, axis=0)
    ones = jnp.ones((8, 128), BF16)
    coarse = stacked.astype(BF16)
    fine = (stacked - coarse.astype(F32)).astype(BF16)
    total = (dot_nt(ones, coarse) + dot_nt(ones, fine))[0:1]
    after = jnp.where(lane_row == 127, 0.0, pltpu.roll(solved, 127, 1))
    inverse = jnp.exp(solved + pltpu.roll(after, 64, 1) - (solved[:, 63:64] - log_k))
    total = total * inverse[:, 0:64]

    everyone = [
        (dx, dy, dz, dc) for dx in range(n_x) for dy in range(n_y) for dz in range(n_z)
        for dc in range(2) if dx or dy or dz or dc
    ]
    everyone.sort(
        key=lambda p: (
            -min(p[2], n_z - p[2]),
            -(min(p[0], n_x - p[0]) + min(p[1], n_y - p[1])),
        )
    )
    others = len(everyone)
    half = (others + 1) // 2
    sum_send[:, 0:64] = total
    places = [1, half]
    for dx, dy, dz, dc in everyone:
        peer = (groups[dx][dc], zs[dz] + ys[dy])
        remote(sum_send, sum_all.at[pl.ds(places[dc], 1)], all_s, all_r, peer).start()
        places[dc] += 1
    sum_all[0:1, 0:64] = total
    sum_all[0:1, 64:128] = jnp.zeros((1, 64), F32)
    swap.wait()
    other = solve_recv[...]
    out_ref[2:3, 0:2] = jnp.where(
        lane_row == 0, jnp.where(core == 0, like, other), jnp.where(core == 0, other, like)
    )[:, 0:2]
    rest = pl.ds(1, others)
    remote(sum_all.at[rest], sum_all.at[rest], all_s, all_r, partner).wait()
    mine = jnp.sum(sum_all[0:half], axis=0, keepdims=True)
    theirs = jnp.sum(sum_all[half:], axis=0, keepdims=True)
    shift = lax.rem(128 - 8 * group, 128)
    mine = pltpu.roll(mine, shift, 1)
    theirs = pltpu.roll(theirs, shift, 1)
    out_ref[0:1, 0:8] = jnp.where(core == 0, mine, theirs)[:, 0:8]
    out_ref[1:2, 0:8] = jnp.where(core == 0, theirs, mine)[:, 0:8]


def hand_over(out_ref, dosage_ref, like_ref):
    dosage_ref[...] = out_ref[0:2, 0:8]
    like_ref[...] = out_ref[2:3, 0:2]


def on_device(n_y, panel, rates, genotypes):
    n_batch = lax.axis_size("batch")
    n_group = lax.axis_size("group")
    n_z = n_batch // n_y
    held = panel.shape[1]
    width = held // (n_group // 2)
    k = held * n_batch
    dma = pltpu.SemaphoreType.DMA
    vmem = pltpu.VMEM
    g1, z1, p1 = n_group - 1, max(n_z - 1, 1), n_group // 2 * n_y - 1
    scratch = [
        vmem((1, BLOCK), F32),
        vmem((2, BLOCK), jnp.int32),
        vmem((BLOCK, held), jnp.int32),
        vmem((BLOCKS, BLOCK, width), jnp.int32),
        vmem((BLOCKS, BLOCK, 128), F32),
        vmem((BLOCKS, BLOCK, 8, 128), jnp.int32),
        vmem((MARKERS, 8, 128), F32),
        vmem((MARKERS, 8, 128), F32),
        vmem((MARKERS, 8, 128), F32),
        vmem((24, 128), F32),
        vmem((p1, 20, 128), F32),
        vmem((24, 128), F32),
        vmem((z1, 20, 128), F32),
        vmem((24, 128), F32),
        vmem((1, 128), F32),
        vmem((1, 128), F32),
        vmem((1, 128), F32),
        vmem((n_group * n_batch, 128), F32),
        dma((3,)),
        dma,
        dma((8,)),
        pltpu.SemaphoreType.REGULAR((3,)),
        dma, dma, dma, dma, dma, dma,
        dma, dma,
        dma, dma,
        dma, dma,
    ]
    out = pl.pallas_call(
        functools.partial(kernel, n_y, n_z, k),
        out_shape=pltpu.VMEM((8, 128), F32),
        in_specs=[
            pl.BlockSpec(memory_space=pl.ANY),
            pl.BlockSpec(memory_space=pl.ANY),
            pl.BlockSpec(memory_space=pl.ANY),
        ],
        out_specs=pl.BlockSpec(memory_space=pltpu.VMEM),
        scratch_shapes=scratch,
        compiler_params=pltpu.CompilerParams(collective_id=0, has_side_effects=True),
    )(panel, rates.reshape(1, BLOCK), genotypes)
    dosage, like = pl.pallas_call(
        hand_over,
        out_shape=(
            jax.ShapeDtypeStruct((2, BLOCK), F32),
            jax.ShapeDtypeStruct((1, 2), F32),
        ),
    )(pltpu.with_memory_space_constraint(out, pltpu.VMEM))
    return dosage, like.reshape(2)


def solution(mesh, n_y=4):
    placed = (P("group", "batch"), P("group"), P(None, "group"))
    return jax.shard_map(
        functools.partial(on_device, n_y),
        mesh=mesh,
        in_specs=placed,
        out_specs=(P(None, "group"), P()),
        check_vma=False,
    )
```
